32 devices in a mesh: seq: 16 (over z, y, core), row: 2 (over x).
Axes of the slice: x: 2, y: 2, z: 4, core: 2. Of those that a mesh axis runs over, the one named last changes fastest.
Arguments:
- latents: bfloat16 [192, 8, 32, 320], P('seq', 'row'), may hold values from -6 to 6
- clip_lengths: int32 [4], replicated, may hold values from 1 to 96, 192 in all
- timesteps: int32 [4], replicated, may hold values from 0 to 999
- spatial_weight: bfloat16 [3, 3, 320, 320], replicated, may hold values from -0.109375 to 0.109375
- time_weight: bfloat16 [320, 320], replicated, may hold values from -0.3125 to 0.3125
- query_weight: bfloat16 [320, 320], replicated, may hold values from -3 to 3
- key_weight: bfloat16 [320, 320], replicated, may hold values from -3 to 3
- value_weight: bfloat16 [320, 320], replicated, may hold values from -0.3125 to 0.3125
- out_weight: bfloat16 [320, 320], replicated, may hold values from -0.3125 to 0.3125
- temporal_weight: bfloat16 [3, 320, 320], replicated, may hold values from -0.1875 to 0.1875
- cotangent: bfloat16 [192, 8, 32, 320], P('seq', 'row'), may hold values from -0.02734375 to 0.02734375
Outputs:
- block_out: bfloat16 [192, 8, 32, 320], P('seq', 'row')
- temporal_grad: float32 [3, 320, 320], replicated
The draws below stay inside these ranges and needn't reach their ends.
Inputs may be any that keep to these rules, and one draw needn't show every extreme that they name: `clip_lengths`: clip frame counts in packing order; they sum to 192 and the largest is exactly 96.
All inputs are finite; a program needn't handle non-finite values.
Results may differ from the reference program's by a relative error of at most 0.011.
Values may be sent and summed in bfloat16 or wider, within the bound.
No kernel may reach another device: no remote copies, remote signals or barrier semaphores. Data moves between devices by JAX's collectives and lax.ppermute only.
A program may use at most 128 MiB of HBM per device.

```python
import math
import jax
import jax.numpy as jnp
import numpy as np
from jax import lax

C = 320
HEADS = 8
W = 32
CLIPS = 4
FRAMES = 192
H = 8


def attention_pair(key):
    base_key, other_key = jax.random.split(jax.random.fold_in(key, 4021), 2)
    base_matrix = jax.random.normal(base_key, (C, C), jnp.float32) * C ** (-0.5)
    other_matrix = jax.random.normal(other_key, (C, C), jnp.float32) * C ** (-0.5)
    return (jnp.clip(base_matrix, -3.0, 3.0), jnp.clip(other_matrix, -3.0, 3.0))


def draw_query_weight(key, part):
    return attention_pair(key)[0].astype(jnp.bfloat16)


def draw_key_weight(key, part):
    return attention_pair(key)[1].astype(jnp.bfloat16)


def set_ends(drawn, stream_key, smallest, high):
    place = [jax.random.randint(jax.random.fold_in(stream_key, axis), (), 0, length) for axis, length in enumerate(drawn.shape)]
    main_axis = drawn.shape.index(max(drawn.shape))
    beside = place[:main_axis] + [(place[main_axis] + 1) % drawn.shape[main_axis]] + place[main_axis + 1:]
    return drawn.at[tuple(place)].set(smallest).at[tuple(beside)].set(high)


def block_levels(key, dims, cuts, low, top_value):
    def one(position, shards_of):
        heights = jax.random.uniform(jax.random.fold_in(jax.random.fold_in(key, 6), position), (shards_of,), jnp.float32, low / len(cuts), top_value / len(cuts))
        return jnp.repeat(jnp.exp(heights), dims[position] // shards_of).reshape((-1,) + (1,) * (len(dims) - position - 1))

    factor_of = one(*cuts[0])
    for cut in cuts[1:]:
        factor_of = factor_of * one(*cut)
    return factor_of


def split_up(amount, total, most, lean):
    weights = [(1 << 20) // math.isqrt(grade ** lean) + 1 for grade in range(2, amount + 1)]
    rest, holding = total - most - (amount - 1), [1] * (amount - 1)
    while rest > 0:
        free = [i for i in range(amount - 1) if holding[i] < most]
        pool, left = sum([weights[i] for i in free]), rest
        for i in free:
            more = min(most - holding[i], max(1, left * weights[i] // pool), rest)
            holding[i] = holding[i] + more
            rest = rest - more
    return np.array([most] + holding)


def ragged(key, count, total, reach, lean):
    if count == 2:
        one = jax.random.randint(key, (), max(1, total - reach), min(reach, total - 1) + 1)
        return jnp.stack([one, total - one])
    tallies = jnp.asarray(split_up(count, total, reach, lean), jnp.int32)
    couples = (count - 1) // 2
    giver, taker = tallies[1:1 + 2 * couples:2], tallies[2:2 + 2 * couples:2]
    room = jnp.minimum(giver - 1, reach - taker)
    moved = jax.random.randint(jax.random.fold_in(key, 1), (couples,), 0, 1 << 20) % (room + 1)
    tallies = tallies.at[1:1 + 2 * couples:2].set(giver - moved).at[2:2 + 2 * couples:2].set(taker + moved)
    return tallies[jax.random.permutation(jax.random.fold_in(key, 2), count)]


def noise(key, dims, width, reach, cuts=(), held_as=jnp.bfloat16):
    factor_of = block_levels(key, dims, cuts, -0.22, 0.18) if cuts else 1.0
    result = jax.random.normal(key, dims, jnp.float32) * width * factor_of
    return jnp.minimum(jnp.maximum(result, -reach), reach).astype(held_as)


def setup_inputs(seed: int = 0) -> dict:
    splits = jax.random.split(jax.random.key(seed), 12)
    latents = noise(splits[0], (FRAMES, H, W, C), 1.0, 6.0, ((0, 16), (1, 2)))
    clip_lengths = ragged(splits[1], CLIPS, FRAMES, FRAMES // 2, 2).astype(jnp.int32)
    timesteps = set_ends(jax.random.randint(splits[2], (CLIPS,), 0, 1000), jax.random.fold_in(splits[2], 1), 0, 999).astype(jnp.int32)
    spatial_weight = noise(splits[3], (3, 3, C, C), (9 * C) ** -0.5, 0.109375)
    time_weight = noise(splits[4], (C, C), C ** -0.5, 0.3125)
    query_weight = draw_query_weight(jax.random.fold_in(splits[11], 71), 0)
    key_weight = draw_key_weight(jax.random.fold_in(splits[11], 71), 0)
    value_weight = noise(splits[7], (C, C), C ** -0.5, 0.3125)
    out_weight = noise(splits[8], (C, C), C ** -0.5, 0.3125)
    temporal_weight = noise(splits[9], (3, C, C), (3 * C) ** -0.5, 0.1875)
    cotangent = noise(splits[10], (FRAMES, H, W, C), ((FRAMES * H * W) ** -0.5), 0.02734375, ((0, 16), (1, 2)))
    return {"latents": latents, "clip_lengths": clip_lengths, "timesteps": timesteps, "spatial_weight": spatial_weight, "time_weight": time_weight, "query_weight": query_weight, "key_weight": key_weight, "value_weight": value_weight, "out_weight": out_weight, "temporal_weight": temporal_weight, "cotangent": cotangent}


def clip_index(frame_ids, clip_lengths):
    boundary = jnp.cumsum(clip_lengths).astype(jnp.int32)
    return lax.optimization_barrier(jnp.sum((frame_ids[:, None] >= boundary[None, :]).astype(jnp.int32), axis=1)).astype(jnp.int32)

def time_table(timesteps, time_weight):
    half_width = time_weight.shape[0] // 2
    frequency = jnp.exp(-math.log(10000.0) * jnp.arange(half_width, dtype=jnp.float32) / half_width)
    angles = timesteps.astype(jnp.float32)[:, None] * frequency[None, :]
    embedded = jnp.concatenate([jnp.cos(angles), jnp.sin(angles)], axis=1)
    return jnp.dot(embedded, time_weight.astype(jnp.float32), precision=lax.Precision.HIGHEST)

def normalize(values):
    center = values - lax.optimization_barrier(jnp.mean(values, axis=-1, keepdims=True))
    spread = lax.optimization_barrier(jnp.mean(center * center, axis=-1, keepdims=True))
    return (center * lax.rsqrt(spread + 1e-05)).astype(jnp.bfloat16)

def attend_pixel(query_cols, key_cols, value_cols, same_clip):
    scale = query_cols.shape[-1] ** (-0.5)
    scores = jnp.einsum('fhd,ghd->hfg', query_cols.astype(jnp.float32), key_cols.astype(jnp.float32)) * scale
    scores = jnp.where(same_clip[None], scores, -jnp.inf)
    highest = lax.optimization_barrier(jnp.max(scores, axis=-1, keepdims=True))
    exponent = jnp.exp(scores - highest)
    weights = (exponent / lax.optimization_barrier(jnp.sum(exponent, axis=-1, keepdims=True))).astype(jnp.bfloat16)
    return jnp.einsum('hfg,ghd->fhd', weights.astype(jnp.float32), value_cols.astype(jnp.float32)).astype(jnp.bfloat16)

def reference(latents, clip_lengths, timesteps, spatial_weight, time_weight, query_weight, key_weight, value_weight, out_weight, temporal_weight, cotangent):
    frames, height, across, channels = latents.shape
    clip_ids = clip_index(jnp.arange(frames, dtype=jnp.int32), clip_lengths)
    padded = jnp.pad(latents, ((0, 0), (1, 1), (1, 1), (0, 0)))
    spatial = jnp.zeros(latents.shape, jnp.float32)
    for tap_row in range(3):
        for tap_col in range(3):
            window = padded[:, tap_row:tap_row + height, tap_col:tap_col + across, :]
            spatial = spatial + jnp.dot(window.reshape(-1, channels), spatial_weight[tap_row, tap_col], preferred_element_type=jnp.float32).reshape(latents.shape)
    table = time_table(timesteps, time_weight)
    onehot = (clip_ids[:, None] == jnp.arange(CLIPS, dtype=jnp.int32)[None, :]).astype(jnp.float32)
    frame_emb = jnp.dot(onehot, table, precision=lax.Precision.HIGHEST)
    active = (latents.astype(jnp.float32) + jax.nn.silu(spatial + frame_emb[:, None, None, :])).astype(jnp.bfloat16)
    normed = normalize(active.astype(jnp.float32))
    flat = normed.reshape(-1, channels)

    def project(weight):
        return jnp.dot(flat, weight, preferred_element_type=jnp.float32).astype(jnp.bfloat16).reshape(frames, height * across, HEADS, channels // HEADS)
    queries = project(query_weight)
    keys_all = project(key_weight)
    values_all = project(value_weight)
    same_clip = clip_ids[:, None] == clip_ids[None, :]
    attended = lax.map(lambda cols: attend_pixel(cols[0], cols[1], cols[2], same_clip), (jnp.moveaxis(queries, 1, 0), jnp.moveaxis(keys_all, 1, 0), jnp.moveaxis(values_all, 1, 0)))
    attended = jnp.moveaxis(attended, 0, 1).reshape(-1, channels)
    mixed = (active.astype(jnp.float32) + jnp.dot(attended, out_weight, preferred_element_type=jnp.float32).reshape(active.shape)).astype(jnp.bfloat16)
    prev_same = jnp.concatenate([jnp.zeros((1,), bool), clip_ids[1:] == clip_ids[:-1]])
    next_same = jnp.concatenate([clip_ids[:-1] == clip_ids[1:], jnp.zeros((1,), bool)])
    zero_frame = jnp.zeros_like(mixed[:1])
    previous = jnp.where(prev_same[:, None, None, None], jnp.concatenate([zero_frame, mixed[:-1]]), jnp.zeros((), jnp.bfloat16))
    following = jnp.where(next_same[:, None, None, None], jnp.concatenate([mixed[1:], zero_frame]), jnp.zeros((), jnp.bfloat16))
    sources = (previous, mixed, following)
    total = mixed.astype(jnp.float32)
    for index in range(3):
        total = total + jnp.dot(sources[index].reshape(-1, channels), temporal_weight[index], preferred_element_type=jnp.float32).reshape(mixed.shape)
    block_out = total.astype(jnp.bfloat16)
    flat_cot = cotangent.reshape(-1, channels)
    grads = jnp.stack([lax.dot_general(source.reshape(-1, channels), flat_cot, (((0,), (0,)), ((), ())), preferred_element_type=jnp.float32) for source in sources])
    return (block_out, grads)
```

```python
import math

import jax
import jax.numpy as jnp
from jax import lax
from jax.experimental import pallas as pl
from jax.experimental.pallas import tpu as pltpu
from jax.sharding import Mesh
from jax.sharding import PartitionSpec as P

HEADS = 8
CLIPS = 4
SEQ = ("z", "y", "c")
PLANE = ("y", "x")
BF16 = jnp.bfloat16
F32 = jnp.float32
VMEM = pltpu.VMEM
SMEM = pltpu.SMEM
PIX = 8


def time_table(timesteps, time_weight):
    half_width = time_weight.shape[0] // 2
    frequency = jnp.exp(-math.log(10000.0) * jnp.arange(half_width, dtype=F32) / half_width)
    angles = timesteps.astype(F32)[:, None] * frequency[None, :]
    embedded = jnp.concatenate([jnp.cos(angles), jnp.sin(angles)], axis=1)
    return jnp.dot(embedded, time_weight.astype(F32), precision=lax.Precision.HIGHEST)


def call(kernel, out_shape, in_spaces, scratch=(), flops=0, bytes_accessed=0, grid=None, **kw):
    return pl.pallas_call(
        kernel,
        out_shape=out_shape,
        in_specs=[pl.BlockSpec(memory_space=s) for s in in_spaces],
        out_specs=jax.tree.map(lambda _: pl.BlockSpec(memory_space=VMEM), out_shape),
        scratch_shapes=scratch,
        cost_estimate=pl.CostEstimate(
            flops=flops, bytes_accessed=bytes_accessed, transcendentals=0
        ),
        compiler_params=pltpu.CompilerParams(vmem_limit_bytes=56 * 2**20),
        **kw,
    )


def pack_pair(ref, index, first, second):
    wide = first.shape[-1] // 128 * 128
    ref[index + (slice(None), slice(0, wide))] = first[:, :wide]
    ref[index + (slice(None), slice(wide, 2 * wide))] = second[:, :wide]
    ref[index + (slice(None), slice(2 * wide, 2 * first.shape[-1]))] = jnp.concatenate(
        [first[:, wide:], second[:, wide:]], axis=-1
    )


def clip_ids(frame, len_ref):
    bound = jnp.int32(0)
    ids = jnp.zeros(frame.shape, jnp.int32)
    for k in range(CLIPS):
        bound = bound + len_ref[k]
        ids = ids + jnp.where(frame >= bound, 1, 0)
    return ids


def take(row, g, real):
    if real == PIX:
        return row[g * PIX : (g + 1) * PIX]
    piece = row[g * real : (g + 1) * real].astype(F32)
    return jnp.concatenate([piece, jnp.zeros((PIX - real, row.shape[-1]), F32)], 0).astype(BF16)


def pack_kernel(x_ref, o_ref):
    frames, rows, across, ch = x_ref.shape
    half = frames // 2
    groups = o_ref.shape[0] // rows
    real = across // groups

    def step(t, _):
        for i in range(rows):
            first, second = x_ref[t, i], x_ref[t + half, i]
            for g in range(groups):
                pack_pair(
                    o_ref, (i * groups + g, t), take(first, g, real), take(second, g, real)
                )
        return 0

    lax.fori_loop(0, half, step, 0)


def unpack_kernel(x_ref, o_ref):
    frames, rows, across, ch = o_ref.shape
    half = frames // 2
    groups = x_ref.shape[0] // rows
    real = across // groups
    wide = ch // 128 * 128

    def join(blocks, low, high):
        if real == PIX:
            return jnp.concatenate([b[:, low:high] for b in blocks], 0)
        return jnp.concatenate([b[:real, low:high].astype(F32) for b in blocks], 0).astype(BF16)

    def step(t, _):
        for i in range(rows):
            blocks = [x_ref[i * groups + g, t] for g in range(groups)]
            o_ref[t, i, :, 0:wide] = join(blocks, 0, wide)
            o_ref[t, i, :, wide:ch] = join(blocks, 2 * wide, wide + ch)
            o_ref[t + half, i, :, 0:wide] = join(blocks, wide, 2 * wide)
            o_ref[t + half, i, :, wide:ch] = join(blocks, wide + ch, 2 * ch)
        return 0

    lax.fori_loop(0, half, step, 0)


def conv_kernel(flag_ref, id_ref, lat_ref, top_ref, bot_ref, w_ref, table_ref, o_ref):
    frames, rows, across, ch = lat_ref.shape
    half = frames // 2
    groups = o_ref.shape[0] // rows
    real = across // groups

    def step(t, _):
        kept = []
        for base in (0, half):
            top = top_ref[t + base]
            bot = bot_ref[t + base]
            top = jnp.where(flag_ref[0] > 0, top, jnp.zeros_like(top))
            bot = jnp.where(flag_ref[1] > 0, bot, jnp.zeros_like(bot))
            lat = [lat_ref[t + base, i] for i in range(rows)]
            kept.append([top] + lat + [bot])
        n_rows = 2 * rows * across
        sums = []
        windows = [
            jnp.concatenate([r for s in kept for r in s[a : a + rows]], axis=0) for a in range(3)
        ]
        for b in range(3):
            acc = jnp.zeros((n_rows, ch), F32)
            for a in range(3):
                acc = acc + jnp.dot(windows[a], w_ref[a, b], preferred_element_type=F32)
            sums.append(acc)
        col = lax.broadcasted_iota(jnp.int32, (n_rows, ch), 0) & (across - 1)
        left = jnp.where(col == 0, 0.0, pltpu.roll(sums[0], 1, 0))
        right = jnp.where(col == across - 1, 0.0, pltpu.roll(sums[2], n_rows - 1, 0))
        spatial = sums[1] + left + right
        per = rows * across
        outs = []
        for k, base in enumerate((0, half)):
            emb = table_ref[pl.ds(id_ref[t + base], 1), :]
            v = spatial[k * per : (k + 1) * per] + emb
            silu = 0.5 * v * (1.0 + jnp.tanh(0.5 * v))
            res = windows[1][k * per : (k + 1) * per].astype(F32)
            outs.append((res + silu).astype(BF16))
        for d in range(rows * groups):
            pack_pair(o_ref, (d, t), take(outs[0], d, real), take(outs[1], d, real))
        return 0

    lax.fori_loop(0, half, step, 0)


def unpack_rows(blk, ch):
    wide = ch // 128 * 128
    blk = blk.astype(F32).reshape(-1, 2 * ch)
    first = (blk[:, :wide], blk[:, 2 * wide : wide + ch])
    second = (blk[:, wide : 2 * wide], blk[:, wide + ch : 2 * ch])
    return first, second


def attention_kernel(
    len_ref, act_ref, wq_ref, wk_ref, wv_ref, wo_ref, tw_ref, o_ref, m_ref, x32, n32, a32, m32, wqkv
):
    shards, half, _, ch2 = act_ref.shape
    ch = ch2 // 2
    wide = ch // 128 * 128
    frames = shards * half * 2
    rows = frames * PIX
    per = half * PIX
    head = ch // HEADS
    pad = n32.shape[0] * 128
    wqkv[...] = jnp.zeros_like(wqkv)
    for j, ref in enumerate((wq_ref, wk_ref, wv_ref)):
        wqkv[0:ch, j * pad : j * pad + ch] = ref[...]

    def load(s, _):
        first, second = unpack_rows(act_ref[s], ch)
        for k, part in enumerate((first, second)):
            at = pl.ds(pl.multiple_of((2 * s + k) * per, 8), per)
            x32[at, 0:wide] = part[0]
            x32[at, wide:ch] = part[1]
        at = pl.ds(pl.multiple_of(2 * s * per, 8), 2 * per)
        v = x32[at, :]
        center = v - jnp.mean(v, axis=-1, keepdims=True)
        spread = jnp.mean(center * center, axis=-1, keepdims=True)
        n = (center * lax.rsqrt(spread + 1e-05)).astype(BF16).astype(F32)
        n = jnp.concatenate([n, jnp.zeros((2 * per, pad - ch), F32)], axis=-1)
        for c in range(pad // 128):
            n32[c, at, :] = n[:, c * 128 : (c + 1) * 128]
        return 0

    lax.fori_loop(0, shards, load, 0)

    f_row = lax.broadcasted_iota(jnp.int32, (frames, frames), 0)
    f_col = lax.broadcasted_iota(jnp.int32, (frames, frames), 1)
    same = clip_ids(f_row, len_ref) == clip_ids(f_col, len_ref)
    scale = head ** (-0.5)
    lane = lax.broadcasted_iota(jnp.int32, (1, pad), 1)

    def pixel(p, _):
        at = pl.ds(p, frames, stride=PIX)
        n = jnp.concatenate([n32[c, at, :] for c in range(pad // 128)], axis=-1).astype(BF16)
        qkv = jnp.dot(n, wqkv[...], preferred_element_type=F32).astype(BF16)
        q, k, v = (qkv[:, j * pad : (j + 1) * pad] for j in range(3))
        acc = [jnp.zeros((frames, 256), F32), jnp.zeros((frames, 256), F32)]
        for h in range(HEADS):
            w = 0 if (h + 1) * head <= 256 else 1
            win = slice(w * 128, w * 128 + 256)
            mine = jnp.where((lane >= h * head) & (lane < (h + 1) * head), 1.0, 0.0).astype(BF16)
            s = lax.dot_general(
                (q * mine)[:, win],
                k[:, win],
                (((1,), (1,)), ((), ())),
                preferred_element_type=F32,
            )
            s = jnp.where(same, s * scale, -1e30)
            e = jnp.exp(s - jnp.max(s, axis=-1, keepdims=True))
            prob = (e * (1.0 / jnp.sum(e, axis=-1, keepdims=True))).astype(BF16)
            acc[w] = acc[w] + jnp.dot(prob, (v * mine)[:, win], preferred_element_type=F32)
        a32[0, at, :] = acc[0][:, :128]
        a32[1, at, :] = acc[0][:, 128:] + acc[1][:, :128]
        a32[2, at, :] = acc[1][:, 128:]
        return 0

    lax.fori_loop(0, PIX, pixel, 0)

    step_rows = 4 * 2 * per
    steps = rows // step_rows
    m32[0:PIX, :] = jnp.zeros((PIX, ch), F32)
    m32[rows + PIX : rows + 2 * PIX, :] = jnp.zeros((PIX, ch), F32)

    def mix(i, _):
        at = pl.ds(pl.multiple_of(i * step_rows, 8), step_rows)
        att = jnp.concatenate([a32[c, at, :] for c in range(pad // 128)], axis=-1)
        att = att[:, :ch].astype(BF16)
        m = (x32[at, :] + jnp.dot(att, wo_ref[...], preferred_element_type=F32)).astype(BF16)
        m_ref[at, :] = m
        m32[pl.ds(pl.multiple_of(i * step_rows + PIX, 8), step_rows), :] = m.astype(F32)
        return 0

    lax.fori_loop(0, steps, mix, 0)

    def temporal(i, _):
        r0 = pl.multiple_of(i * step_rows, 8)
        f = (r0 + lax.broadcasted_iota(jnp.int32, (step_rows, 1), 0)) >> 3
        here = clip_ids(f, len_ref)
        before = jnp.where((clip_ids(f - 1, len_ref) == here) & (f > 0), 1.0, 0.0)
        after = jnp.where((clip_ids(f + 1, len_ref) == here) & (f < frames - 1), 1.0, 0.0)
        prev = (m32[pl.ds(r0, step_rows), :] * before).astype(BF16)
        cur32 = m32[pl.ds(pl.multiple_of(r0 + PIX, 8), step_rows), :]
        nxt = (m32[pl.ds(pl.multiple_of(r0 + 2 * PIX, 8), step_rows), :] * after).astype(BF16)
        total = cur32 + jnp.dot(prev, tw_ref[0], preferred_element_type=F32)
        total = total + jnp.dot(cur32.astype(BF16), tw_ref[1], preferred_element_type=F32)
        total = total + jnp.dot(nxt, tw_ref[2], preferred_element_type=F32)
        for k in range(4):
            base = k * 2 * per
            a = total[base : base + per].astype(BF16).reshape(half, PIX, ch)
            b = total[base + per : base + 2 * per].astype(BF16).reshape(half, PIX, ch)
            d = i * 4 + k
            o_ref[d, :, :, 0:wide] = a[:, :, :wide]
            o_ref[d, :, :, wide : 2 * wide] = b[:, :, :wide]
            o_ref[d, :, :, 2 * wide : 2 * ch] = jnp.concatenate([a[:, :, wide:], b[:, :, wide:]], -1)
        return 0

    lax.fori_loop(0, steps, temporal, 0)


def grad_kernel(len_ref, m_ref, cot_ref, o_ref, c32):
    shards, half, _, ch2 = cot_ref.shape
    ch = ch2 // 2
    wide = ch // 128 * 128
    frames = shards * half * 2
    rows = frames * PIX
    per = half * PIX
    c32[0:PIX, :] = jnp.zeros((PIX, ch), F32)
    c32[rows + PIX : rows + 2 * PIX, :] = jnp.zeros((PIX, ch), F32)

    def load(s, _):
        first, second = unpack_rows(cot_ref[s], ch)
        for k, part in enumerate((first, second)):
            at = pl.ds(pl.multiple_of((2 * s + k) * per + PIX, 8), per)
            c32[at, 0:wide] = part[0]
            c32[at, wide:ch] = part[1]
        return 0

    lax.fori_loop(0, shards, load, 0)
    step_rows = 4 * 2 * per
    o_ref[...] = jnp.zeros_like(o_ref)

    def step(i, _):
        r0 = pl.multiple_of(i * step_rows, 8)
        f = (r0 + lax.broadcasted_iota(jnp.int32, (step_rows, 1), 0)) >> 3
        here = clip_ids(f, len_ref)
        before = jnp.where((clip_ids(f - 1, len_ref) == here) & (f > 0), 1.0, 0.0)
        after = jnp.where((clip_ids(f + 1, len_ref) == here) & (f < frames - 1), 1.0, 0.0)
        m = m_ref[pl.ds(r0, step_rows), :]
        pieces = (
            (c32[pl.ds(pl.multiple_of(r0 + 2 * PIX, 8), step_rows), :] * after).astype(BF16),
            c32[pl.ds(pl.multiple_of(r0 + PIX, 8), step_rows), :].astype(BF16),
            (c32[pl.ds(r0, step_rows), :] * before).astype(BF16),
        )
        for j, piece in enumerate(pieces):
            at = slice(j * ch, (j + 1) * ch)
            o_ref[at, :] += lax.dot_general(
                m, piece, (((0,), (0,)), ((), ())), preferred_element_type=F32
            )
        return 0

    lax.fori_loop(0, rows // step_rows, step, 0)


def tree(parts):
    while len(parts) > 1:
        parts = [parts[i] + parts[i + 1] for i in range(0, len(parts), 2)]
    return parts[0]


def swaps(n, k):
    return [(i, i ^ k) for i in range(n)]


def reduce_all(g):
    core = lax.axis_index("c")
    n_plane = lax.axis_size("y") * lax.axis_size("x")
    place = lax.axis_index("y") * lax.axis_size("x") + lax.axis_index("x")
    n_z = lax.axis_size("z")
    half = g.shape[0] // 2
    share = half // n_plane

    def cut(v, i, size):
        return lax.dynamic_slice_in_dim(v, i * size, size, 0)

    other = lax.ppermute(cut(g, 1 - core, half).astype(BF16), "c", swaps(2, 1))
    g = cut(g, core, half) + other.astype(F32)
    parts = [cut(g, place, share)]
    for k in range(1, n_plane):
        sent = cut(g, place ^ k, share).astype(BF16)
        parts.append(lax.ppermute(sent, PLANE, swaps(n_plane, k)).astype(F32))
    mine = tree(parts).astype(BF16)
    parts = [mine.astype(F32)]
    for k in range(1, n_z):
        parts.append(lax.ppermute(mine, "z", swaps(n_z, k)).astype(F32))
    total = tree(parts).astype(BF16)
    parts = [total] + [lax.ppermute(total, PLANE, swaps(n_plane, k)) for k in range(1, n_plane)]
    stacked = jnp.stack(parts)
    ordered = jnp.concatenate(
        [lax.dynamic_index_in_dim(stacked, place ^ j, 0, False) for j in range(n_plane)], 0
    )
    other = lax.ppermute(ordered, "c", swaps(2, 1))
    low = jnp.where(core == 0, ordered, other)
    high = jnp.where(core == 0, other, ordered)
    return jnp.concatenate([low, high], 0).astype(F32)


def exchange(x):
    shape = x.shape
    flat = x.reshape(shape[0], shape[1] * shape[2], shape[3])
    flat = lax.all_to_all(flat, SEQ, split_axis=0, concat_axis=0, tiled=True)
    return flat.reshape(shape)


def body(
    latents,
    clip_lengths,
    timesteps,
    spatial_weight,
    time_weight,
    query_weight,
    key_weight,
    value_weight,
    out_weight,
    temporal_weight,
    cotangent,
):
    f_dev, rows, across, ch = latents.shape
    shards = lax.axis_size("z") * lax.axis_size("y") * lax.axis_size("c")
    n_rows = lax.axis_size("x")
    assert rows * across <= shards * PIX and shards % rows == 0 and f_dev % 2 == 0
    half = f_dev // 2
    packed = jax.ShapeDtypeStruct((shards, half, PIX, 2 * ch), BF16)
    positions = f_dev * rows * across
    size = positions * ch * 2
    dense = 2 * positions * ch * ch

    row = lax.axis_index("x")
    if n_rows == 2:
        edge = jnp.where(row == 0, latents[:, rows - 1], latents[:, 0])
        got = lax.ppermute(edge, "x", swaps(2, 1))
        top, bot = got, got
    else:
        up = [(i, i + 1) for i in range(n_rows - 1)]
        top = lax.ppermute(latents[:, rows - 1], "x", up)
        bot = lax.ppermute(latents[:, 0], "x", [(j, i) for i, j in up])
    flags = jnp.stack([row > 0, row < n_rows - 1]).astype(jnp.int32)

    table = time_table(timesteps, time_weight)
    seq = (lax.axis_index("z") * lax.axis_size("y") + lax.axis_index("y")) * 2 + lax.axis_index("c")
    frame = seq * f_dev + jnp.arange(f_dev, dtype=jnp.int32)
    local_ids = jnp.sum(
        (frame[:, None] >= jnp.cumsum(clip_lengths)[None, :]).astype(jnp.int32), axis=1
    )
    active = call(
        conv_kernel,
        packed,
        [SMEM, SMEM, VMEM, VMEM, VMEM, VMEM, VMEM],
        flops=9 * dense,
        bytes_accessed=2 * size + 9 * ch * ch * 2,
    )(flags, local_ids, latents, top, bot, spatial_weight, table)
    active = exchange(active)

    cot = call(pack_kernel, packed, [VMEM], bytes_accessed=2 * size)(cotangent)
    cot, active = lax.optimization_barrier((cot, active))
    cot = exchange(cot)

    total_rows = shards * f_dev * PIX
    tiles = -(-ch // 128)
    columns = pltpu.VMEM((tiles, total_rows, 128), F32)
    block, mixed = call(
        attention_kernel,
        (packed, jax.ShapeDtypeStruct((total_rows, ch), BF16)),
        [SMEM] + [VMEM] * 6,
        scratch=[
            pltpu.VMEM((total_rows, ch), F32),
            columns,
            columns,
            pltpu.VMEM((total_rows + 2 * PIX, ch), F32),
            pltpu.VMEM((tiles * 128, 3 * tiles * 128), BF16),
        ],
        flops=10 * dense,
        bytes_accessed=3 * size,
    )(
        clip_lengths,
        active,
        query_weight,
        key_weight,
        value_weight,
        out_weight,
        temporal_weight,
    )
    block = exchange(block)
    grads = call(
        grad_kernel,
        jax.ShapeDtypeStruct((3 * ch, ch), F32),
        [SMEM, VMEM, VMEM],
        scratch=[pltpu.VMEM((total_rows + 2 * PIX, ch), F32)],
        flops=3 * dense,
        bytes_accessed=2 * size + 3 * ch * ch * 4,
    )(clip_lengths, mixed, cot)
    grads = reduce_all(grads).reshape(3, ch, ch)
    block_out = call(
        unpack_kernel,
        jax.ShapeDtypeStruct(latents.shape, BF16),
        [VMEM],
        bytes_accessed=2 * size,
    )(block)
    return block_out, grads


def solution(mesh):
    n_seq, n_row = mesh.devices.shape
    grid = Mesh(mesh.devices.reshape(n_seq // 4, 2, 2, n_row), ("z", "y", "c", "x"))
    spread = P(SEQ, "x", None, None)
    in_specs = (spread,) + (P(),) * 9 + (spread,)
    return jax.shard_map(
        body, mesh=grid, in_specs=in_specs, out_specs=(spread, P()), check_vma=False
    )
```

```python
import math

import jax
import jax.numpy as jnp
from jax import lax
from jax.experimental import pallas as pl
from jax.experimental.pallas import tpu as pltpu
from jax.sharding import Mesh
from jax.sharding import PartitionSpec as P

HEADS = 8
CLIPS = 4
SEQ = ("z", "y", "c")
PLANE = ("y", "x")
BF16 = jnp.bfloat16
F32 = jnp.float32
VMEM = pltpu.VMEM
SMEM = pltpu.SMEM
PIX = 8


def time_table(timesteps, time_weight):
    half_width = time_weight.shape[0] // 2
    frequency = jnp.exp(-math.log(10000.0) * jnp.arange(half_width, dtype=F32) / half_width)
    angles = timesteps.astype(F32)[:, None] * frequency[None, :]
    embedded = jnp.concatenate([jnp.cos(angles), jnp.sin(angles)], axis=1)
    return jnp.dot(embedded, time_weight.astype(F32), precision=lax.Precision.HIGHEST)


def call(kernel, out_shape, in_spaces, scratch=(), flops=0, bytes_accessed=0, grid=None, **kw):
    return pl.pallas_call(
        kernel,
        out_shape=out_shape,
        in_specs=[pl.BlockSpec(memory_space=s) for s in in_spaces],
        out_specs=jax.tree.map(lambda _: pl.BlockSpec(memory_space=VMEM), out_shape),
        scratch_shapes=scratch,
        cost_estimate=pl.CostEstimate(
            flops=flops, bytes_accessed=bytes_accessed, transcendentals=0
        ),
        compiler_params=pltpu.CompilerParams(vmem_limit_bytes=56 * 2**20),
        **kw,
    )


def pack_pair(ref, index, first, second):
    wide = first.shape[-1] // 128 * 128
    ref[index + (slice(None), slice(0, wide))] = first[:, :wide]
    ref[index + (slice(None), slice(wide, 2 * wide))] = second[:, :wide]
    ref[index + (slice(None), slice(2 * wide, 2 * first.shape[-1]))] = jnp.concatenate(
        [first[:, wide:], second[:, wide:]], axis=-1
    )


def clip_ids(frame, len_ref):
    bound = jnp.int32(0)
    ids = jnp.zeros(frame.shape, jnp.int32)
    for k in range(CLIPS):
        bound = bound + len_ref[k]
        ids = ids + jnp.where(frame >= bound, 1, 0)
    return ids


def take(row, g, real):
    if real == PIX:
        return row[g * PIX : (g + 1) * PIX]
    piece = row[g * real : (g + 1) * real].astype(F32)
    return jnp.concatenate([piece, jnp.zeros((PIX - real, row.shape[-1]), F32)], 0).astype(BF16)


def pack_kernel(x_ref, o_ref):
    frames, rows, across, ch = x_ref.shape
    half = frames // 2
    groups = o_ref.shape[0] // rows
    real = across // groups

    def step(t, _):
        for i in range(rows):
            first, second = x_ref[2 * t, i], x_ref[2 * t + 1, i]
            for g in range(groups):
                pack_pair(
                    o_ref, (i * groups + g, t), take(first, g, real), take(second, g, real)
                )
        return 0

    lax.fori_loop(0, half, step, 0)


def unpack_kernel(x_ref, o_ref):
    frames, rows, across, ch = o_ref.shape
    half = frames // 2
    groups = x_ref.shape[0] // rows
    real = across // groups
    wide = ch // 128 * 128

    def join(blocks, low, high):
        if real == PIX:
            return jnp.concatenate([b[:, low:high] for b in blocks], 0)
        return jnp.concatenate([b[:real, low:high].astype(F32) for b in blocks], 0).astype(BF16)

    def step(t, _):
        for i in range(rows):
            blocks = [x_ref[i * groups + g, t] for g in range(groups)]
            o_ref[2 * t, i, :, 0:wide] = join(blocks, 0, wide)
            o_ref[2 * t, i, :, wide:ch] = join(blocks, 2 * wide, wide + ch)
            o_ref[2 * t + 1, i, :, 0:wide] = join(blocks, wide, 2 * wide)
            o_ref[2 * t + 1, i, :, wide:ch] = join(blocks, wide + ch, 2 * ch)
        return 0

    lax.fori_loop(0, half, step, 0)


def conv_kernel(flag_ref, id_ref, lat_ref, top_ref, bot_ref, w_ref, table_ref, o_ref):
    frames, rows, across, ch = lat_ref.shape
    half = frames // 2
    groups = o_ref.shape[0] // rows
    real = across // groups

    def step(t, _):
        kept = []
        for base in (0, 1):
            top = top_ref[2 * t + base]
            bot = bot_ref[2 * t + base]
            top = jnp.where(flag_ref[0] > 0, top, jnp.zeros_like(top))
            bot = jnp.where(flag_ref[1] > 0, bot, jnp.zeros_like(bot))
            lat = [lat_ref[2 * t + base, i] for i in range(rows)]
            kept.append([top] + lat + [bot])
        n_rows = 2 * rows * across
        sums = []
        windows = [
            jnp.concatenate([r for s in kept for r in s[a : a + rows]], axis=0) for a in range(3)
        ]
        for b in range(3):
            acc = jnp.zeros((n_rows, ch), F32)
            for a in range(3):
                acc = acc + jnp.dot(windows[a], w_ref[a, b], preferred_element_type=F32)
            sums.append(acc)
        col = lax.broadcasted_iota(jnp.int32, (n_rows, ch), 0) & (across - 1)
        left = jnp.where(col == 0, 0.0, pltpu.roll(sums[0], 1, 0))
        right = jnp.where(col == across - 1, 0.0, pltpu.roll(sums[2], n_rows - 1, 0))
        spatial = sums[1] + left + right
        per = rows * across
        outs = []
        for k in (0, 1):
            emb = table_ref[pl.ds(id_ref[2 * t + k], 1), :]
            v = spatial[k * per : (k + 1) * per] + emb
            silu = 0.5 * v * (1.0 + jnp.tanh(0.5 * v))
            res = windows[1][k * per : (k + 1) * per].astype(F32)
            outs.append((res + silu).astype(BF16))
        for d in range(rows * groups):
            pack_pair(o_ref, (d, t), take(outs[0], d, real), take(outs[1], d, real))
        return 0

    lax.fori_loop(0, half, step, 0)


def low_lanes():
    return lax.broadcasted_iota(jnp.int32, (1, 128), 1) < 64


def swap_halves(tail):
    return pltpu.roll(tail, 64, 1)


def split_pair(x):
    tail = x[:, 512:640]
    even = jnp.concatenate([x[:, 0:256], tail], axis=1)
    odd = jnp.concatenate([x[:, 256:512], swap_halves(tail)], axis=1)
    return even, odd


def join_pair(even, odd):
    tail = jnp.where(low_lanes(), even[:, 256:384], swap_halves(odd[:, 256:384]))
    return even[:, 0:256], odd[:, 0:256], tail


def pad_weight(dst, src, row, col):
    ch = src.shape[-1]
    dst[pl.ds(row, dst_tile(ch)), pl.ds(col, dst_tile(ch))] = jnp.zeros(
        (dst_tile(ch), dst_tile(ch)), BF16
    )
    dst[pl.ds(row, ch), pl.ds(col, ch)] = src


def dst_tile(ch):
    return -(-ch // 128) * 128


def sources(m32, r0, n, frames, len_ref):
    cur = split_pair(m32[pl.ds(pl.multiple_of(r0 + PIX, 8), n), :])
    before = split_pair(m32[pl.ds(pl.multiple_of(r0, 8), n), :])[1]
    after = split_pair(m32[pl.ds(pl.multiple_of(r0 + 2 * PIX, 8), n), :])[0]
    even = ((r0 + lax.broadcasted_iota(jnp.int32, (n, 1), 0)) >> 3) * 2
    ids = [clip_ids(even + k, len_ref) for k in (-1, 0, 1, 2)]
    into = jnp.where((ids[0] == ids[1]) & (even > 0), 1.0, 0.0)
    inside = jnp.where(ids[1] == ids[2], 1.0, 0.0)
    out = jnp.where((ids[2] == ids[3]) & (even < frames - 2), 1.0, 0.0)
    stack = lambda a, b: jnp.concatenate([a, b], axis=0)
    previous = stack(before * into, cur[0] * inside)
    following = stack(cur[1] * inside, after * out)
    return previous, stack(*cur), following


def attention_kernel(
    len_ref, act_ref, wq_ref, wk_ref, wv_ref, wo_ref, tw_ref, o_ref, m_ref,
    n5, d5, m32, bias, wqkv, wo, tw,
):
    rows, ch2 = act_ref.shape
    ch = ch2 // 2
    pad = dst_tile(ch)
    units = rows // PIX
    frames = units * 2
    head = ch // HEADS
    for j, ref in enumerate((wq_ref, wk_ref, wv_ref)):
        pad_weight(wqkv, ref[...], 0, j * pad)
    pad_weight(wo, wo_ref[...], 0, 0)
    for j in range(3):
        pad_weight(tw, tw_ref[j], j * pad, 0)

    place = lambda axis: lax.broadcasted_iota(jnp.int32, (frames, frames), axis)
    frame = lambda i: jnp.where(i < units, 2 * i, 2 * (i - units) + 1)
    same = clip_ids(frame(place(0)), len_ref) == clip_ids(frame(place(1)), len_ref)
    bias[...] = jnp.where(same, 0.0, -1e30)

    chunk = 96
    low = low_lanes()

    def norm(i, _):
        at = pl.ds(pl.multiple_of(i * chunk, 8), chunk)
        x = act_ref[at, :].astype(F32)
        cols = [x[:, c * 128 : (c + 1) * 128] for c in range(5)]

        def sums(v):
            a = v[0] + v[1] + jnp.where(low, v[4], 0.0)
            b = v[2] + v[3] + jnp.where(low, 0.0, v[4])
            return [jnp.sum(t, axis=-1, keepdims=True) * (1.0 / ch) for t in (a, b)]

        def spread_out(a, b):
            return [a, a, b, b, jnp.where(low, a, b)]

        center = [v - m for v, m in zip(cols, spread_out(*sums(cols)))]
        var = sums([v * v for v in center])
        gain = spread_out(*[lax.rsqrt(v + 1e-05) for v in var])
        for c in range(5):
            n5[c, at, :] = (center[c] * gain[c]).astype(BF16).astype(F32)
        return 0

    lax.fori_loop(0, rows // chunk, norm, 0)

    factor = head ** (-0.5) * math.log2(math.e)
    lane = lax.broadcasted_iota(jnp.int32, (1, pad), 1)
    group = 2

    def pixels(i, _):
        parts = []
        for g in range(group):
            at = pl.ds(i * group + g, units, stride=PIX)
            cols = [n5[c, at, :] for c in range(5)]
            parts.append(jnp.concatenate([cols[0], cols[1], cols[4]], axis=1))
            parts.append(jnp.concatenate([cols[2], cols[3], swap_halves(cols[4])], axis=1))
        n = jnp.concatenate(parts, axis=0).astype(BF16)
        qkv = jnp.dot(n, wqkv[...], preferred_element_type=F32).astype(BF16)
        att = []
        for g in range(group):
            q, k, v = (
                qkv[g * frames : (g + 1) * frames, j * pad : (j + 1) * pad] for j in range(3)
            )
            acc = [None, None]
            for h in range(HEADS):
                w = 0 if (h + 1) * head <= 256 else 1
                win = slice(w * 128, w * 128 + 256)
                mine = (lane >= h * head) & (lane < (h + 1) * head)
                mine = jnp.where(mine, 1.0, 0.0).astype(BF16)
                s = lax.dot_general(
                    (q * mine)[:, win],
                    k[:, win],
                    (((1,), (1,)), ((), ())),
                    preferred_element_type=F32,
                )
                s = s * factor + bias[...]
                e = jnp.exp2(s - jnp.max(s, axis=-1, keepdims=True))
                prob = (e * (1.0 / jnp.sum(e, axis=-1, keepdims=True))).astype(BF16)
                got = jnp.dot(prob, (v * mine)[:, win], preferred_element_type=F32)
                acc[w] = got if acc[w] is None else acc[w] + got
            att.append(
                jnp.concatenate(
                    [acc[0][:, :128], acc[0][:, 128:] + acc[1][:, :128], acc[1][:, 128:]], axis=1
                )
            )
        att = jnp.concatenate(att, axis=0).astype(BF16)
        delta = jnp.dot(att, wo[...], preferred_element_type=F32)
        for g in range(group):
            at = pl.ds(i * group + g, units, stride=PIX)
            base = g * frames
            even, odd = delta[base : base + units], delta[base + units : base + frames]
            d5[0, at, :] = even[:, 0:128]
            d5[1, at, :] = even[:, 128:256]
            d5[2, at, :] = odd[:, 0:128]
            d5[3, at, :] = odd[:, 128:256]
            d5[4, at, :] = even[:, 256:384] + swap_halves(odd[:, 256:384])
        return 0

    lax.fori_loop(0, PIX // group, pixels, 0)

    m32[0:PIX, :] = jnp.zeros((PIX, ch2), F32)
    m32[rows + PIX : rows + 2 * PIX, :] = jnp.zeros((PIX, ch2), F32)

    def mix(i, _):
        at = pl.ds(pl.multiple_of(i * chunk, 8), chunk)
        delta = jnp.concatenate([d5[c, at, :] for c in range(5)], axis=1)
        m = (act_ref[at, :].astype(F32) + delta).astype(BF16)
        m_ref[at, :] = m
        m32[pl.ds(pl.multiple_of(i * chunk + PIX, 8), chunk), :] = m.astype(F32)
        return 0

    lax.fori_loop(0, rows // chunk, mix, 0)
    big = 192

    def temporal(i, _):
        r0 = i * big
        src = sources(m32, r0, big, frames, len_ref)
        total = src[1] + jnp.dot(
            jnp.concatenate([v.astype(BF16) for v in src], axis=1),
            tw[...],
            preferred_element_type=F32,
        )
        even, odd, tail = join_pair(total[:big], total[big:])
        at = pl.ds(pl.multiple_of(r0, 8), big)
        o_ref[at, 0:256] = even.astype(BF16)
        o_ref[at, 256:512] = odd.astype(BF16)
        o_ref[at, 512:640] = tail.astype(BF16)
        return 0

    lax.fori_loop(0, rows // big, temporal, 0)


def grad_kernel(len_ref, m_ref, cot_ref, o_ref, m32, total):
    rows, ch2 = cot_ref.shape
    ch = ch2 // 2
    pad = dst_tile(ch)
    frames = rows // PIX * 2
    big = 192
    m32[0:PIX, :] = jnp.zeros((PIX, ch2), F32)
    m32[rows + PIX : rows + 2 * PIX, :] = jnp.zeros((PIX, ch2), F32)

    def load(i, _):
        at = pl.ds(pl.multiple_of(i * big, 8), big)
        m32[pl.ds(pl.multiple_of(i * big + PIX, 8), big), :] = m_ref[at, :].astype(F32)
        return 0

    lax.fori_loop(0, rows // big, load, 0)
    total[...] = jnp.zeros_like(total)

    def step(i, _):
        r0 = i * big
        src = sources(m32, r0, big, frames, len_ref)
        src = jnp.concatenate([v.astype(BF16) for v in src], axis=1)
        cot = split_pair(cot_ref[pl.ds(pl.multiple_of(r0, 8), big), :].astype(F32))
        cot = jnp.concatenate(cot, axis=0).astype(BF16)
        total[...] += lax.dot_general(
            cot, src, (((0,), (0,)), ((), ())), preferred_element_type=F32
        )
        return 0

    lax.fori_loop(0, rows // big, step, 0)
    for j in range(3):
        o_ref[j * ch : (j + 1) * ch, :] = total[:, j * pad : (j + 1) * pad].T[:ch, :ch]


def tree(parts):
    while len(parts) > 1:
        parts = [parts[i] + parts[i + 1] for i in range(0, len(parts), 2)]
    return parts[0]


def swaps(n, k):
    return [(i, i ^ k) for i in range(n)]


def reduce_all(g):
    core = lax.axis_index("c")
    n_plane = lax.axis_size("y") * lax.axis_size("x")
    place = lax.axis_index("y") * lax.axis_size("x") + lax.axis_index("x")
    n_z = lax.axis_size("z")
    half = g.shape[0] // 2
    share = half // n_plane

    def cut(v, i, size):
        return lax.dynamic_slice_in_dim(v, i * size, size, 0)

    other = lax.ppermute(cut(g, 1 - core, half).astype(BF16), "c", swaps(2, 1))
    g = cut(g, core, half) + other.astype(F32)
    parts = [cut(g, place, share)]
    for k in range(1, n_plane):
        sent = cut(g, place ^ k, share).astype(BF16)
        parts.append(lax.ppermute(sent, PLANE, swaps(n_plane, k)).astype(F32))
    mine = tree(parts).astype(BF16)
    parts = [mine.astype(F32)]
    for k in range(1, n_z):
        parts.append(lax.ppermute(mine, "z", swaps(n_z, k)).astype(F32))
    total = tree(parts).astype(BF16)
    parts = [total] + [lax.ppermute(total, PLANE, swaps(n_plane, k)) for k in range(1, n_plane)]
    stacked = jnp.stack(parts)
    ordered = jnp.concatenate(
        [lax.dynamic_index_in_dim(stacked, place ^ j, 0, False) for j in range(n_plane)], 0
    )
    other = lax.ppermute(ordered, "c", swaps(2, 1))
    low = jnp.where(core == 0, ordered, other)
    high = jnp.where(core == 0, other, ordered)
    return jnp.concatenate([low, high], 0).astype(F32)


def exchange(x):
    shape = x.shape
    flat = x.reshape(shape[0], shape[1] * shape[2], shape[3])
    flat = lax.all_to_all(flat, SEQ, split_axis=0, concat_axis=0, tiled=True)
    return flat.reshape(shape)


def body(
    latents,
    clip_lengths,
    timesteps,
    spatial_weight,
    time_weight,
    query_weight,
    key_weight,
    value_weight,
    out_weight,
    temporal_weight,
    cotangent,
):
    f_dev, rows, across, ch = latents.shape
    shards = lax.axis_size("z") * lax.axis_size("y") * lax.axis_size("c")
    n_rows = lax.axis_size("x")
    assert rows * across <= shards * PIX and shards % rows == 0 and f_dev % 2 == 0
    half = f_dev // 2
    packed = jax.ShapeDtypeStruct((shards, half, PIX, 2 * ch), BF16)
    positions = f_dev * rows * across
    size = positions * ch * 2
    dense = 2 * positions * ch * ch

    row = lax.axis_index("x")
    if n_rows == 2:
        edge = jnp.where(row == 0, latents[:, rows - 1], latents[:, 0])
        got = lax.ppermute(edge, "x", swaps(2, 1))
        top, bot = got, got
    else:
        up = [(i, i + 1) for i in range(n_rows - 1)]
        top = lax.ppermute(latents[:, rows - 1], "x", up)
        bot = lax.ppermute(latents[:, 0], "x", [(j, i) for i, j in up])
    flags = jnp.stack([row > 0, row < n_rows - 1]).astype(jnp.int32)

    table = time_table(timesteps, time_weight)
    seq = (lax.axis_index("z") * lax.axis_size("y") + lax.axis_index("y")) * 2 + lax.axis_index("c")
    frame = seq * f_dev + jnp.arange(f_dev, dtype=jnp.int32)
    local_ids = jnp.sum(
        (frame[:, None] >= jnp.cumsum(clip_lengths)[None, :]).astype(jnp.int32), axis=1
    )
    active = call(
        conv_kernel,
        packed,
        [SMEM, SMEM, VMEM, VMEM, VMEM, VMEM, VMEM],
        flops=9 * dense,
        bytes_accessed=2 * size + 9 * ch * ch * 2,
    )(flags, local_ids, latents, top, bot, spatial_weight, table)
    active = exchange(active)

    cot = call(pack_kernel, packed, [VMEM], bytes_accessed=2 * size)(cotangent)
    cot, active = lax.optimization_barrier((cot, active))
    cot = exchange(cot)

    n_packed = shards * half * PIX
    flat = jax.ShapeDtypeStruct((n_packed, 2 * ch), BF16)
    units = n_packed // PIX
    tiles = -(-ch // 128)
    columns = pltpu.VMEM((5, n_packed, 128), F32)
    shifted = pltpu.VMEM((n_packed + 2 * PIX, 2 * ch), F32)
    pad = tiles * 128
    block, mixed = call(
        attention_kernel,
        (flat, flat),
        [SMEM] + [VMEM] * 6,
        scratch=[
            columns,
            columns,
            shifted,
            pltpu.VMEM((2 * units, 2 * units), F32),
            pltpu.VMEM((pad, 3 * pad), BF16),
            pltpu.VMEM((pad, pad), BF16),
            pltpu.VMEM((3 * pad, pad), BF16),
        ],
        flops=10 * dense,
        bytes_accessed=3 * size,
    )(
        clip_lengths,
        active.reshape(flat.shape),
        query_weight,
        key_weight,
        value_weight,
        out_weight,
        temporal_weight,
    )
    block = exchange(block.reshape(packed.shape))
    grads = call(
        grad_kernel,
        jax.ShapeDtypeStruct((3 * ch, ch), F32),
        [SMEM, VMEM, VMEM],
        scratch=[shifted, pltpu.VMEM((pad, 3 * pad), F32)],
        flops=3 * dense,
        bytes_accessed=2 * size + 3 * ch * ch * 4,
    )(clip_lengths, mixed, cot.reshape(flat.shape))
    grads = reduce_all(grads).reshape(3, ch, ch)
    block_out = call(
        unpack_kernel,
        jax.ShapeDtypeStruct(latents.shape, BF16),
        [VMEM],
        bytes_accessed=2 * size,
    )(block)
    return block_out, grads


def solution(mesh):
    n_seq, n_row = mesh.devices.shape
    grid = Mesh(mesh.devices.reshape(n_seq // 4, 2, 2, n_row), ("z", "y", "c", "x"))
    spread = P(SEQ, "x", None, None)
    in_specs = (spread,) + (P(),) * 9 + (spread,)
    return jax.shard_map(
        body, mesh=grid, in_specs=in_specs, out_specs=(spread, P()), check_vma=False
    )
```

```python
import math

import jax
import jax.numpy as jnp
from jax import lax
from jax.experimental import pallas as pl
from jax.experimental.pallas import tpu as pltpu
from jax.sharding import Mesh
from jax.sharding import PartitionSpec as P

HEADS = 8
CLIPS = 4
SEQ = ("z", "y", "c")
PLANE = ("y", "x")
BF16 = jnp.bfloat16
F32 = jnp.float32
VMEM = pltpu.VMEM
SMEM = pltpu.SMEM
PIX = 8
BIG = 384


def time_table(timesteps, time_weight):
    half_width = time_weight.shape[0] // 2
    frequency = jnp.exp(-math.log(10000.0) * jnp.arange(half_width, dtype=F32) / half_width)
    angles = timesteps.astype(F32)[:, None] * frequency[None, :]
    embedded = jnp.concatenate([jnp.cos(angles), jnp.sin(angles)], axis=1)
    return jnp.dot(embedded, time_weight.astype(F32), precision=lax.Precision.HIGHEST)


def call(kernel, out_shape, in_spaces, scratch=(), flops=0, bytes_accessed=0, grid=None, **kw):
    return pl.pallas_call(
        kernel,
        out_shape=out_shape,
        in_specs=[pl.BlockSpec(memory_space=s) for s in in_spaces],
        out_specs=jax.tree.map(lambda _: pl.BlockSpec(memory_space=VMEM), out_shape),
        scratch_shapes=scratch,
        cost_estimate=pl.CostEstimate(
            flops=flops, bytes_accessed=bytes_accessed, transcendentals=0
        ),
        compiler_params=pltpu.CompilerParams(vmem_limit_bytes=40 * 2**20),
        **kw,
    )


def clip_ids(frame, len_ref):
    bound = jnp.int32(0)
    ids = jnp.zeros(frame.shape, jnp.int32)
    for k in range(CLIPS):
        bound = bound + len_ref[k]
        ids = ids + jnp.where(frame >= bound, 1, 0)
    return ids


def take(row, g, real):
    if real == PIX:
        return row[g * PIX : (g + 1) * PIX]
    piece = row[g * real : (g + 1) * real].astype(F32)
    return jnp.concatenate([piece, jnp.zeros((PIX - real, row.shape[-1]), F32)], 0).astype(BF16)


def pack_kernel(x_ref, early_ref, late_ref):
    frames, rows, across, ch = x_ref.shape
    half = frames // 2
    real = across * rows // early_ref.shape[0]
    wide = 256
    for o_ref, start in ((early_ref, 0), (late_ref, half // 2)):

        def step(t, _, o_ref=o_ref, start=start):
            flat = [
                jnp.concatenate([x_ref[2 * (t + start) + q, i] for i in range(rows)], axis=0)
                for q in range(2)
            ]
            for q in range(2):
                store_groups(o_ref, t, slice(q * wide, (q + 1) * wide), flat[q][:, :wide], real)
            tail = jnp.concatenate([flat[0][:, wide:], flat[1][:, wide:]], axis=1)
            store_groups(o_ref, t, slice(2 * wide, 2 * ch), tail, real)
            return 0

        lax.fori_loop(0, half // 2, step, 0)


def unpack_kernel(x_ref, o_ref):
    frames, rows, across, ch = o_ref.shape
    half = frames // 2
    groups = x_ref.shape[0] // rows
    real = across // groups
    wide = ch // 128 * 128

    def join(blocks, low, high):
        if real == PIX:
            return jnp.concatenate([b[:, low:high] for b in blocks], 0)
        return jnp.concatenate([b[:real, low:high].astype(F32) for b in blocks], 0).astype(BF16)

    def step(t, _):
        for i in range(rows):
            blocks = [x_ref[i * groups + g, t] for g in range(groups)]
            o_ref[2 * t, i, :, 0:wide] = join(blocks, 0, wide)
            o_ref[2 * t, i, :, wide:ch] = join(blocks, 2 * wide, wide + ch)
            o_ref[2 * t + 1, i, :, 0:wide] = join(blocks, wide, 2 * wide)
            o_ref[2 * t + 1, i, :, wide:ch] = join(blocks, wide + ch, 2 * ch)
        return 0

    lax.fori_loop(0, half, step, 0)


def conv_weight_kernel(w_ref, o_ref):
    ch = w_ref.shape[-1]
    wide = 256
    rest = ch - wide
    none = jnp.zeros((ch, rest), BF16)
    for a in range(3):
        taps = [w_ref[a, b] for b in range(3)]
        tails = [
            jnp.concatenate([taps[0][:, wide:], taps[1][:, wide:]], axis=1),
            jnp.concatenate([taps[2][:, wide:], none], axis=1),
        ]
        for src, dst, size in ((0, a * wide, wide), (wide, 3 * wide + a * rest, rest)):
            rows = pl.ds(dst, size)
            for b in range(3):
                o_ref[rows, b * wide : (b + 1) * wide] = taps[b][src : src + size, :wide]
            for k in range(2):
                o_ref[rows, 3 * wide + k * 128 : 3 * wide + (k + 1) * 128] = tails[k][
                    src : src + size
                ]
    o_ref[3 * wide + 3 * rest :, :] = jnp.zeros((rest, 4 * wide), BF16)


def store_groups(o_ref, t, lanes, value, real):
    shards = o_ref.shape[0]
    value = value.astype(BF16)
    if real == PIX:
        o_ref[:, t, :, lanes] = value.reshape(shards, PIX, value.shape[-1])
        return
    for d in range(shards):
        o_ref[d, t, :, lanes] = take(value, d, real)


def silu(v):
    return 0.5 * v * (1.0 + jnp.tanh(0.5 * v))


def conv_kernel(flag_ref, len_ref, lat_ref, top_ref, bot_ref, w_ref, table_ref, o_ref):
    frames, rows, across, ch = lat_ref.shape
    real = across * rows // o_ref.shape[0]
    wide = 256
    pos = rows * across
    low = low_lanes()
    pairs = 3 if (frames // 2) % 3 == 0 else 1
    count = 2 * pairs

    def clip_of(frame):
        bound = jnp.int32(0)
        place = jnp.int32(0)
        for k in range(CLIPS):
            bound = bound + len_ref[k]
            place = place + jnp.where(frame >= bound, 1, 0)
        return jnp.minimum(place, CLIPS - 1)

    def step(g, _):
        kept = []
        for k in range(count):
            f = g * count + k
            top, bot = top_ref[f], bot_ref[f]
            top = jnp.where(flag_ref[0] > 0, top, jnp.zeros_like(top))
            bot = jnp.where(flag_ref[1] > 0, bot, jnp.zeros_like(bot))
            kept.append([top] + [lat_ref[f, i] for i in range(rows)] + [bot])
        window = [
            jnp.concatenate([r for lines in kept for r in lines[a : a + rows]], axis=0)
            for a in range(3)
        ]
        tails = [w[:, wide:] for w in window]
        x = jnp.concatenate(
            [w[:, :wide] for w in window]
            + [
                jnp.concatenate([tails[0], tails[1]], axis=1),
                jnp.concatenate([tails[2], jnp.zeros_like(tails[2])], axis=1),
            ],
            axis=1,
        )
        y = jnp.dot(x, w_ref[...], preferred_element_type=F32)
        n = count * pos
        col = lax.broadcasted_iota(jnp.int32, (n, 128), 0) & (across - 1)
        first, last = col == 0, col == across - 1

        def shifted(left, right):
            return jnp.where(first, 0.0, pltpu.roll(left, 1, 0)) + jnp.where(
                last, 0.0, pltpu.roll(right, n - 1, 0)
            )

        cols = []
        for c in range(2):
            at = lambda b: y[:, b * wide + c * 128 : b * wide + (c + 1) * 128]
            cols.append(shifted(at(0), at(2)) + at(1))
        mid = y[:, 3 * wide : 3 * wide + 128]
        side = shifted(mid, y[:, 3 * wide + 128 :])
        for k in range(pairs):
            t = g * pairs + k
            even = slice(2 * k * pos, (2 * k + 1) * pos)
            odd = slice((2 * k + 1) * pos, (2 * k + 2) * pos)
            base = flag_ref[2] + 2 * t
            emb = [table_ref[pl.ds(clip_of(base + q), 1), :] for q in range(2)]
            for q, rs in enumerate((even, odd)):
                for c in range(2):
                    lanes = slice(c * 128, (c + 1) * 128)
                    v = cols[c][rs] + emb[q][:, lanes]
                    got = window[1][rs, lanes].astype(F32) + silu(v)
                    dst = slice(q * wide + c * 128, q * wide + (c + 1) * 128)
                    store_groups(o_ref, t, dst, got, real)
            tail = jnp.where(
                low, side[even] + swap_halves(mid[even]), swap_halves(side[odd]) + mid[odd]
            )
            tail = tail + jnp.concatenate([emb[0][:, wide:], emb[1][:, wide:]], axis=1)
            res = jnp.concatenate([tails[1][even], tails[1][odd]], axis=1).astype(F32)
            store_groups(o_ref, t, slice(2 * wide, 2 * wide + 128), res + silu(tail), real)
        return 0

    lax.fori_loop(0, frames // count, step, 0)


def low_lanes():
    return lax.broadcasted_iota(jnp.int32, (1, 128), 1) < 64


def swap_halves(tail):
    return pltpu.roll(tail, 64, 1)


def split_pair(x):
    tail = x[:, 512:640]
    even = jnp.concatenate([x[:, 0:256], tail], axis=1)
    odd = jnp.concatenate([x[:, 256:512], swap_halves(tail)], axis=1)
    return even, odd


def join_pair(even, odd):
    tail = jnp.where(low_lanes(), even[:, 256:384], swap_halves(odd[:, 256:384]))
    return even[:, 0:256], odd[:, 0:256], tail


def pad_weight(dst, src, row, col):
    ch = src.shape[-1]
    dst[pl.ds(row, dst_tile(ch)), pl.ds(col, dst_tile(ch))] = jnp.zeros(
        (dst_tile(ch), dst_tile(ch)), BF16
    )
    dst[pl.ds(row, ch), pl.ds(col, ch)] = src


def dst_tile(ch):
    return -(-ch // 128) * 128


def sources(m32, r0, n, frames, len_ref):
    cur = split_pair(m32[pl.ds(pl.multiple_of(r0 + PIX, 8), n), :])
    before = split_pair(m32[pl.ds(pl.multiple_of(r0, 8), n), :])[1]
    after = split_pair(m32[pl.ds(pl.multiple_of(r0 + 2 * PIX, 8), n), :])[0]
    even = ((r0 + lax.broadcasted_iota(jnp.int32, (n, 1), 0)) >> 3) * 2
    ids = [clip_ids(even + k, len_ref) for k in (-1, 0, 1, 2)]
    into = jnp.where((ids[0] == ids[1]) & (even > 0), 1.0, 0.0)
    inside = jnp.where(ids[1] == ids[2], 1.0, 0.0)
    out = jnp.where((ids[2] == ids[3]) & (even < frames - 2), 1.0, 0.0)
    stack = lambda a, b: jnp.concatenate([a, b], axis=0)
    previous = stack(before * into, cur[0] * inside)
    following = stack(cur[1] * inside, after * out)
    return previous, stack(*cur), following


def prepare_kernel(len_ref, wq_ref, wk_ref, wv_ref, wo_ref, tw_ref, wqkv, wo, tw, bias):
    pad = wo.shape[0]
    frames = bias.shape[0]
    units = frames // 2
    for j, ref in enumerate((wq_ref, wk_ref, wv_ref)):
        pad_weight(wqkv, ref[...], 0, j * pad)
    pad_weight(wo, wo_ref[...], 0, 0)
    for j in range(3):
        pad_weight(tw, tw_ref[j], j * pad, 0)
    place = lambda axis: lax.broadcasted_iota(jnp.int32, (frames, frames), axis)
    frame = lambda i: jnp.where(i < units, 2 * i, 2 * (i - units) + 1)
    same = clip_ids(frame(place(0)), len_ref) == clip_ids(frame(place(1)), len_ref)
    bias[...] = jnp.where(same, 0.0, -1e30)


def attention_kernel(
    act_ref, wqkv, wo, bias, m_ref, n5, d5
):
    rows, ch2 = act_ref.shape
    ch = ch2 // 2
    pad = dst_tile(ch)
    units = rows // PIX
    frames = units * 2
    head = ch // HEADS
    chunk = 96
    low = low_lanes()

    def norm(i, _):
        at = pl.ds(pl.multiple_of(i * chunk, 8), chunk)
        x = act_ref[at, :].astype(F32)
        cols = [x[:, c * 128 : (c + 1) * 128] for c in range(5)]

        def sums(v):
            a = v[0] + v[1] + jnp.where(low, v[4], 0.0)
            b = v[2] + v[3] + jnp.where(low, 0.0, v[4])
            return [jnp.sum(t, axis=-1, keepdims=True) * (1.0 / ch) for t in (a, b)]

        def spread_out(a, b):
            return [a, a, b, b, jnp.where(low, a, b)]

        center = [v - m for v, m in zip(cols, spread_out(*sums(cols)))]
        var = sums([v * v for v in center])
        gain = spread_out(*[lax.rsqrt(v + 1e-05) for v in var])
        for c in range(5):
            n5[c, at, :] = (center[c] * gain[c]).astype(BF16).astype(F32)
        return 0

    lax.fori_loop(0, rows // chunk, norm, 0)

    factor = head ** (-0.5) * math.log2(math.e)
    lane = lax.broadcasted_iota(jnp.int32, (1, pad), 1)
    group = 4

    def pixels(i, _):
        parts = []
        for g in range(group):
            at = pl.ds(i * group + g, units, stride=PIX)
            cols = [n5[c, at, :] for c in range(5)]
            parts.append(jnp.concatenate([cols[0], cols[1], cols[4]], axis=1))
            parts.append(jnp.concatenate([cols[2], cols[3], swap_halves(cols[4])], axis=1))
        n = jnp.concatenate(parts, axis=0).astype(BF16)
        qkv = jnp.dot(n, wqkv[...], preferred_element_type=F32).astype(BF16)
        att = []
        for g in range(group):
            q, k, v = (
                qkv[g * frames : (g + 1) * frames, j * pad : (j + 1) * pad] for j in range(3)
            )
            acc = [None, None]
            for h in range(HEADS):
                w = 0 if (h + 1) * head <= 256 else 1
                win = slice(w * 128, w * 128 + 256)
                mine = (lane >= h * head) & (lane < (h + 1) * head)
                mine = jnp.where(mine, 1.0, 0.0).astype(BF16)
                s = lax.dot_general(
                    (q * mine)[:, win],
                    k[:, win],
                    (((1,), (1,)), ((), ())),
                    preferred_element_type=F32,
                )
                s = s * factor + bias[...]
                e = jnp.exp2(s - jnp.max(s, axis=-1, keepdims=True))
                prob = (e * (1.0 / jnp.sum(e, axis=-1, keepdims=True))).astype(BF16)
                got = jnp.dot(prob, (v * mine)[:, win], preferred_element_type=F32)
                acc[w] = got if acc[w] is None else acc[w] + got
            att.append(
                jnp.concatenate(
                    [acc[0][:, :128], acc[0][:, 128:] + acc[1][:, :128], acc[1][:, 128:]], axis=1
                )
            )
        att = jnp.concatenate(att, axis=0).astype(BF16)
        delta = jnp.dot(att, wo[...], preferred_element_type=F32)
        for g in range(group):
            at = pl.ds(i * group + g, units, stride=PIX)
            base = g * frames
            even, odd = delta[base : base + units], delta[base + units : base + frames]
            d5[0, at, :] = even[:, 0:128]
            d5[1, at, :] = even[:, 128:256]
            d5[2, at, :] = odd[:, 0:128]
            d5[3, at, :] = odd[:, 128:256]
            d5[4, at, :] = even[:, 256:384] + swap_halves(odd[:, 256:384])
        return 0

    lax.fori_loop(0, PIX // group, pixels, 0)

    def mix(i, _):
        at = pl.ds(pl.multiple_of(i * chunk, 8), chunk)
        delta = jnp.concatenate([d5[c, at, :] for c in range(5)], axis=1)
        m_ref[at, :] = (act_ref[at, :].astype(F32) + delta).astype(BF16)
        return 0

    lax.fori_loop(0, rows // chunk, mix, 0)


def temporal_kernel(
    core_ref, len_ref, m_ref, early_ref, late_ref, tw,
    o_ref, mine_ref, other_ref, m32, grad, full
):
    rows, ch2 = m_ref.shape
    ch = ch2 // 2
    pad = dst_tile(ch)
    frames = rows // PIX * 2
    big = BIG
    m32[0:PIX, :] = jnp.zeros((PIX, ch2), F32)
    m32[rows + PIX : rows + 2 * PIX, :] = jnp.zeros((PIX, ch2), F32)
    m32[PIX : rows + PIX, :] = m_ref[...].astype(F32)
    grad[...] = jnp.zeros_like(grad)

    def temporal(i, _):
        r0 = i * big
        src = sources(m32, r0, big, frames, len_ref)
        rounded = jnp.concatenate([v.astype(BF16) for v in src], axis=1)
        total = src[1] + jnp.dot(rounded, tw[...], preferred_element_type=F32)
        each = early_ref.shape[1]
        spans = big // (2 * each)
        cot = [ref[i * spans + k] for k in range(spans) for ref in (early_ref, late_ref)]
        cot = split_pair(jnp.concatenate([c.astype(F32) for c in cot], axis=0))
        cot = jnp.concatenate(cot, axis=0).astype(BF16)
        grad[...] += lax.dot_general(
            cot, rounded, (((0,), (0,)), ((), ())), preferred_element_type=F32
        )
        even, odd, tail = join_pair(total[:big], total[big:])
        at = pl.ds(pl.multiple_of(r0, 8), big)
        o_ref[at, 0:256] = even.astype(BF16)
        o_ref[at, 256:512] = odd.astype(BF16)
        o_ref[at, 512:640] = tail.astype(BF16)
        return 0

    lax.fori_loop(0, rows // big, temporal, 0)
    for j in range(3):
        full[j * ch : (j + 1) * ch, :] = grad[:, j * pad : (j + 1) * pad].T[:ch, :ch]
    core = core_ref[0]
    n = mine_ref.shape[0]
    mine_ref[...] = full[pl.ds(pl.multiple_of(core * n, 8), n), :]
    other_ref[...] = full[pl.ds(pl.multiple_of((1 - core) * n, 8), n), :].astype(BF16)


def tree(parts):
    while len(parts) > 1:
        parts = [parts[i] + parts[i + 1] for i in range(0, len(parts), 2)]
    return parts[0]


def swaps(n, k):
    return [(i, i ^ k) for i in range(n)]


def reduce_all(g, other):
    core = lax.axis_index("c")
    n_plane = lax.axis_size("y") * lax.axis_size("x")
    place = lax.axis_index("y") * lax.axis_size("x") + lax.axis_index("x")
    n_z = lax.axis_size("z")
    share = g.shape[0] // n_plane

    def cut(v, i, size):
        return lax.dynamic_slice_in_dim(v, i * size, size, 0)

    g = g + lax.ppermute(other, "c", swaps(2, 1)).astype(F32)
    parts = [cut(g, place, share)]
    for k in range(1, n_plane):
        sent = cut(g, place ^ k, share).astype(BF16)
        parts.append(lax.ppermute(sent, PLANE, swaps(n_plane, k)).astype(F32))
    total = tree(parts).astype(BF16)
    step = 1
    while step < n_z:
        got = lax.ppermute(total, "z", swaps(n_z, step))
        total = (total.astype(F32) + got.astype(F32)).astype(BF16)
        step *= 2
    parts = [total] + [lax.ppermute(total, PLANE, swaps(n_plane, k)) for k in range(1, n_plane)]
    stacked = jnp.stack(parts)
    ordered = jnp.concatenate(
        [lax.dynamic_index_in_dim(stacked, place ^ j, 0, False) for j in range(n_plane)], 0
    )
    other = lax.ppermute(ordered, "c", swaps(2, 1))
    low = jnp.where(core == 0, ordered, other)
    high = jnp.where(core == 0, other, ordered)
    return jnp.concatenate([low, high], 0).astype(F32)


def exchange(x):
    shape = x.shape
    flat = x.reshape(shape[0], shape[1] * shape[2], shape[3])
    flat = lax.all_to_all(flat, SEQ, split_axis=0, concat_axis=0, tiled=True)
    return flat.reshape(shape)


def body(
    latents,
    clip_lengths,
    timesteps,
    spatial_weight,
    time_weight,
    query_weight,
    key_weight,
    value_weight,
    out_weight,
    temporal_weight,
    cotangent,
):
    f_dev, rows, across, ch = latents.shape
    shards = lax.axis_size("z") * lax.axis_size("y") * lax.axis_size("c")
    n_rows = lax.axis_size("x")
    assert rows * across <= shards * PIX and shards % rows == 0 and f_dev % 2 == 0
    half = f_dev // 2
    packed = jax.ShapeDtypeStruct((shards, half, PIX, 2 * ch), BF16)
    positions = f_dev * rows * across
    size = positions * ch * 2
    dense = 2 * positions * ch * ch

    row = lax.axis_index("x")
    if n_rows == 2:
        edge = jnp.where(row == 0, latents[:, rows - 1], latents[:, 0])
        got = lax.ppermute(edge, "x", swaps(2, 1))
        top, bot = got, got
    else:
        up = [(i, i + 1) for i in range(n_rows - 1)]
        top = lax.ppermute(latents[:, rows - 1], "x", up)
        bot = lax.ppermute(latents[:, 0], "x", [(j, i) for i, j in up])
    seq = (lax.axis_index("z") * lax.axis_size("y") + lax.axis_index("y")) * 2 + lax.axis_index("c")
    flags = jnp.stack([row > 0, row < n_rows - 1, seq * f_dev]).astype(jnp.int32)
    table = time_table(timesteps, time_weight)
    taps = call(
        conv_weight_kernel,
        jax.ShapeDtypeStruct((1024, 1024), BF16),
        [VMEM],
        bytes_accessed=2 * size,
    )(spatial_weight)
    active = call(
        conv_kernel,
        packed,
        [SMEM, SMEM, VMEM, VMEM, VMEM, VMEM, VMEM],
        flops=9 * dense,
        bytes_accessed=2 * size + 9 * ch * ch * 2,
    )(flags, clip_lengths, latents, top, bot, taps, table)
    part = jax.ShapeDtypeStruct((shards, half // 2, PIX, 2 * ch), BF16)
    early, late = call(pack_kernel, (part, part), [VMEM], bytes_accessed=2 * size)(cotangent)
    early = exchange(early)
    early, active = lax.optimization_barrier((early, active))
    active = exchange(active)
    n_packed = shards * half * PIX
    flat = jax.ShapeDtypeStruct((n_packed, 2 * ch), BF16)
    units = n_packed // PIX
    tiles = -(-ch // 128)
    columns = pltpu.VMEM((5, n_packed, 128), F32)
    shifted = pltpu.VMEM((n_packed + 2 * PIX, 2 * ch), F32)
    pad = tiles * 128
    weights = [
        jax.ShapeDtypeStruct((pad, 3 * pad), BF16),
        jax.ShapeDtypeStruct((pad, pad), BF16),
        jax.ShapeDtypeStruct((3 * pad, pad), BF16),
        jax.ShapeDtypeStruct((2 * units, 2 * units), F32),
    ]
    prepared = call(prepare_kernel, weights, [SMEM] + [VMEM] * 5, bytes_accessed=4 * size)(
        clip_lengths, query_weight, key_weight, value_weight, out_weight, temporal_weight
    )
    late, active, prepared = lax.optimization_barrier((late, active, prepared))
    wqkv, wo, tw, bias = prepared
    late = exchange(late)
    mixed = call(
        attention_kernel,
        flat,
        [VMEM] * 4,
        scratch=[columns, columns],
        flops=7 * dense,
        bytes_accessed=4 * size,
    )(active.reshape(flat.shape), wqkv, wo, bias)
    half_grad = (3 * ch // 2, ch)
    block, mine, other = call(
        temporal_kernel,
        (flat, jax.ShapeDtypeStruct(half_grad, F32), jax.ShapeDtypeStruct(half_grad, BF16)),
        [SMEM, SMEM] + [VMEM] * 4,
        scratch=[
            shifted,
            pltpu.VMEM((pad, 3 * pad), F32),
            pltpu.VMEM((3 * ch, ch), F32),
        ],
        flops=6 * dense,
        bytes_accessed=4 * size,
    )(
        lax.axis_index("c")[None],
        clip_lengths,
        mixed,
        early.reshape(shards, half // 2 * PIX, 2 * ch),
        late.reshape(shards, half // 2 * PIX, 2 * ch),
        tw,
    )
    block = exchange(block.reshape(packed.shape))
    grads = reduce_all(mine, other).reshape(3, ch, ch)
    block_out = call(
        unpack_kernel,
        jax.ShapeDtypeStruct(latents.shape, BF16),
        [VMEM],
        bytes_accessed=2 * size,
    )(block)
    return block_out, grads


def solution(mesh):
    n_seq, n_row = mesh.devices.shape
    grid = Mesh(mesh.devices.reshape(n_seq // 4, 2, 2, n_row), ("z", "y", "c", "x"))
    spread = P(SEQ, "x", None, None)
    in_specs = (spread,) + (P(),) * 9 + (spread,)
    return jax.shard_map(
        body, mesh=grid, in_specs=in_specs, out_specs=(spread, P()), check_vma=False
    )
```

```python
import math

import jax
import jax.numpy as jnp
from jax import lax
from jax.experimental import pallas as pl
from jax.experimental.pallas import tpu as pltpu
from jax.sharding import Mesh
from jax.sharding import PartitionSpec as P

HEADS = 8
CLIPS = 4
SEQ = ("z", "y", "c")
PLANE = ("y", "x")
BF16 = jnp.bfloat16
F32 = jnp.float32
VMEM = pltpu.VMEM
SMEM = pltpu.SMEM
ANY = pl.ANY
PIX = 8
BIG = 384
VMEM_LIMIT = 24 * 2**20
WHOLE_VMEM = 60 * 2**20


def time_table(timesteps, time_weight):
    half_width = time_weight.shape[0] // 2
    frequency = jnp.exp(-math.log(10000.0) * jnp.arange(half_width, dtype=F32) / half_width)
    angles = timesteps.astype(F32)[:, None] * frequency[None, :]
    embedded = jnp.concatenate([jnp.cos(angles), jnp.sin(angles)], axis=1)
    return jnp.dot(embedded, time_weight.astype(F32), precision=lax.Precision.HIGHEST)


def call(kernel, out_shape, in_spaces, scratch=(), flops=0, bytes_accessed=0, out_space=VMEM):
    return pl.pallas_call(
        kernel,
        out_shape=out_shape,
        in_specs=[pl.BlockSpec(memory_space=s) for s in in_spaces],
        out_specs=jax.tree.map(lambda _: pl.BlockSpec(memory_space=out_space), out_shape),
        scratch_shapes=scratch,
        cost_estimate=pl.CostEstimate(
            flops=flops, bytes_accessed=bytes_accessed, transcendentals=0
        ),
        compiler_params=pltpu.CompilerParams(vmem_limit_bytes=VMEM_LIMIT if ANY not in in_spaces else WHOLE_VMEM),
    )


def clip_ids(frame, len_ref):
    bound = jnp.int32(0)
    ids = jnp.zeros(frame.shape, jnp.int32)
    for k in range(CLIPS):
        bound = bound + len_ref[k]
        ids = ids + jnp.where(frame >= bound, 1, 0)
    return ids


def take(row, g, real):
    if real == PIX:
        return row[g * PIX : (g + 1) * PIX]
    piece = row[g * real : (g + 1) * real].astype(F32)
    return jnp.concatenate([piece, jnp.zeros((PIX - real, row.shape[-1]), F32)], 0).astype(BF16)


def pack_kernel(x_ref, early_ref, late_ref):
    frames, rows, across, ch = x_ref.shape
    half = frames // 2
    real = across * rows // early_ref.shape[0]
    wide = 256
    for o_ref, start in ((early_ref, 0), (late_ref, half // 2)):

        def step(t, _, o_ref=o_ref, start=start):
            flat = [
                jnp.concatenate([x_ref[2 * (t + start) + q, i] for i in range(rows)], axis=0)
                for q in range(2)
            ]
            for q in range(2):
                store_groups(o_ref, t, slice(q * wide, (q + 1) * wide), flat[q][:, :wide], real)
            tail = jnp.concatenate([flat[0][:, wide:], flat[1][:, wide:]], axis=1)
            store_groups(o_ref, t, slice(2 * wide, 2 * ch), tail, real)
            return 0

        lax.fori_loop(0, half // 2, step, 0)


def unpack_kernel(x_ref, o_ref):
    frames, rows, across, ch = o_ref.shape
    half = frames // 2
    groups = x_ref.shape[0] // rows
    real = across // groups
    wide = ch // 128 * 128

    def join(blocks, low, high):
        if real == PIX:
            return jnp.concatenate([b[:, low:high] for b in blocks], 0)
        return jnp.concatenate([b[:real, low:high].astype(F32) for b in blocks], 0).astype(BF16)

    def step(t, _):
        for i in range(rows):
            blocks = [x_ref[i * groups + g, t] for g in range(groups)]
            o_ref[2 * t, i, :, 0:wide] = join(blocks, 0, wide)
            o_ref[2 * t, i, :, wide:ch] = join(blocks, 2 * wide, wide + ch)
            o_ref[2 * t + 1, i, :, 0:wide] = join(blocks, wide, 2 * wide)
            o_ref[2 * t + 1, i, :, wide:ch] = join(blocks, wide + ch, 2 * ch)
        return 0

    lax.fori_loop(0, half, step, 0)


def conv_weight_kernel(w_ref, o_ref):
    ch = w_ref.shape[-1]
    wide = 256
    rest = ch - wide
    none = jnp.zeros((ch, rest), BF16)
    for a in range(3):
        taps = [w_ref[a, b] for b in range(3)]
        tails = [
            jnp.concatenate([taps[0][:, wide:], taps[1][:, wide:]], axis=1),
            jnp.concatenate([taps[2][:, wide:], none], axis=1),
        ]
        for src, dst, size in ((0, a * wide, wide), (wide, 3 * wide + a * rest, rest)):
            rows = pl.ds(dst, size)
            for b in range(3):
                o_ref[rows, b * wide : (b + 1) * wide] = taps[b][src : src + size, :wide]
            for k in range(2):
                o_ref[rows, 3 * wide + k * 128 : 3 * wide + (k + 1) * 128] = tails[k][
                    src : src + size
                ]
    o_ref[3 * wide + 3 * rest :, :] = jnp.zeros((rest, 4 * wide), BF16)


def store_groups(o_ref, t, lanes, value, real):
    shards = o_ref.shape[0]
    value = value.astype(BF16)
    if real == PIX:
        o_ref[:, t, :, lanes] = value.reshape(shards, PIX, value.shape[-1])
        return
    for d in range(shards):
        o_ref[d, t, :, lanes] = take(value, d, real)


def silu(v):
    return 0.5 * v * (1.0 + jnp.tanh(0.5 * v))


def conv_kernel(flag_ref, len_ref, lat_ref, top_ref, bot_ref, w_ref, table_ref, o_ref):
    frames, rows, across, ch = lat_ref.shape
    real = across * rows // o_ref.shape[0]
    wide = 256
    pos = rows * across
    low = low_lanes()
    pairs = 3 if (frames // 2) % 3 == 0 else 1
    count = 2 * pairs

    def clip_of(frame):
        bound = jnp.int32(0)
        place = jnp.int32(0)
        for k in range(CLIPS):
            bound = bound + len_ref[k]
            place = place + jnp.where(frame >= bound, 1, 0)
        return jnp.minimum(place, CLIPS - 1)

    def step(g, _):
        kept = []
        for k in range(count):
            f = g * count + k
            top, bot = top_ref[f], bot_ref[f]
            top = jnp.where(flag_ref[0] > 0, top, jnp.zeros_like(top))
            bot = jnp.where(flag_ref[1] > 0, bot, jnp.zeros_like(bot))
            kept.append([top] + [lat_ref[f, i] for i in range(rows)] + [bot])
        window = [
            jnp.concatenate([r for lines in kept for r in lines[a : a + rows]], axis=0)
            for a in range(3)
        ]
        tails = [w[:, wide:] for w in window]
        x = jnp.concatenate(
            [w[:, :wide] for w in window]
            + [
                jnp.concatenate([tails[0], tails[1]], axis=1),
                jnp.concatenate([tails[2], jnp.zeros_like(tails[2])], axis=1),
            ],
            axis=1,
        )
        y = jnp.dot(x, w_ref[...], preferred_element_type=F32)
        n = count * pos
        col = lax.broadcasted_iota(jnp.int32, (n, 128), 0) & (across - 1)
        first, last = col == 0, col == across - 1

        def shifted(left, right):
            return jnp.where(first, 0.0, pltpu.roll(left, 1, 0)) + jnp.where(
                last, 0.0, pltpu.roll(right, n - 1, 0)
            )

        cols = []
        for c in range(2):
            at = lambda b: y[:, b * wide + c * 128 : b * wide + (c + 1) * 128]
            cols.append(shifted(at(0), at(2)) + at(1))
        mid = y[:, 3 * wide : 3 * wide + 128]
        side = shifted(mid, y[:, 3 * wide + 128 :])
        for k in range(pairs):
            t = g * pairs + k
            even = slice(2 * k * pos, (2 * k + 1) * pos)
            odd = slice((2 * k + 1) * pos, (2 * k + 2) * pos)
            base = flag_ref[2] + 2 * t
            emb = [table_ref[pl.ds(clip_of(base + q), 1), :] for q in range(2)]
            for q, rs in enumerate((even, odd)):
                for c in range(2):
                    lanes = slice(c * 128, (c + 1) * 128)
                    v = cols[c][rs] + emb[q][:, lanes]
                    got = window[1][rs, lanes].astype(F32) + silu(v)
                    dst = slice(q * wide + c * 128, q * wide + (c + 1) * 128)
                    store_groups(o_ref, t, dst, got, real)
            tail = jnp.where(
                low, side[even] + swap_halves(mid[even]), swap_halves(side[odd]) + mid[odd]
            )
            tail = tail + jnp.concatenate([emb[0][:, wide:], emb[1][:, wide:]], axis=1)
            res = jnp.concatenate([tails[1][even], tails[1][odd]], axis=1).astype(F32)
            store_groups(o_ref, t, slice(2 * wide, 2 * wide + 128), res + silu(tail), real)
        return 0

    lax.fori_loop(0, frames // count, step, 0)


def low_lanes():
    return lax.broadcasted_iota(jnp.int32, (1, 128), 1) < 64


def swap_halves(tail):
    return pltpu.roll(tail, 64, 1)


def split_pair(x):
    tail = x[:, 512:640]
    even = jnp.concatenate([x[:, 0:256], tail], axis=1)
    odd = jnp.concatenate([x[:, 256:512], swap_halves(tail)], axis=1)
    return even, odd


def join_pair(even, odd):
    tail = jnp.where(low_lanes(), even[:, 256:384], swap_halves(odd[:, 256:384]))
    return even[:, 0:256], odd[:, 0:256], tail


def pad_weight(dst, src, row, col):
    ch = src.shape[-1]
    dst[pl.ds(row, dst_tile(ch)), pl.ds(col, dst_tile(ch))] = jnp.zeros(
        (dst_tile(ch), dst_tile(ch)), BF16
    )
    dst[pl.ds(row, ch), pl.ds(col, ch)] = src


def dst_tile(ch):
    return -(-ch // 128) * 128


def sources(m32, r0, n, frames, len_ref):
    cur = split_pair(m32[pl.ds(pl.multiple_of(r0 + PIX, 8), n), :])
    before = split_pair(m32[pl.ds(pl.multiple_of(r0, 8), n), :])[1]
    after = split_pair(m32[pl.ds(pl.multiple_of(r0 + 2 * PIX, 8), n), :])[0]
    even = ((r0 + lax.broadcasted_iota(jnp.int32, (n, 1), 0)) >> 3) * 2
    ids = [clip_ids(even + k, len_ref) for k in (-1, 0, 1, 2)]
    into = jnp.where((ids[0] == ids[1]) & (even > 0), 1.0, 0.0)
    inside = jnp.where(ids[1] == ids[2], 1.0, 0.0)
    out = jnp.where((ids[2] == ids[3]) & (even < frames - 2), 1.0, 0.0)
    stack = lambda a, b: jnp.concatenate([a, b], axis=0)
    previous = stack(before * into, cur[0] * inside)
    following = stack(cur[1] * inside, after * out)
    return previous, stack(*cur), following


def prepare_kernel(len_ref, wq_ref, wk_ref, wv_ref, wo_ref, tw_ref, wqkv, wo, tw, bias):
    pad = wo.shape[0]
    frames = bias.shape[0]
    units = frames // 2
    for j, ref in enumerate((wq_ref, wk_ref, wv_ref)):
        pad_weight(wqkv, ref[...], 0, j * pad)
    pad_weight(wo, wo_ref[...], 0, 0)
    for j in range(3):
        pad_weight(tw, tw_ref[j], j * pad, 0)
    place = lambda axis: lax.broadcasted_iota(jnp.int32, (frames, frames), axis)
    frame = lambda i: jnp.where(i < units, 2 * i, 2 * (i - units) + 1)
    same = clip_ids(frame(place(0)), len_ref) == clip_ids(frame(place(1)), len_ref)
    bias[...] = jnp.where(same, 0.0, -1e30)


def attention_kernel(
    act_ref, wqkv_hbm, wo_hbm, bias_hbm, m_hbm, n5, d5, wqkv, wo, bias, m_ref, sems
):
    rows, ch2 = act_ref.shape
    ch = ch2 // 2
    pad = dst_tile(ch)
    units = rows // PIX
    frames = units * 2
    head = ch // HEADS
    fetches = [
        pltpu.make_async_copy(src, dst, sems.at[k])
        for k, (src, dst) in enumerate(((wqkv_hbm, wqkv), (wo_hbm, wo), (bias_hbm, bias)))
    ]
    for f in fetches:
        f.start()
    chunk = 96
    low = low_lanes()

    def norm(i, _):
        at = pl.ds(pl.multiple_of(i * chunk, 8), chunk)
        x = act_ref[at, :].astype(F32)
        cols = [x[:, c * 128 : (c + 1) * 128] for c in range(5)]

        def sums(v):
            a = v[0] + v[1] + jnp.where(low, v[4], 0.0)
            b = v[2] + v[3] + jnp.where(low, 0.0, v[4])
            return [jnp.sum(t, axis=-1, keepdims=True) * (1.0 / ch) for t in (a, b)]

        def spread_out(a, b):
            return [a, a, b, b, jnp.where(low, a, b)]

        center = [v - m for v, m in zip(cols, spread_out(*sums(cols)))]
        var = sums([v * v for v in center])
        gain = spread_out(*[lax.rsqrt(v + 1e-05) for v in var])
        for c in range(5):
            n5[c, at, :] = (center[c] * gain[c]).astype(BF16).astype(F32)
        return 0

    lax.fori_loop(0, rows // chunk, norm, 0)
    for f in fetches:
        f.wait()

    factor = head ** (-0.5) * math.log2(math.e)
    lane = lax.broadcasted_iota(jnp.int32, (1, pad), 1)
    group = 4

    def pixels(i, _):
        parts = []
        for g in range(group):
            at = pl.ds(i * group + g, units, stride=PIX)
            cols = [n5[c, at, :] for c in range(5)]
            parts.append(jnp.concatenate([cols[0], cols[1], cols[4]], axis=1))
            parts.append(jnp.concatenate([cols[2], cols[3], swap_halves(cols[4])], axis=1))
        n = jnp.concatenate(parts, axis=0).astype(BF16)
        qkv = jnp.dot(n, wqkv[...], preferred_element_type=F32).astype(BF16)
        att = []
        for g in range(group):
            q, k, v = (
                qkv[g * frames : (g + 1) * frames, j * pad : (j + 1) * pad] for j in range(3)
            )
            acc = [None, None]
            for h in range(HEADS):
                w = 0 if (h + 1) * head <= 256 else 1
                win = slice(w * 128, w * 128 + 256)
                mine = (lane >= h * head) & (lane < (h + 1) * head)
                mine = jnp.where(mine, 1.0, 0.0).astype(BF16)
                s = lax.dot_general(
                    (q * mine)[:, win],
                    k[:, win],
                    (((1,), (1,)), ((), ())),
                    preferred_element_type=F32,
                )
                s = s * factor + bias[...]
                e = jnp.exp2(s - jnp.max(s, axis=-1, keepdims=True))
                prob = (e * (1.0 / jnp.sum(e, axis=-1, keepdims=True))).astype(BF16)
                got = jnp.dot(prob, (v * mine)[:, win], preferred_element_type=F32)
                acc[w] = got if acc[w] is None else acc[w] + got
            att.append(
                jnp.concatenate(
                    [acc[0][:, :128], acc[0][:, 128:] + acc[1][:, :128], acc[1][:, 128:]], axis=1
                )
            )
        att = jnp.concatenate(att, axis=0).astype(BF16)
        delta = jnp.dot(att, wo[...], preferred_element_type=F32)
        for g in range(group):
            at = pl.ds(i * group + g, units, stride=PIX)
            base = g * frames
            even, odd = delta[base : base + units], delta[base + units : base + frames]
            d5[0, at, :] = even[:, 0:128]
            d5[1, at, :] = even[:, 128:256]
            d5[2, at, :] = odd[:, 0:128]
            d5[3, at, :] = odd[:, 128:256]
            d5[4, at, :] = even[:, 256:384] + swap_halves(odd[:, 256:384])
        return 0

    lax.fori_loop(0, PIX // group, pixels, 0)

    def mix(i, _):
        at = pl.ds(pl.multiple_of(i * chunk, 8), chunk)
        delta = jnp.concatenate([d5[c, at, :] for c in range(5)], axis=1)
        m_ref[at, :] = (act_ref[at, :].astype(F32) + delta).astype(BF16)
        return 0

    lax.fori_loop(0, rows // chunk, mix, 0)
    out = pltpu.make_async_copy(m_ref, m_hbm, sems.at[3])
    out.start()
    out.wait()


def shift_store(m_ref, m32):
    rows, ch2 = m_ref.shape
    m32[0:PIX, :] = jnp.zeros((PIX, ch2), F32)
    m32[rows + PIX : rows + 2 * PIX, :] = jnp.zeros((PIX, ch2), F32)
    m32[PIX : rows + PIX, :] = m_ref[...].astype(F32)


def temporal_kernel(len_ref, m_hbm, tw_hbm, o_ref, m32, m_ref, tw, sems):
    fetches = [
        pltpu.make_async_copy(src, dst, sems.at[k])
        for k, (src, dst) in enumerate(((m_hbm, m_ref), (tw_hbm, tw)))
    ]
    for f in fetches:
        f.start()
    for f in fetches:
        f.wait()
    rows, ch2 = m_ref.shape
    frames = rows // PIX * 2
    shift_store(m_ref, m32)

    def step(i, _):
        r0 = i * BIG
        src = sources(m32, r0, BIG, frames, len_ref)
        rounded = jnp.concatenate([v.astype(BF16) for v in src], axis=1)
        total = src[1] + jnp.dot(rounded, tw[...], preferred_element_type=F32)
        even, odd, tail = join_pair(total[:BIG], total[BIG:])
        at = pl.ds(pl.multiple_of(r0, 8), BIG)
        o_ref[at, 0:256] = even.astype(BF16)
        o_ref[at, 256:512] = odd.astype(BF16)
        o_ref[at, 512:640] = tail.astype(BF16)
        return 0

    lax.fori_loop(0, rows // BIG, step, 0)


def grad_kernel(
    core_ref, len_ref, m_hbm, early_hbm, late_hbm, mine_ref, other_ref,
    m32, grad, full, m_ref, early_ref, late_ref, sems,
):
    fetches = [
        pltpu.make_async_copy(src, dst, sems.at[k])
        for k, (src, dst) in enumerate(
            ((m_hbm, m_ref), (early_hbm, early_ref), (late_hbm, late_ref))
        )
    ]
    for f in fetches:
        f.start()
    fetches[0].wait()
    rows, ch2 = m_ref.shape
    ch = ch2 // 2
    pad = dst_tile(ch)
    frames = rows // PIX * 2
    shift_store(m_ref, m32)
    fetches[1].wait()
    fetches[2].wait()
    each = early_ref.shape[1]
    spans = BIG // (2 * each)

    def step(i, _):
        r0 = i * BIG
        src = sources(m32, r0, BIG, frames, len_ref)
        rounded = jnp.concatenate([v.astype(BF16) for v in src], axis=1)
        cot = [ref[i * spans + k] for k in range(spans) for ref in (early_ref, late_ref)]
        cot = split_pair(jnp.concatenate([c.astype(F32) for c in cot], axis=0))
        cot = jnp.concatenate(cot, axis=0).astype(BF16)
        got = lax.dot_general(cot, rounded, (((0,), (0,)), ((), ())), preferred_element_type=F32)

        @pl.when(i == 0)
        def _():
            grad[...] = got

        @pl.when(i > 0)
        def _():
            grad[...] += got

        return 0

    lax.fori_loop(0, rows // BIG, step, 0)
    for j in range(3):
        full[j * ch : (j + 1) * ch, :] = grad[:, j * pad : (j + 1) * pad].T[:ch, :ch]
    core = core_ref[0]
    n = mine_ref.shape[0]
    mine_ref[...] = full[pl.ds(pl.multiple_of(core * n, 8), n), :]
    other_ref[...] = full[pl.ds(pl.multiple_of((1 - core) * n, 8), n), :].astype(BF16)


def tree(parts):
    while len(parts) > 1:
        parts = [parts[i] + parts[i + 1] for i in range(0, len(parts), 2)]
    return parts[0]


def swaps(n, k):
    return [(i, i ^ k) for i in range(n)]


def ordered(parts, place):
    stacked = jnp.stack(parts)
    return jnp.concatenate(
        [lax.dynamic_index_in_dim(stacked, place ^ j, 0, False) for j in range(len(parts))], 0
    )


def reduce_all(g, other):
    core = lax.axis_index("c")
    n_plane = lax.axis_size("y") * lax.axis_size("x")
    place = lax.axis_index("y") * lax.axis_size("x") + lax.axis_index("x")
    n_z = lax.axis_size("z")
    share = g.shape[0] // n_plane

    def cut(v, i, size):
        return lax.dynamic_slice_in_dim(v, i * size, size, 0)

    g = g + lax.ppermute(other, "c", swaps(2, 1)).astype(F32)
    parts = [cut(g, place, share)]
    for k in range(1, n_plane):
        sent = cut(g, place ^ k, share).astype(BF16)
        parts.append(lax.ppermute(sent, PLANE, swaps(n_plane, k)).astype(F32))
    total = tree(parts)
    level = lax.axis_index("z")
    piece = -(-share // n_z // 8) * 8
    total = jnp.pad(total, ((0, piece * n_z - share), (0, 0)))
    parts = [cut(total, level, piece)]
    for k in range(1, n_z):
        sent = cut(total, level ^ k, piece).astype(BF16)
        parts.append(lax.ppermute(sent, "z", swaps(n_z, k)).astype(F32))
    total = tree(parts).astype(BF16)
    parts = [total] + [lax.ppermute(total, "z", swaps(n_z, k)) for k in range(1, n_z)]
    total = ordered(parts, level)[:share]
    parts = [total] + [lax.ppermute(total, PLANE, swaps(n_plane, k)) for k in range(1, n_plane)]
    own = ordered(parts, place)
    other = lax.ppermute(own, "c", swaps(2, 1))
    low = jnp.where(core == 0, own, other)
    high = jnp.where(core == 0, other, own)
    return jnp.concatenate([low, high], 0).astype(F32)


def exchange(x):
    shape = x.shape
    flat = x.reshape(shape[0], shape[1] * shape[2], shape[3])
    flat = lax.all_to_all(flat, SEQ, split_axis=0, concat_axis=0, tiled=True)
    return flat.reshape(shape)


def body(
    latents,
    clip_lengths,
    timesteps,
    spatial_weight,
    time_weight,
    query_weight,
    key_weight,
    value_weight,
    out_weight,
    temporal_weight,
    cotangent,
):
    f_dev, rows, across, ch = latents.shape
    shards = lax.axis_size("z") * lax.axis_size("y") * lax.axis_size("c")
    n_rows = lax.axis_size("x")
    assert rows * across <= shards * PIX and shards % rows == 0 and f_dev % 2 == 0
    half = f_dev // 2
    packed = jax.ShapeDtypeStruct((shards, half, PIX, 2 * ch), BF16)
    positions = f_dev * rows * across
    size = positions * ch * 2
    dense = 2 * positions * ch * ch

    row = lax.axis_index("x")
    if n_rows == 2:
        edge = lax.dynamic_index_in_dim(latents, (1 - row) * (rows - 1), 1, False)
        got = lax.ppermute(edge, "x", swaps(2, 1))
        top, bot = got, got
    else:
        up = [(i, i + 1) for i in range(n_rows - 1)]
        top = lax.ppermute(latents[:, rows - 1], "x", up)
        bot = lax.ppermute(latents[:, 0], "x", [(j, i) for i, j in up])
    seq = (lax.axis_index("z") * lax.axis_size("y") + lax.axis_index("y")) * 2 + lax.axis_index("c")
    flags = jnp.stack([row > 0, row < n_rows - 1, seq * f_dev]).astype(jnp.int32)
    table = time_table(timesteps, time_weight)
    taps = call(
        conv_weight_kernel,
        jax.ShapeDtypeStruct((1024, 1024), BF16),
        [VMEM],
        bytes_accessed=2 * size,
    )(spatial_weight)
    active = call(
        conv_kernel,
        packed,
        [SMEM, SMEM, VMEM, VMEM, VMEM, VMEM, VMEM],
        flops=9 * dense,
        bytes_accessed=2 * size + 9 * ch * ch * 2,
    )(flags, clip_lengths, latents, top, bot, taps, table)
    part = jax.ShapeDtypeStruct((shards, half // 2, PIX, 2 * ch), BF16)
    early, late = call(pack_kernel, (part, part), [VMEM], bytes_accessed=2 * size)(cotangent)
    early = exchange(early)
    early, active = lax.optimization_barrier((early, active))
    active = exchange(active)
    n_packed = shards * half * PIX
    flat = jax.ShapeDtypeStruct((n_packed, 2 * ch), BF16)
    units = n_packed // PIX
    tiles = -(-ch // 128)
    columns = pltpu.VMEM((5, n_packed, 128), F32)
    whole = pltpu.VMEM(flat.shape, BF16)
    shifted = pltpu.VMEM((n_packed + 2 * PIX, 2 * ch), F32)
    pad = tiles * 128
    weights = [
        jax.ShapeDtypeStruct((pad, 3 * pad), BF16),
        jax.ShapeDtypeStruct((pad, pad), BF16),
        jax.ShapeDtypeStruct((3 * pad, pad), BF16),
        jax.ShapeDtypeStruct((2 * units, 2 * units), F32),
    ]
    prepared = call(prepare_kernel, weights, [SMEM] + [VMEM] * 5, bytes_accessed=4 * size)(
        clip_lengths, query_weight, key_weight, value_weight, out_weight, temporal_weight
    )
    late, active, prepared = lax.optimization_barrier((late, active, prepared))
    wqkv, wo, tw, bias = prepared
    late = exchange(late)
    mixed = call(
        attention_kernel,
        flat,
        [VMEM] + [ANY] * 3,
        scratch=[columns, columns]
        + [pltpu.VMEM(w.shape, w.dtype) for w in (weights[0], weights[1], weights[3])]
        + [whole, pltpu.SemaphoreType.DMA((4,))],
        out_space=ANY,
        flops=7 * dense,
        bytes_accessed=4 * size,
    )(active.reshape(flat.shape), wqkv, wo, bias)
    half_grad = (3 * ch // 2, ch)
    mine, other = call(
        grad_kernel,
        (jax.ShapeDtypeStruct(half_grad, F32), jax.ShapeDtypeStruct(half_grad, BF16)),
        [SMEM, SMEM, ANY, ANY, ANY],
        scratch=[
            shifted,
            pltpu.VMEM((pad, 3 * pad), F32),
            pltpu.VMEM((3 * ch, ch), F32),
            whole,
            pltpu.VMEM((shards, half // 2 * PIX, 2 * ch), BF16),
            pltpu.VMEM((shards, half // 2 * PIX, 2 * ch), BF16),
            pltpu.SemaphoreType.DMA((3,)),
        ],
        flops=3 * dense,
        bytes_accessed=3 * size,
    )(
        lax.axis_index("c")[None],
        clip_lengths,
        mixed,
        early.reshape(shards, half // 2 * PIX, 2 * ch),
        late.reshape(shards, half // 2 * PIX, 2 * ch),
    )
    mixed, mine, other = lax.optimization_barrier((mixed, mine, other))
    block = call(
        temporal_kernel,
        flat,
        [SMEM, ANY, ANY],
        scratch=[
            shifted,
            whole,
            pltpu.VMEM(weights[2].shape, BF16),
            pltpu.SemaphoreType.DMA((2,)),
        ],
        flops=3 * dense,
        bytes_accessed=3 * size,
    )(clip_lengths, mixed, tw)
    block = exchange(block.reshape(packed.shape))
    block_out = call(
        unpack_kernel,
        jax.ShapeDtypeStruct(latents.shape, BF16),
        [VMEM],
        bytes_accessed=2 * size,
    )(block)
    grads = reduce_all(mine, other).reshape(3, ch, ch)
    return block_out, grads


def solution(mesh):
    n_seq, n_row = mesh.devices.shape
    grid = Mesh(mesh.devices.reshape(n_seq // 4, 2, 2, n_row), ("z", "y", "c", "x"))
    spread = P(SEQ, "x", None, None)
    in_specs = (spread,) + (P(),) * 9 + (spread,)
    return jax.shard_map(
        body, mesh=grid, in_specs=in_specs, out_specs=(spread, P()), check_vma=False
    )
```

```python
import math

import jax
import jax.numpy as jnp
from jax import lax
from jax.experimental import pallas as pl
from jax.experimental.pallas import tpu as pltpu
from jax.sharding import Mesh
from jax.sharding import PartitionSpec as P

HEADS = 8
CLIPS = 4
SEQ = ("z", "y", "c")
PLANE = ("y", "x")
BF16 = jnp.bfloat16
F32 = jnp.float32
VMEM = pltpu.VMEM
SMEM = pltpu.SMEM
ANY = pl.ANY
PIX = 8
VMEM_LIMIT = 24 * 2**20
WHOLE_VMEM = 60 * 2**20


def time_table(timesteps, time_weight):
    half_width = time_weight.shape[0] // 2
    frequency = jnp.exp(-math.log(10000.0) * jnp.arange(half_width, dtype=F32) / half_width)
    angles = timesteps.astype(F32)[:, None] * frequency[None, :]
    embedded = jnp.concatenate([jnp.cos(angles), jnp.sin(angles)], axis=1)
    return jnp.dot(embedded, time_weight.astype(F32), precision=lax.Precision.HIGHEST)


def call(kernel, out_shape, in_spaces, scratch=(), flops=0, bytes_accessed=0, out_space=VMEM):
    return pl.pallas_call(
        kernel,
        out_shape=out_shape,
        in_specs=[pl.BlockSpec(memory_space=s) for s in in_spaces],
        out_specs=jax.tree.map(lambda _: pl.BlockSpec(memory_space=out_space), out_shape),
        scratch_shapes=scratch,
        cost_estimate=pl.CostEstimate(
            flops=flops, bytes_accessed=bytes_accessed, transcendentals=0
        ),
        compiler_params=pltpu.CompilerParams(vmem_limit_bytes=VMEM_LIMIT if ANY not in in_spaces else WHOLE_VMEM),
    )


def clip_ids(frame, len_ref):
    bound = jnp.int32(0)
    ids = jnp.zeros(frame.shape, jnp.int32)
    for k in range(CLIPS):
        bound = bound + len_ref[k]
        ids = ids + jnp.where(frame >= bound, 1, 0)
    return ids


def take(row, g, real):
    if real == PIX:
        return row[g * PIX : (g + 1) * PIX]
    piece = row[g * real : (g + 1) * real].astype(F32)
    return jnp.concatenate([piece, jnp.zeros((PIX - real, row.shape[-1]), F32)], 0).astype(BF16)


def pack_kernel(x_ref, o_ref):
    frames, rows, across, ch = x_ref.shape
    real = across * rows // o_ref.shape[0]
    wide = 256

    def step(t, _):
        flat = [
            jnp.concatenate([x_ref[2 * t + q, i] for i in range(rows)], axis=0) for q in range(2)
        ]
        for q in range(2):
            store_groups(o_ref, t, slice(q * wide, (q + 1) * wide), flat[q][:, :wide], real)
        tail = jnp.concatenate([flat[0][:, wide:], flat[1][:, wide:]], axis=1)
        store_groups(o_ref, t, slice(2 * wide, 2 * ch), tail, real)
        return 0

    lax.fori_loop(0, frames // 2, step, 0)


def conv_weight_kernel(w_ref, o_ref):
    ch = w_ref.shape[-1]
    wide = 256
    rest = ch - wide
    none = jnp.zeros((ch, rest), BF16)
    for a in range(3):
        taps = [w_ref[a, b] for b in range(3)]
        tails = [
            jnp.concatenate([taps[0][:, wide:], taps[1][:, wide:]], axis=1),
            jnp.concatenate([taps[2][:, wide:], none], axis=1),
        ]
        for src, dst, size in ((0, a * wide, wide), (wide, 3 * wide + a * rest, rest)):
            rows = pl.ds(dst, size)
            for b in range(3):
                o_ref[rows, b * wide : (b + 1) * wide] = taps[b][src : src + size, :wide]
            for k in range(2):
                o_ref[rows, 3 * wide + k * 128 : 3 * wide + (k + 1) * 128] = tails[k][
                    src : src + size
                ]
    o_ref[3 * wide + 3 * rest :, :] = jnp.zeros((rest, 4 * wide), BF16)


def store_groups(o_ref, t, lanes, value, real):
    shards = o_ref.shape[0]
    value = value.astype(BF16)
    if real == PIX:
        o_ref[:, t, :, lanes] = value.reshape(shards, PIX, value.shape[-1])
        return
    for d in range(shards):
        o_ref[d, t, :, lanes] = take(value, d, real)


def silu(v):
    return 0.5 * v * (1.0 + jnp.tanh(0.5 * v))


def conv_kernel(flag_ref, len_ref, lat_ref, top_ref, bot_ref, w_ref, table_ref, o_ref):
    frames, rows, across, ch = lat_ref.shape
    real = across * rows // o_ref.shape[0]
    wide = 256
    pos = rows * across
    low = low_lanes()
    pairs = 3 if (frames // 2) % 3 == 0 else 1
    count = 2 * pairs

    def clip_of(frame):
        bound = jnp.int32(0)
        place = jnp.int32(0)
        for k in range(CLIPS):
            bound = bound + len_ref[k]
            place = place + jnp.where(frame >= bound, 1, 0)
        return jnp.minimum(place, CLIPS - 1)

    def step(g, _):
        kept = []
        for k in range(count):
            f = g * count + k
            top, bot = top_ref[f], bot_ref[f]
            top = jnp.where(flag_ref[0] > 0, top, jnp.zeros_like(top))
            bot = jnp.where(flag_ref[1] > 0, bot, jnp.zeros_like(bot))
            kept.append([top] + [lat_ref[f, i] for i in range(rows)] + [bot])
        window = [
            jnp.concatenate([r for lines in kept for r in lines[a : a + rows]], axis=0)
            for a in range(3)
        ]
        tails = [w[:, wide:] for w in window]
        x = jnp.concatenate(
            [w[:, :wide] for w in window]
            + [
                jnp.concatenate([tails[0], tails[1]], axis=1),
                jnp.concatenate([tails[2], jnp.zeros_like(tails[2])], axis=1),
            ],
            axis=1,
        )
        y = jnp.dot(x, w_ref[...], preferred_element_type=F32)
        n = count * pos
        col = lax.broadcasted_iota(jnp.int32, (n, 128), 0) & (across - 1)
        first, last = col == 0, col == across - 1

        def shifted(left, right):
            return jnp.where(first, 0.0, pltpu.roll(left, 1, 0)) + jnp.where(
                last, 0.0, pltpu.roll(right, n - 1, 0)
            )

        cols = []
        for c in range(2):
            at = lambda b: y[:, b * wide + c * 128 : b * wide + (c + 1) * 128]
            cols.append(shifted(at(0), at(2)) + at(1))
        mid = y[:, 3 * wide : 3 * wide + 128]
        side = shifted(mid, y[:, 3 * wide + 128 :])
        for k in range(pairs):
            t = g * pairs + k
            even = slice(2 * k * pos, (2 * k + 1) * pos)
            odd = slice((2 * k + 1) * pos, (2 * k + 2) * pos)
            base = flag_ref[2] + 2 * t
            emb = [table_ref[pl.ds(clip_of(base + q), 1), :] for q in range(2)]
            for q, rs in enumerate((even, odd)):
                for c in range(2):
                    lanes = slice(c * 128, (c + 1) * 128)
                    v = cols[c][rs] + emb[q][:, lanes]
                    got = window[1][rs, lanes].astype(F32) + silu(v)
                    dst = slice(q * wide + c * 128, q * wide + (c + 1) * 128)
                    store_groups(o_ref, t, dst, got, real)
            tail = jnp.where(
                low, side[even] + swap_halves(mid[even]), swap_halves(side[odd]) + mid[odd]
            )
            tail = tail + jnp.concatenate([emb[0][:, wide:], emb[1][:, wide:]], axis=1)
            res = jnp.concatenate([tails[1][even], tails[1][odd]], axis=1).astype(F32)
            store_groups(o_ref, t, slice(2 * wide, 2 * wide + 128), res + silu(tail), real)
        return 0

    lax.fori_loop(0, frames // count, step, 0)


def low_lanes():
    return lax.broadcasted_iota(jnp.int32, (1, 128), 1) < 64


def swap_halves(tail):
    return pltpu.roll(tail, 64, 1)


def split_pair(x):
    tail = x[:, 512:640]
    even = jnp.concatenate([x[:, 0:256], tail], axis=1)
    odd = jnp.concatenate([x[:, 256:512], swap_halves(tail)], axis=1)
    return even, odd


def join_pair(even, odd):
    tail = jnp.where(low_lanes(), even[:, 256:384], swap_halves(odd[:, 256:384]))
    return even[:, 0:256], odd[:, 0:256], tail


def pad_weight(dst, src, row, col):
    ch = src.shape[-1]
    dst[pl.ds(row, dst_tile(ch)), pl.ds(col, dst_tile(ch))] = jnp.zeros(
        (dst_tile(ch), dst_tile(ch)), BF16
    )
    dst[pl.ds(row, ch), pl.ds(col, ch)] = src


def dst_tile(ch):
    return -(-ch // 128) * 128


def spread_units(m_ref, m32):
    own = m_ref.shape[1] - PIX
    for s in range(m_ref.shape[0]):
        x = m_ref[s].astype(F32)
        m32[s, PIX : PIX + own, :] = x[:own]
        m32[s, 0:PIX, :] = x[own:]
        m32[s, PIX + own :, :] = x[own:]


def sources(m32, start, count, base, frames, len_ref):
    own = m32.shape[1] - 2 * PIX

    def rows(first):
        x = m32[pl.ds(start, count), first : first + own, :]
        return split_pair(x.reshape(count * own, x.shape[-1]))

    cur, before, after = rows(PIX), rows(0)[1], rows(2 * PIX)[0]
    unit = lax.broadcasted_iota(jnp.int32, (count, own, 1), 1).reshape(count * own, 1) >> 3
    even = base + 2 * unit
    ids = [clip_ids(even + k, len_ref) for k in (-1, 0, 1, 2)]
    into = jnp.where((ids[0] == ids[1]) & (even > 0), 1.0, 0.0)
    inside = jnp.where(ids[1] == ids[2], 1.0, 0.0)
    out = jnp.where((ids[2] == ids[3]) & (even < frames - 2), 1.0, 0.0)
    stack = lambda a, b: jnp.concatenate([a, b], axis=0)
    previous = stack(before * into, cur[0] * inside)
    following = stack(cur[1] * inside, after * out)
    return previous, stack(*cur), following


def prepare_kernel(len_ref, wq_ref, wk_ref, wv_ref, wo_ref, tw_ref, wqkv, wo, tw, bias):
    pad = wo.shape[0]
    frames = bias.shape[0]
    units = frames // 2
    for j, ref in enumerate((wq_ref, wk_ref, wv_ref)):
        pad_weight(wqkv, ref[...], 0, j * pad)
    pad_weight(wo, wo_ref[...], 0, 0)
    for j in range(3):
        pad_weight(tw, tw_ref[j], j * pad, 0)
    place = lambda axis: lax.broadcasted_iota(jnp.int32, (frames, frames), axis)
    frame = lambda i: jnp.where(i < units, 2 * i, 2 * (i - units) + 1)
    same = clip_ids(frame(place(0)), len_ref) == clip_ids(frame(place(1)), len_ref)
    bias[...] = jnp.where(same, 0.0, -1e30)


def attention_kernel(
    act_ref, wqkv_hbm, wo_hbm, bias_hbm, o_ref, n5, d5, wqkv, wo, bias, m32, sems
):
    rows, ch2 = act_ref.shape
    ch = ch2 // 2
    pad = dst_tile(ch)
    units = rows // PIX
    frames = units * 2
    head = ch // HEADS
    fetches = [
        pltpu.make_async_copy(src, dst, sems.at[k])
        for k, (src, dst) in enumerate(((wqkv_hbm, wqkv), (wo_hbm, wo), (bias_hbm, bias)))
    ]
    for f in fetches:
        f.start()
    chunk = 96
    low = low_lanes()

    def norm(i, _):
        at = pl.ds(pl.multiple_of(i * chunk, 8), chunk)
        x = act_ref[at, :].astype(F32)
        cols = [x[:, c * 128 : (c + 1) * 128] for c in range(5)]

        def sums(v):
            a = v[0] + v[1] + jnp.where(low, v[4], 0.0)
            b = v[2] + v[3] + jnp.where(low, 0.0, v[4])
            return [jnp.sum(t, axis=-1, keepdims=True) * (1.0 / ch) for t in (a, b)]

        def spread_out(a, b):
            return [a, a, b, b, jnp.where(low, a, b)]

        center = [v - m for v, m in zip(cols, spread_out(*sums(cols)))]
        var = sums([v * v for v in center])
        gain = spread_out(*[lax.rsqrt(v + 1e-05) for v in var])
        for c in range(5):
            n5[c, at, :] = (center[c] * gain[c]).astype(BF16).astype(F32)
        return 0

    lax.fori_loop(0, rows // chunk, norm, 0)
    for f in fetches:
        f.wait()

    factor = head ** (-0.5) * math.log2(math.e)
    lane = lax.broadcasted_iota(jnp.int32, (1, pad), 1)
    group = 4

    def pixels(i, _):
        parts = []
        for g in range(group):
            at = pl.ds(i * group + g, units, stride=PIX)
            cols = [n5[c, at, :] for c in range(5)]
            parts.append(jnp.concatenate([cols[0], cols[1], cols[4]], axis=1))
            parts.append(jnp.concatenate([cols[2], cols[3], swap_halves(cols[4])], axis=1))
        n = jnp.concatenate(parts, axis=0).astype(BF16)
        qkv = jnp.dot(n, wqkv[...], preferred_element_type=F32).astype(BF16)
        att = []
        for g in range(group):
            q, k, v = (
                qkv[g * frames : (g + 1) * frames, j * pad : (j + 1) * pad] for j in range(3)
            )
            acc = [None, None]
            for h in range(HEADS):
                w = 0 if (h + 1) * head <= 256 else 1
                win = slice(w * 128, w * 128 + 256)
                mine = (lane >= h * head) & (lane < (h + 1) * head)
                mine = jnp.where(mine, 1.0, 0.0).astype(BF16)
                s = lax.dot_general(
                    (q * mine)[:, win],
                    k[:, win],
                    (((1,), (1,)), ((), ())),
                    preferred_element_type=F32,
                )
                s = s * factor + bias[...]
                e = jnp.exp2(s - jnp.max(s, axis=-1, keepdims=True))
                prob = (e * (1.0 / jnp.sum(e, axis=-1, keepdims=True))).astype(BF16)
                got = jnp.dot(prob, (v * mine)[:, win], preferred_element_type=F32)
                acc[w] = got if acc[w] is None else acc[w] + got
            att.append(
                jnp.concatenate(
                    [acc[0][:, :128], acc[0][:, 128:] + acc[1][:, :128], acc[1][:, 128:]], axis=1
                )
            )
        att = jnp.concatenate(att, axis=0).astype(BF16)
        delta = jnp.dot(att, wo[...], preferred_element_type=F32)
        for g in range(group):
            at = pl.ds(i * group + g, units, stride=PIX)
            base = g * frames
            even, odd = delta[base : base + units], delta[base + units : base + frames]
            d5[0, at, :] = even[:, 0:128]
            d5[1, at, :] = even[:, 128:256]
            d5[2, at, :] = odd[:, 0:128]
            d5[3, at, :] = odd[:, 128:256]
            d5[4, at, :] = even[:, 256:384] + swap_halves(odd[:, 256:384])
        return 0

    lax.fori_loop(0, PIX // group, pixels, 0)

    own = o_ref.shape[1] - PIX

    def mix(i, _):
        at = pl.ds(pl.multiple_of(i * own, 8), own)
        delta = jnp.concatenate([d5[c, at, :] for c in range(5)], axis=1)
        m = (act_ref[at, :].astype(F32) + delta).astype(BF16)
        o_ref[i, 0:own, :] = m
        m32[at, :] = m.astype(F32)
        return 0

    lax.fori_loop(0, rows // own, mix, 0)

    def edges(i, _):
        after = m32[pl.ds(pl.multiple_of(jnp.minimum((i + 1) * own, rows - PIX), 8), PIX), :]
        before = m32[pl.ds(pl.multiple_of(jnp.maximum(i * own - PIX, 0), 8), PIX), :]
        tail = jnp.where(low, after[:, 512:640], before[:, 512:640])
        edge = jnp.concatenate([after[:, 0:256], before[:, 256:512], tail], axis=1)
        o_ref[i, own : own + PIX, :] = edge.astype(BF16)
        return 0

    lax.fori_loop(0, rows // own, edges, 0)


def temporal_kernel(flag_ref, len_ref, m_ref, tw, o_ref, m32):
    shards = m_ref.shape[0]
    frames, rows, across, ch = o_ref.shape
    units = frames // 2
    groups = shards // rows
    real = across // groups
    total_frames = flag_ref[3]
    spread_units(m_ref, m32)

    def join(blocks):
        return jnp.concatenate([b[:real] for b in blocks], axis=0).astype(BF16)

    def step(i, _):
        src = sources(m32, i * groups, groups, flag_ref[2], total_frames, len_ref)
        rounded = jnp.concatenate([v.astype(BF16) for v in src], axis=1)
        total = src[1] + jnp.dot(rounded, tw[...], preferred_element_type=F32)
        total = total.reshape(2, groups, units, PIX, total.shape[-1])
        for u in range(units):
            for q in range(2):
                got = join([total[q, g, u] for g in range(groups)])
                o_ref[2 * u + q, i] = got[:, :ch]
        return 0

    lax.fori_loop(0, rows, step, 0)


def grad_kernel(flag_ref, len_ref, m_ref, cot_ref, mine_ref, other_ref, m32, grad, full):
    shards = m_ref.shape[0]
    ch = m_ref.shape[-1] // 2
    pad = dst_tile(ch)
    count = 8
    spread_units(m_ref, m32)

    def step(i, _):
        src = sources(m32, i * count, count, flag_ref[2], flag_ref[3], len_ref)
        rounded = jnp.concatenate([v.astype(BF16) for v in src], axis=1)
        cot = cot_ref[pl.ds(i * count, count), :, :].astype(F32)
        cot = split_pair(cot.reshape(-1, 2 * ch))
        cot = jnp.concatenate(cot, axis=0).astype(BF16)
        got = lax.dot_general(cot, rounded, (((0,), (0,)), ((), ())), preferred_element_type=F32)

        @pl.when(i == 0)
        def _():
            grad[...] = got

        @pl.when(i > 0)
        def _():
            grad[...] += got

        return 0

    lax.fori_loop(0, shards // count, step, 0)
    for j in range(3):
        full[j * ch : (j + 1) * ch, :] = grad[:, j * pad : (j + 1) * pad].T[:ch, :ch]
    core = flag_ref[4]
    n = mine_ref.shape[0]
    mine_ref[...] = full[pl.ds(pl.multiple_of(core * n, 8), n), :]
    other_ref[...] = full[pl.ds(pl.multiple_of((1 - core) * n, 8), n), :].astype(BF16)


def tree(parts):
    while len(parts) > 1:
        parts = [parts[i] + parts[i + 1] for i in range(0, len(parts), 2)]
    return parts[0]


def swaps(n, k):
    return [(i, i ^ k) for i in range(n)]


def ordered(parts, place):
    stacked = jnp.stack(parts)
    return jnp.concatenate(
        [lax.dynamic_index_in_dim(stacked, place ^ j, 0, False) for j in range(len(parts))], 0
    )


def reduce_all(g, other):
    core = lax.axis_index("c")
    n_plane = lax.axis_size("y") * lax.axis_size("x")
    place = lax.axis_index("y") * lax.axis_size("x") + lax.axis_index("x")
    n_z = lax.axis_size("z")
    share = g.shape[0] // n_plane

    def cut(v, i, size):
        return lax.dynamic_slice_in_dim(v, i * size, size, 0)

    g = g + lax.ppermute(other, "c", swaps(2, 1)).astype(F32)
    parts = [cut(g, place, share)]
    for k in range(1, n_plane):
        sent = cut(g, place ^ k, share).astype(BF16)
        parts.append(lax.ppermute(sent, PLANE, swaps(n_plane, k)).astype(F32))
    mine = tree(parts).astype(BF16)
    parts = [mine.astype(F32)]
    for k in range(1, n_z):
        parts.append(lax.ppermute(mine, "z", swaps(n_z, k)).astype(F32))
    total = tree(parts).astype(BF16)
    parts = [total] + [lax.ppermute(total, PLANE, swaps(n_plane, k)) for k in range(1, n_plane)]
    own = ordered(parts, place)
    other = lax.ppermute(own, "c", swaps(2, 1))
    low = jnp.where(core == 0, own, other)
    high = jnp.where(core == 0, other, own)
    return jnp.concatenate([low, high], 0).astype(F32)


def exchange(x):
    shape = x.shape
    flat = x.reshape(shape[0], shape[1] * shape[2], shape[3])
    flat = lax.all_to_all(flat, SEQ, split_axis=0, concat_axis=0, tiled=True)
    return flat.reshape(shape)


def body(
    latents,
    clip_lengths,
    timesteps,
    spatial_weight,
    time_weight,
    query_weight,
    key_weight,
    value_weight,
    out_weight,
    temporal_weight,
    cotangent,
):
    f_dev, rows, across, ch = latents.shape
    shards = lax.axis_size("z") * lax.axis_size("y") * lax.axis_size("c")
    n_rows = lax.axis_size("x")
    assert rows * across <= shards * PIX and shards % rows == 0 and f_dev % 2 == 0
    half = f_dev // 2
    packed = jax.ShapeDtypeStruct((shards, half, PIX, 2 * ch), BF16)
    positions = f_dev * rows * across
    size = positions * ch * 2
    dense = 2 * positions * ch * ch

    row = lax.axis_index("x")
    if n_rows == 2:
        edge = lax.dynamic_index_in_dim(latents, (1 - row) * (rows - 1), 1, False)
        got = lax.ppermute(edge, "x", swaps(2, 1))
        top, bot = got, got
    else:
        up = [(i, i + 1) for i in range(n_rows - 1)]
        top = lax.ppermute(latents[:, rows - 1], "x", up)
        bot = lax.ppermute(latents[:, 0], "x", [(j, i) for i, j in up])
    seq = (lax.axis_index("z") * lax.axis_size("y") + lax.axis_index("y")) * 2 + lax.axis_index("c")
    flags = jnp.stack(
        [row > 0, row < n_rows - 1, seq * f_dev, shards * f_dev, lax.axis_index("c")]
    ).astype(jnp.int32)
    table = time_table(timesteps, time_weight)
    taps = call(
        conv_weight_kernel,
        jax.ShapeDtypeStruct((1024, 1024), BF16),
        [VMEM],
        bytes_accessed=2 * size,
    )(spatial_weight)
    active = call(
        conv_kernel,
        packed,
        [SMEM, SMEM, VMEM, VMEM, VMEM, VMEM, VMEM],
        flops=9 * dense,
        bytes_accessed=2 * size + 9 * ch * ch * 2,
    )(flags, clip_lengths, latents, top, bot, taps, table)
    active = exchange(active)
    cot = call(pack_kernel, packed, [VMEM], bytes_accessed=2 * size)(cotangent)

    n_packed = shards * half * PIX
    flat = jax.ShapeDtypeStruct((n_packed, 2 * ch), BF16)
    units = n_packed // PIX
    tiles = -(-ch // 128)
    columns = pltpu.VMEM((5, n_packed, 128), F32)
    whole = pltpu.VMEM(flat.shape, F32)
    around = pltpu.VMEM((shards, (half + 2) * PIX, 2 * ch), F32)
    pad = tiles * 128
    weights = [
        jax.ShapeDtypeStruct((pad, 3 * pad), BF16),
        jax.ShapeDtypeStruct((pad, pad), BF16),
        jax.ShapeDtypeStruct((3 * pad, pad), BF16),
        jax.ShapeDtypeStruct((2 * units, 2 * units), F32),
    ]
    prepared = call(prepare_kernel, weights, [SMEM] + [VMEM] * 5, bytes_accessed=4 * size)(
        clip_lengths, query_weight, key_weight, value_weight, out_weight, temporal_weight
    )
    cot, active, prepared = lax.optimization_barrier((cot, active, prepared))
    wqkv, wo, tw, bias = prepared
    mixed = call(
        attention_kernel,
        jax.ShapeDtypeStruct((shards, (half + 1) * PIX, 2 * ch), BF16),
        [VMEM] + [ANY] * 3,
        scratch=[columns, columns]
        + [pltpu.VMEM(w.shape, w.dtype) for w in (weights[0], weights[1], weights[3])]
        + [whole, pltpu.SemaphoreType.DMA((3,))],
        flops=7 * dense,
        bytes_accessed=4 * size,
    )(active.reshape(flat.shape), wqkv, wo, bias)
    mixed = lax.all_to_all(mixed, SEQ, split_axis=0, concat_axis=0, tiled=True)
    half_grad = (3 * ch // 2, ch)
    mine, other = call(
        grad_kernel,
        (jax.ShapeDtypeStruct(half_grad, F32), jax.ShapeDtypeStruct(half_grad, BF16)),
        [SMEM, SMEM, VMEM, VMEM],
        scratch=[around, pltpu.VMEM((pad, 3 * pad), F32), pltpu.VMEM((3 * ch, ch), F32)],
        flops=3 * dense,
        bytes_accessed=3 * size,
    )(flags, clip_lengths, mixed, cot.reshape(shards, half * PIX, 2 * ch))
    mixed, mine, other = lax.optimization_barrier((mixed, mine, other))
    block_out = call(
        temporal_kernel,
        jax.ShapeDtypeStruct(latents.shape, BF16),
        [SMEM, SMEM, VMEM, VMEM],
        scratch=[around],
        flops=3 * dense,
        bytes_accessed=3 * size,
    )(flags, clip_lengths, mixed, tw)
    grads = reduce_all(mine, other).reshape(3, ch, ch)
    return block_out, grads


def solution(mesh):
    n_seq, n_row = mesh.devices.shape
    grid = Mesh(mesh.devices.reshape(n_seq // 4, 2, 2, n_row), ("z", "y", "c", "x"))
    spread = P(SEQ, "x", None, None)
    in_specs = (spread,) + (P(),) * 9 + (spread,)
    return jax.shard_map(
        body, mesh=grid, in_specs=in_specs, out_specs=(spread, P()), check_vma=False
    )
```

```python
import math

import jax
import jax.numpy as jnp
from jax import lax
from jax.experimental import pallas as pl
from jax.experimental.pallas import tpu as pltpu
from jax.sharding import Mesh
from jax.sharding import PartitionSpec as P

HEADS = 8
CLIPS = 4
SEQ = ("z", "y", "c")
PLANE = ("y", "x")
BF16 = jnp.bfloat16
F32 = jnp.float32
VMEM = pltpu.VMEM
SMEM = pltpu.SMEM
ANY = pl.ANY
PIX = 8
VMEM_LIMIT = 24 * 2**20
WHOLE_VMEM = 60 * 2**20


def time_table(timesteps, time_weight):
    half_width = time_weight.shape[0] // 2
    frequency = jnp.exp(-math.log(10000.0) * jnp.arange(half_width, dtype=F32) / half_width)
    angles = timesteps.astype(F32)[:, None] * frequency[None, :]
    embedded = jnp.concatenate([jnp.cos(angles), jnp.sin(angles)], axis=1)
    return jnp.dot(embedded, time_weight.astype(F32), precision=lax.Precision.HIGHEST)


def call(
    kernel, out_shape, in_spaces, scratch=(), flops=0, bytes_accessed=0, out_space=VMEM, aliases=None, limit=VMEM_LIMIT
):
    return pl.pallas_call(
        kernel,
        out_shape=out_shape,
        in_specs=[pl.BlockSpec(memory_space=s) for s in in_spaces],
        out_specs=jax.tree.map(lambda _: pl.BlockSpec(memory_space=out_space), out_shape),
        scratch_shapes=scratch,
        input_output_aliases=aliases or {},
        cost_estimate=pl.CostEstimate(
            flops=flops, bytes_accessed=bytes_accessed, transcendentals=0
        ),
        compiler_params=pltpu.CompilerParams(vmem_limit_bytes=limit),
    )


def clip_ids(frame, len_ref):
    bound = jnp.int32(0)
    ids = jnp.zeros(frame.shape, jnp.int32)
    for k in range(CLIPS):
        bound = bound + len_ref[k]
        ids = ids + jnp.where(frame >= bound, 1, 0)
    return ids


def take(row, g, real):
    if real == PIX:
        return row[g * PIX : (g + 1) * PIX]
    piece = row[g * real : (g + 1) * real].astype(F32)
    return jnp.concatenate([piece, jnp.zeros((PIX - real, row.shape[-1]), F32)], 0).astype(BF16)


def pack_kernel(x_ref, o_ref):
    frames, rows, across, ch = x_ref.shape
    real = across * rows // o_ref.shape[0]
    wide = 256

    def step(t, _):
        flat = [
            jnp.concatenate([x_ref[2 * t + q, i] for i in range(rows)], axis=0) for q in range(2)
        ]
        for q in range(2):
            store_groups(o_ref, t, slice(q * wide, (q + 1) * wide), flat[q][:, :wide], real)
        tail = jnp.concatenate([flat[0][:, wide:], flat[1][:, wide:]], axis=1)
        store_groups(o_ref, t, slice(2 * wide, 2 * ch), tail, real)
        return 0

    lax.fori_loop(0, frames // 2, step, 0)


def conv_weight_kernel(w_ref, o_ref):
    ch = w_ref.shape[-1]
    wide = 256
    rest = ch - wide
    none = jnp.zeros((ch, rest), BF16)
    for a in range(3):
        taps = [w_ref[a, b] for b in range(3)]
        tails = [
            jnp.concatenate([taps[0][:, wide:], taps[1][:, wide:]], axis=1),
            jnp.concatenate([taps[2][:, wide:], none], axis=1),
        ]
        for src, dst, size in ((0, a * wide, wide), (wide, 3 * wide + a * rest, rest)):
            rows = pl.ds(dst, size)
            for b in range(3):
                o_ref[rows, b * wide : (b + 1) * wide] = taps[b][src : src + size, :wide]
            for k in range(2):
                o_ref[rows, 3 * wide + k * 128 : 3 * wide + (k + 1) * 128] = tails[k][
                    src : src + size
                ]
    o_ref[3 * wide + 3 * rest :, :] = jnp.zeros((rest, 4 * wide), BF16)


def store_groups(o_ref, t, lanes, value, real):
    shards = o_ref.shape[0]
    value = value.astype(BF16)
    if real == PIX:
        o_ref[:, t, :, lanes] = value.reshape(shards, PIX, value.shape[-1])
        return
    for d in range(shards):
        o_ref[d, t, :, lanes] = take(value, d, real)


def silu(v):
    return 0.5 * v * (1.0 + jnp.tanh(0.5 * v))


def conv_rows(lines, store, count, n_rows, base, steps, len_ref, w_ref, table_ref):
    wide = 256
    low = low_lanes()

    def clip_of(frame):
        bound = jnp.int32(0)
        place = jnp.int32(0)
        for k in range(CLIPS):
            bound = bound + len_ref[k]
            place = place + jnp.where(frame >= bound, 1, 0)
        return jnp.minimum(place, CLIPS - 1)

    def step(g, _):
        kept = [lines(g * count + k) for k in range(count)]
        across = kept[0][0].shape[0]
        pos = n_rows * across
        window = [
            jnp.concatenate([r for one in kept for r in one[a : a + n_rows]], axis=0)
            for a in range(3)
        ]
        tails = [w[:, wide:] for w in window]
        x = jnp.concatenate(
            [w[:, :wide] for w in window]
            + [
                jnp.concatenate([tails[0], tails[1]], axis=1),
                jnp.concatenate([tails[2], jnp.zeros_like(tails[2])], axis=1),
            ],
            axis=1,
        )
        y = jnp.dot(x, w_ref[...], preferred_element_type=F32)
        n = count * pos
        col = lax.broadcasted_iota(jnp.int32, (n, 128), 0) & (across - 1)
        first, last = col == 0, col == across - 1

        def shifted(left, right):
            return jnp.where(first, 0.0, pltpu.roll(left, 1, 0)) + jnp.where(
                last, 0.0, pltpu.roll(right, n - 1, 0)
            )

        cols = []
        for c in range(2):
            at = lambda b: y[:, b * wide + c * 128 : b * wide + (c + 1) * 128]
            cols.append(shifted(at(0), at(2)) + at(1))
        mid = y[:, 3 * wide : 3 * wide + 128]
        side = shifted(mid, y[:, 3 * wide + 128 :])
        for k in range(count // 2):
            t = g * (count // 2) + k
            even = slice(2 * k * pos, (2 * k + 1) * pos)
            odd = slice((2 * k + 1) * pos, (2 * k + 2) * pos)
            emb = [table_ref[pl.ds(clip_of(base + 2 * t + q), 1), :] for q in range(2)]
            for q, rs in enumerate((even, odd)):
                for c in range(2):
                    lanes = slice(c * 128, (c + 1) * 128)
                    v = cols[c][rs] + emb[q][:, lanes]
                    got = window[1][rs, lanes].astype(F32) + silu(v)
                    store(t, slice(q * wide + c * 128, q * wide + (c + 1) * 128), got)
            tail = jnp.where(
                low, side[even] + swap_halves(mid[even]), swap_halves(side[odd]) + mid[odd]
            )
            tail = tail + jnp.concatenate([emb[0][:, wide:], emb[1][:, wide:]], axis=1)
            res = jnp.concatenate([tails[1][even], tails[1][odd]], axis=1).astype(F32)
            store(t, slice(2 * wide, 2 * wide + 128), res + silu(tail))
        return 0

    lax.fori_loop(0, steps, step, 0)


def keep_if(condition, x):
    return jnp.where(condition, x, jnp.zeros_like(x))


def conv_kernel(flag_ref, len_ref, lat_ref, top_ref, bot_ref, w_ref, table_ref, o_ref):
    frames, rows, across, _ = lat_ref.shape
    real = across * rows // o_ref.shape[0]

    def lines(f):
        top = keep_if(flag_ref[0] > 0, top_ref[f])
        bot = keep_if(flag_ref[1] > 0, bot_ref[f])
        return [top] + [lat_ref[f, i] for i in range(rows)] + [bot]

    def store(t, lanes, value):
        store_groups(o_ref, t, lanes, value, real)

    conv_rows(lines, store, 2, rows, flag_ref[2], frames // 2, len_ref, w_ref, table_ref)


def inner_kernel(flag_ref, len_ref, lat_ref, w_ref, table_ref, o_ref):
    frames, rows, across, _ = lat_ref.shape
    groups = o_ref.shape[0] // rows
    first = flag_ref[0]

    def lines(f):
        above = keep_if(first == 1, lat_ref[f, 0])
        below = keep_if(first == 0, lat_ref[f, rows - 1])
        return [above] + [lat_ref[f, k + first] for k in range(rows - 1)] + [below]

    def store(t, lanes, value):
        dst = o_ref.at[pl.ds(first * groups, (rows - 1) * groups)]
        store_groups(dst, t, lanes, value, PIX)

    count = 6 if frames % 6 == 0 else 2
    conv_rows(
        lines, store, count, rows - 1, flag_ref[2], frames // count, len_ref, w_ref, table_ref
    )


def edge_kernel(
    flag_ref, len_ref, lat_ref, halo_ref, w_ref, table_ref, inner_hbm, o_hbm, edge, sem
):
    frames, rows, across, _ = lat_ref.shape
    groups = edge.shape[0]
    first = flag_ref[0]

    def lines(f):
        halo = halo_ref[f]
        above = jnp.where(first == 1, halo, lat_ref[f, rows - 2])
        below = jnp.where(first == 0, halo, lat_ref[f, 1])
        return [above, lat_ref[f, (1 - first) * (rows - 1)], below]

    def store(t, lanes, value):
        store_groups(edge, t, lanes, value, PIX)

    conv_rows(lines, store, frames, 1, flag_ref[2], 1, len_ref, w_ref, table_ref)
    dst = o_hbm.at[pl.ds((1 - first) * (rows - 1) * groups, groups)]
    out = pltpu.make_async_copy(edge, dst, sem)
    out.start()
    out.wait()


def low_lanes():
    return lax.broadcasted_iota(jnp.int32, (1, 128), 1) < 64


def swap_halves(tail):
    return pltpu.roll(tail, 64, 1)


def split_pair(x):
    tail = x[:, 512:640]
    even = jnp.concatenate([x[:, 0:256], tail], axis=1)
    odd = jnp.concatenate([x[:, 256:512], swap_halves(tail)], axis=1)
    return even, odd


def join_pair(even, odd):
    tail = jnp.where(low_lanes(), even[:, 256:384], swap_halves(odd[:, 256:384]))
    return even[:, 0:256], odd[:, 0:256], tail


def pad_weight(dst, src, row, col):
    ch = src.shape[-1]
    dst[pl.ds(row, dst_tile(ch)), pl.ds(col, dst_tile(ch))] = jnp.zeros(
        (dst_tile(ch), dst_tile(ch)), BF16
    )
    dst[pl.ds(row, ch), pl.ds(col, ch)] = src


def dst_tile(ch):
    return -(-ch // 128) * 128


def spread_units(m_ref, m32):
    own = m_ref.shape[1] - PIX
    for s in range(m_ref.shape[0]):
        x = m_ref[s].astype(F32)
        m32[s, PIX : PIX + own, :] = x[:own]
        m32[s, 0:PIX, :] = x[own:]
        m32[s, PIX + own :, :] = x[own:]


def sources(m32, start, count, base, frames, len_ref):
    own = m32.shape[1] - 2 * PIX

    def rows(first):
        x = m32[pl.ds(start, count), first : first + own, :]
        return split_pair(x.reshape(count * own, x.shape[-1]))

    cur, before, after = rows(PIX), rows(0)[1], rows(2 * PIX)[0]
    unit = lax.broadcasted_iota(jnp.int32, (count, own, 1), 1).reshape(count * own, 1) >> 3
    even = base + 2 * unit
    ids = [clip_ids(even + k, len_ref) for k in (-1, 0, 1, 2)]
    into = jnp.where((ids[0] == ids[1]) & (even > 0), 1.0, 0.0)
    inside = jnp.where(ids[1] == ids[2], 1.0, 0.0)
    out = jnp.where((ids[2] == ids[3]) & (even < frames - 2), 1.0, 0.0)
    stack = lambda a, b: jnp.concatenate([a, b], axis=0)
    previous = stack(before * into, cur[0] * inside)
    following = stack(cur[1] * inside, after * out)
    return previous, stack(*cur), following


def prepare_kernel(len_ref, wq_ref, wk_ref, wv_ref, wo_ref, tw_ref, wqkv, wo, tw, bias):
    pad = wo.shape[0]
    frames = bias.shape[0]
    units = frames // 2
    for j, ref in enumerate((wq_ref, wk_ref, wv_ref)):
        pad_weight(wqkv, ref[...], 0, j * pad)
    pad_weight(wo, wo_ref[...], 0, 0)
    for j in range(3):
        pad_weight(tw, tw_ref[j], j * pad, 0)
    place = lambda axis: lax.broadcasted_iota(jnp.int32, (frames, frames), axis)
    frame = lambda i: jnp.where(i < units, 2 * i, 2 * (i - units) + 1)
    same = clip_ids(frame(place(0)), len_ref) == clip_ids(frame(place(1)), len_ref)
    bias[...] = jnp.where(same, 0.0, -1e30)


def attention_kernel(
    act_ref, wqkv_hbm, wo_hbm, bias_hbm, o_ref, n5, d5, wqkv, wo, bias, m32, sems
):
    rows, ch2 = act_ref.shape
    ch = ch2 // 2
    pad = dst_tile(ch)
    units = rows // PIX
    frames = units * 2
    head = ch // HEADS
    fetches = [
        pltpu.make_async_copy(src, dst, sems.at[k])
        for k, (src, dst) in enumerate(((wqkv_hbm, wqkv), (wo_hbm, wo), (bias_hbm, bias)))
    ]
    for f in fetches:
        f.start()
    chunk = 96
    low = low_lanes()

    def norm(i, _):
        at = pl.ds(pl.multiple_of(i * chunk, 8), chunk)
        x = act_ref[at, :].astype(F32)
        cols = [x[:, c * 128 : (c + 1) * 128] for c in range(5)]

        def sums(v):
            a = v[0] + v[1] + jnp.where(low, v[4], 0.0)
            b = v[2] + v[3] + jnp.where(low, 0.0, v[4])
            return [jnp.sum(t, axis=-1, keepdims=True) * (1.0 / ch) for t in (a, b)]

        def spread_out(a, b):
            return [a, a, b, b, jnp.where(low, a, b)]

        center = [v - m for v, m in zip(cols, spread_out(*sums(cols)))]
        var = sums([v * v for v in center])
        gain = spread_out(*[lax.rsqrt(v + 1e-05) for v in var])
        for c in range(5):
            n5[c, at, :] = (center[c] * gain[c]).astype(BF16).astype(F32)
        return 0

    lax.fori_loop(0, rows // chunk, norm, 0)
    for f in fetches:
        f.wait()

    factor = head ** (-0.5) * math.log2(math.e)
    lane = lax.broadcasted_iota(jnp.int32, (1, pad), 1)
    group = 4

    def pixels(i, _):
        parts = []
        for g in range(group):
            at = pl.ds(i * group + g, units, stride=PIX)
            cols = [n5[c, at, :] for c in range(5)]
            parts.append(jnp.concatenate([cols[0], cols[1], cols[4]], axis=1))
            parts.append(jnp.concatenate([cols[2], cols[3], swap_halves(cols[4])], axis=1))
        n = jnp.concatenate(parts, axis=0).astype(BF16)
        qkv = jnp.dot(n, wqkv[...], preferred_element_type=F32).astype(BF16)
        att = []
        for g in range(group):
            q, k, v = (
                qkv[g * frames : (g + 1) * frames, j * pad : (j + 1) * pad] for j in range(3)
            )
            acc = [None, None]
            for h in range(HEADS):
                w = 0 if (h + 1) * head <= 256 else 1
                win = slice(w * 128, w * 128 + 256)
                mine = (lane >= h * head) & (lane < (h + 1) * head)
                mine = jnp.where(mine, 1.0, 0.0).astype(BF16)
                s = lax.dot_general(
                    (q * mine)[:, win],
                    k[:, win],
                    (((1,), (1,)), ((), ())),
                    preferred_element_type=F32,
                )
                s = s * factor + bias[...]
                e = jnp.exp2(s - jnp.max(s, axis=-1, keepdims=True))
                prob = (e * (1.0 / jnp.sum(e, axis=-1, keepdims=True))).astype(BF16)
                got = jnp.dot(prob, (v * mine)[:, win], preferred_element_type=F32)
                acc[w] = got if acc[w] is None else acc[w] + got
            att.append(
                jnp.concatenate(
                    [acc[0][:, :128], acc[0][:, 128:] + acc[1][:, :128], acc[1][:, 128:]], axis=1
                )
            )
        att = jnp.concatenate(att, axis=0).astype(BF16)
        delta = jnp.dot(att, wo[...], preferred_element_type=F32)
        for g in range(group):
            at = pl.ds(i * group + g, units, stride=PIX)
            base = g * frames
            even, odd = delta[base : base + units], delta[base + units : base + frames]
            d5[0, at, :] = even[:, 0:128]
            d5[1, at, :] = even[:, 128:256]
            d5[2, at, :] = odd[:, 0:128]
            d5[3, at, :] = odd[:, 128:256]
            d5[4, at, :] = even[:, 256:384] + swap_halves(odd[:, 256:384])
        return 0

    lax.fori_loop(0, PIX // group, pixels, 0)

    own = o_ref.shape[1] - PIX

    def mix(i, _):
        at = pl.ds(pl.multiple_of(i * own, 8), own)
        delta = jnp.concatenate([d5[c, at, :] for c in range(5)], axis=1)
        m = (act_ref[at, :].astype(F32) + delta).astype(BF16)
        o_ref[i, 0:own, :] = m
        m32[at, :] = m.astype(F32)
        return 0

    lax.fori_loop(0, rows // own, mix, 0)

    def edges(i, _):
        after = m32[pl.ds(pl.multiple_of(jnp.minimum((i + 1) * own, rows - PIX), 8), PIX), :]
        before = m32[pl.ds(pl.multiple_of(jnp.maximum(i * own - PIX, 0), 8), PIX), :]
        tail = jnp.where(low, after[:, 512:640], before[:, 512:640])
        edge = jnp.concatenate([after[:, 0:256], before[:, 256:512], tail], axis=1)
        o_ref[i, own : own + PIX, :] = edge.astype(BF16)
        return 0

    lax.fori_loop(0, rows // own, edges, 0)


def temporal_kernel(flag_ref, len_ref, m_ref, tw, o_ref, m32):
    shards = m_ref.shape[0]
    frames, rows, across, ch = o_ref.shape
    units = frames // 2
    groups = shards // rows
    real = across // groups
    total_frames = flag_ref[3]
    spread_units(m_ref, m32)

    def join(blocks):
        return jnp.concatenate([b[:real] for b in blocks], axis=0).astype(BF16)

    def step(i, _):
        src = sources(m32, i * groups, groups, flag_ref[2], total_frames, len_ref)
        rounded = jnp.concatenate([v.astype(BF16) for v in src], axis=1)
        total = src[1] + jnp.dot(rounded, tw[...], preferred_element_type=F32)
        total = total.reshape(2, groups, units, PIX, total.shape[-1])
        for u in range(units):
            for q in range(2):
                got = join([total[q, g, u] for g in range(groups)])
                o_ref[2 * u + q, i] = got[:, :ch]
        return 0

    lax.fori_loop(0, rows, step, 0)


def grad_kernel(flag_ref, len_ref, m_ref, cot_ref, mine_ref, other_ref, m32, grad, full):
    shards = m_ref.shape[0]
    ch = m_ref.shape[-1] // 2
    pad = dst_tile(ch)
    count = 8
    spread_units(m_ref, m32)

    def step(i, _):
        src = sources(m32, i * count, count, flag_ref[2], flag_ref[3], len_ref)
        rounded = jnp.concatenate([v.astype(BF16) for v in src], axis=1)
        cot = cot_ref[pl.ds(i * count, count), :, :].astype(F32)
        cot = split_pair(cot.reshape(-1, 2 * ch))
        cot = jnp.concatenate(cot, axis=0).astype(BF16)
        got = lax.dot_general(cot, rounded, (((0,), (0,)), ((), ())), preferred_element_type=F32)

        @pl.when(i == 0)
        def _():
            grad[...] = got

        @pl.when(i > 0)
        def _():
            grad[...] += got

        return 0

    lax.fori_loop(0, shards // count, step, 0)
    for j in range(3):
        full[j * ch : (j + 1) * ch, :] = grad[:, j * pad : (j + 1) * pad].T[:ch, :ch]
    core = flag_ref[4]
    n = mine_ref.shape[0]
    mine_ref[...] = full[pl.ds(pl.multiple_of(core * n, 8), n), :]
    other_ref[...] = full[pl.ds(pl.multiple_of((1 - core) * n, 8), n), :].astype(BF16)


def tree(parts):
    while len(parts) > 1:
        parts = [parts[i] + parts[i + 1] for i in range(0, len(parts), 2)]
    return parts[0]


def swaps(n, k):
    return [(i, i ^ k) for i in range(n)]


def ordered(parts, place):
    stacked = jnp.stack(parts)
    return jnp.concatenate(
        [lax.dynamic_index_in_dim(stacked, place ^ j, 0, False) for j in range(len(parts))], 0
    )


def finish_kernel(flag_ref, own_ref, other_ref, o_ref):
    parts, share, _ = own_ref.shape
    for k in range(parts):
        at = (flag_ref[5] ^ k) * share
        mine = at + flag_ref[4] * parts * share
        theirs = at + (1 - flag_ref[4]) * parts * share
        o_ref[pl.ds(pl.multiple_of(mine, 8), share), :] = own_ref[k].astype(F32)
        o_ref[pl.ds(pl.multiple_of(theirs, 8), share), :] = other_ref[k].astype(F32)


def reduce_all(g, other, block_out, flags):
    core = lax.axis_index("c")
    n_plane = lax.axis_size("y") * lax.axis_size("x")
    place = lax.axis_index("y") * lax.axis_size("x") + lax.axis_index("x")
    n_z = lax.axis_size("z")
    share = g.shape[0] // n_plane

    def cut(v, i, size):
        return lax.dynamic_slice_in_dim(v, i * size, size, 0)

    g = g + lax.ppermute(other, "c", swaps(2, 1)).astype(F32)
    parts = [cut(g, place, share)]
    for k in range(1, n_plane):
        sent = cut(g, place ^ k, share).astype(BF16)
        parts.append(lax.ppermute(sent, PLANE, swaps(n_plane, k)).astype(F32))
    mine = tree(parts).astype(BF16)
    mine, block_out = lax.optimization_barrier((mine, block_out))
    parts = [mine.astype(F32)]
    for k in range(1, n_z):
        parts.append(lax.ppermute(mine, "z", swaps(n_z, k)).astype(F32))
    total = tree(parts).astype(BF16)
    parts = [total] + [lax.ppermute(total, PLANE, swaps(n_plane, k)) for k in range(1, n_plane)]
    if share % 8:
        own = ordered(parts, place)
        other = lax.ppermute(own, "c", swaps(2, 1))
        low = jnp.where(core == 0, own, other)
        high = jnp.where(core == 0, other, own)
        return jnp.concatenate([low, high], 0).astype(F32), block_out
    own = jnp.stack(parts)
    other = lax.ppermute(own, "c", swaps(2, 1))
    whole = jax.ShapeDtypeStruct((2 * g.shape[0], g.shape[1]), F32)
    grads = call(finish_kernel, whole, [SMEM, VMEM, VMEM], bytes_accessed=4 * g.size)(
        flags, own, other
    )
    return grads, block_out


def exchange(x):
    shape = x.shape
    flat = x.reshape(shape[0], shape[1] * shape[2], shape[3])
    flat = lax.all_to_all(flat, SEQ, split_axis=0, concat_axis=0, tiled=True)
    return flat.reshape(shape)


def body(
    latents,
    clip_lengths,
    timesteps,
    spatial_weight,
    time_weight,
    query_weight,
    key_weight,
    value_weight,
    out_weight,
    temporal_weight,
    cotangent,
):
    f_dev, rows, across, ch = latents.shape
    shards = lax.axis_size("z") * lax.axis_size("y") * lax.axis_size("c")
    n_rows = lax.axis_size("x")
    assert rows * across <= shards * PIX and shards % rows == 0 and f_dev % 2 == 0
    half = f_dev // 2
    packed = jax.ShapeDtypeStruct((shards, half, PIX, 2 * ch), BF16)
    positions = f_dev * rows * across
    size = positions * ch * 2
    dense = 2 * positions * ch * ch

    row = lax.axis_index("x")
    if n_rows == 2:
        edge = lax.dynamic_index_in_dim(latents, (1 - row) * (rows - 1), 1, False)
        got = lax.ppermute(edge, "x", swaps(2, 1))
        top, bot = got, got
    else:
        up = [(i, i + 1) for i in range(n_rows - 1)]
        top = lax.ppermute(latents[:, rows - 1], "x", up)
        bot = lax.ppermute(latents[:, 0], "x", [(j, i) for i, j in up])
    seq = (lax.axis_index("z") * lax.axis_size("y") + lax.axis_index("y")) * 2 + lax.axis_index("c")
    place = lax.axis_index("y") * n_rows + row
    core = lax.axis_index("c")
    flags = jnp.stack(
        [row > 0, row < n_rows - 1, seq * f_dev, shards * f_dev, core, place]
    ).astype(jnp.int32)
    table = time_table(timesteps, time_weight)
    taps = call(
        conv_weight_kernel,
        jax.ShapeDtypeStruct((1024, 1024), BF16),
        [VMEM],
        bytes_accessed=2 * size,
    )(spatial_weight)
    work = dict(flops=9 * dense, bytes_accessed=2 * size + 9 * ch * ch * 2)
    if n_rows == 2 and rows * across == shards * PIX and rows > 2:
        inner = call(inner_kernel, packed, [SMEM, SMEM] + [VMEM] * 3, **work)(
            flags, clip_lengths, latents, taps, table
        )
        active = call(
            edge_kernel,
            packed,
            [SMEM, SMEM] + [VMEM] * 4 + [ANY],
            scratch=[
                pltpu.VMEM((shards // rows, half, PIX, 2 * ch), BF16),
                pltpu.SemaphoreType.DMA(()),
            ],
            out_space=ANY,
            aliases={6: 0},
            **work,
        )(flags, clip_lengths, latents, top, taps, table, inner)
    else:
        active = call(conv_kernel, packed, [SMEM, SMEM] + [VMEM] * 5, **work)(
            flags, clip_lengths, latents, top, bot, taps, table
        )
    active = exchange(active)
    cot = call(pack_kernel, packed, [VMEM], bytes_accessed=2 * size)(cotangent)

    n_packed = shards * half * PIX
    flat = jax.ShapeDtypeStruct((n_packed, 2 * ch), BF16)
    units = n_packed // PIX
    tiles = -(-ch // 128)
    columns = pltpu.VMEM((5, n_packed, 128), F32)
    whole = pltpu.VMEM(flat.shape, F32)
    around = pltpu.VMEM((shards, (half + 2) * PIX, 2 * ch), F32)
    pad = tiles * 128
    weights = [
        jax.ShapeDtypeStruct((pad, 3 * pad), BF16),
        jax.ShapeDtypeStruct((pad, pad), BF16),
        jax.ShapeDtypeStruct((3 * pad, pad), BF16),
        jax.ShapeDtypeStruct((2 * units, 2 * units), F32),
    ]
    prepared = call(prepare_kernel, weights, [SMEM] + [VMEM] * 5, bytes_accessed=4 * size)(
        clip_lengths, query_weight, key_weight, value_weight, out_weight, temporal_weight
    )
    cot, active, prepared = lax.optimization_barrier((cot, active, prepared))
    wqkv, wo, tw, bias = prepared
    mixed = call(
        attention_kernel,
        jax.ShapeDtypeStruct((shards, (half + 1) * PIX, 2 * ch), BF16),
        [VMEM] + [ANY] * 3,
        scratch=[columns, columns]
        + [pltpu.VMEM(w.shape, w.dtype) for w in (weights[0], weights[1], weights[3])]
        + [whole, pltpu.SemaphoreType.DMA((3,))],
        flops=7 * dense,
        bytes_accessed=4 * size,
        limit=WHOLE_VMEM,
    )(active.reshape(flat.shape), wqkv, wo, bias)
    mixed = lax.all_to_all(mixed, SEQ, split_axis=0, concat_axis=0, tiled=True)
    half_grad = (3 * ch // 2, ch)
    mine, other = call(
        grad_kernel,
        (jax.ShapeDtypeStruct(half_grad, F32), jax.ShapeDtypeStruct(half_grad, BF16)),
        [SMEM, SMEM, VMEM, VMEM],
        scratch=[around, pltpu.VMEM((pad, 3 * pad), F32), pltpu.VMEM((3 * ch, ch), F32)],
        flops=3 * dense,
        bytes_accessed=3 * size,
    )(flags, clip_lengths, mixed, cot.reshape(shards, half * PIX, 2 * ch))
    mixed, mine, other = lax.optimization_barrier((mixed, mine, other))
    block_out = call(
        temporal_kernel,
        jax.ShapeDtypeStruct(latents.shape, BF16),
        [SMEM, SMEM, VMEM, VMEM],
        scratch=[around],
        flops=3 * dense,
        bytes_accessed=3 * size,
    )(flags, clip_lengths, mixed, tw)
    grads, block_out = reduce_all(mine, other, block_out, flags)
    return block_out, grads.reshape(3, ch, ch)


def solution(mesh):
    n_seq, n_row = mesh.devices.shape
    grid = Mesh(mesh.devices.reshape(n_seq // 4, 2, 2, n_row), ("z", "y", "c", "x"))
    spread = P(SEQ, "x", None, None)
    in_specs = (spread,) + (P(),) * 9 + (spread,)
    return jax.shard_map(
        body, mesh=grid, in_specs=in_specs, out_specs=(spread, P()), check_vma=False
    )
```

```python
import math

import jax
import jax.numpy as jnp
from jax import lax
from jax.experimental import pallas as pl
from jax.experimental.pallas import tpu as pltpu
from jax.sharding import Mesh
from jax.sharding import PartitionSpec as P

HEADS = 8
CLIPS = 4
SEQ = ("z", "y", "c")
PLANE = ("y", "x")
BF16 = jnp.bfloat16
F32 = jnp.float32
VMEM = pltpu.VMEM
SMEM = pltpu.SMEM
ANY = pl.ANY
PIX = 8
VMEM_LIMIT = 24 * 2**20
WHOLE_VMEM = 60 * 2**20


def angles_of(timesteps, half_width):
    frequency = jnp.exp(-math.log(10000.0) * jnp.arange(half_width, dtype=F32) / half_width)
    angles = timesteps.astype(F32)[:, None] * frequency[None, :]
    return jnp.cos(angles), jnp.sin(angles)


def call(
    kernel, out_shape, in_spaces, scratch=(), flops=0, bytes_accessed=0, out_space=VMEM, aliases=None, limit=VMEM_LIMIT
):
    return pl.pallas_call(
        kernel,
        out_shape=out_shape,
        in_specs=[pl.BlockSpec(memory_space=s) for s in in_spaces],
        out_specs=jax.tree.map(lambda _: pl.BlockSpec(memory_space=out_space), out_shape),
        scratch_shapes=scratch,
        input_output_aliases=aliases or {},
        cost_estimate=pl.CostEstimate(
            flops=flops, bytes_accessed=bytes_accessed, transcendentals=0
        ),
        compiler_params=pltpu.CompilerParams(vmem_limit_bytes=limit),
    )


def clip_ids(frame, len_ref):
    bound = jnp.int32(0)
    ids = jnp.zeros(frame.shape, jnp.int32)
    for k in range(CLIPS):
        bound = bound + len_ref[k]
        ids = ids + jnp.where(frame >= bound, 1, 0)
    return ids


def take(row, g, real):
    if real == PIX:
        return row[g * PIX : (g + 1) * PIX]
    piece = row[g * real : (g + 1) * real].astype(F32)
    return jnp.concatenate([piece, jnp.zeros((PIX - real, row.shape[-1]), F32)], 0).astype(BF16)


def pack_kernel(x_ref, o_ref):
    frames, rows, across, ch = x_ref.shape
    real = across * rows // o_ref.shape[0]
    wide = 256

    def step(t, _):
        flat = [
            jnp.concatenate([x_ref[2 * t + q, i] for i in range(rows)], axis=0) for q in range(2)
        ]
        for q in range(2):
            store_groups(o_ref, t, slice(q * wide, (q + 1) * wide), flat[q][:, :wide], real)
        tail = jnp.concatenate([flat[0][:, wide:], flat[1][:, wide:]], axis=1)
        store_groups(o_ref, t, slice(2 * wide, 2 * ch), tail, real)
        return 0

    lax.fori_loop(0, frames // 2, step, 0)


def exact_product(x, w):
    total = 0.0
    for _ in range(3):
        part = x.astype(BF16)
        total = total + jnp.dot(part, w, preferred_element_type=F32)
        x = x - part.astype(F32)
    return total


def conv_weight_kernel(w_ref, cos_ref, sin_ref, time_ref, o_ref, table_ref):
    half_width = cos_ref.shape[1]
    table_ref[...] = exact_product(cos_ref[...], time_ref[:half_width]) + exact_product(
        sin_ref[...], time_ref[half_width:]
    )
    ch = w_ref.shape[-1]
    wide = 256
    rest = ch - wide
    none = jnp.zeros((ch, rest), BF16)
    for a in range(3):
        taps = [w_ref[a, b] for b in range(3)]
        tails = [
            jnp.concatenate([taps[0][:, wide:], taps[1][:, wide:]], axis=1),
            jnp.concatenate([taps[2][:, wide:], none], axis=1),
        ]
        for src, dst, size in ((0, a * wide, wide), (wide, 3 * wide + a * rest, rest)):
            rows = pl.ds(dst, size)
            for b in range(3):
                o_ref[rows, b * wide : (b + 1) * wide] = taps[b][src : src + size, :wide]
            for k in range(2):
                o_ref[rows, 3 * wide + k * 128 : 3 * wide + (k + 1) * 128] = tails[k][
                    src : src + size
                ]
    o_ref[3 * wide + 3 * rest :, :] = jnp.zeros((rest, 4 * wide), BF16)


def store_groups(o_ref, t, lanes, value, real):
    shards = o_ref.shape[0]
    value = value.astype(BF16)
    if real == PIX:
        o_ref[:, t, :, lanes] = value.reshape(shards, PIX, value.shape[-1])
        return
    for d in range(shards):
        o_ref[d, t, :, lanes] = take(value, d, real)


def silu(v):
    return 0.5 * v * (1.0 + jnp.tanh(0.5 * v))


def conv_rows(lines, store, count, n_rows, base, steps, len_ref, w_ref, table_ref):
    wide = 256
    low = low_lanes()

    def clip_of(frame):
        bound = jnp.int32(0)
        place = jnp.int32(0)
        for k in range(CLIPS):
            bound = bound + len_ref[k]
            place = place + jnp.where(frame >= bound, 1, 0)
        return jnp.minimum(place, CLIPS - 1)

    def step(g, _):
        kept = [lines(g * count + k) for k in range(count)]
        across = kept[0][0].shape[0]
        pos = n_rows * across
        window = [
            jnp.concatenate([r for one in kept for r in one[a : a + n_rows]], axis=0)
            for a in range(3)
        ]
        tails = [w[:, wide:] for w in window]
        x = jnp.concatenate(
            [w[:, :wide] for w in window]
            + [
                jnp.concatenate([tails[0], tails[1]], axis=1),
                jnp.concatenate([tails[2], jnp.zeros_like(tails[2])], axis=1),
            ],
            axis=1,
        )
        y = jnp.dot(x, w_ref[...], preferred_element_type=F32)
        n = count * pos
        col = lax.broadcasted_iota(jnp.int32, (n, 128), 0) & (across - 1)
        first, last = col == 0, col == across - 1

        def shifted(left, right):
            return jnp.where(first, 0.0, pltpu.roll(left, 1, 0)) + jnp.where(
                last, 0.0, pltpu.roll(right, n - 1, 0)
            )

        cols = []
        for c in range(2):
            at = lambda b: y[:, b * wide + c * 128 : b * wide + (c + 1) * 128]
            cols.append(shifted(at(0), at(2)) + at(1))
        mid = y[:, 3 * wide : 3 * wide + 128]
        side = shifted(mid, y[:, 3 * wide + 128 :])
        for k in range(count // 2):
            t = g * (count // 2) + k
            even = slice(2 * k * pos, (2 * k + 1) * pos)
            odd = slice((2 * k + 1) * pos, (2 * k + 2) * pos)
            emb = [table_ref[pl.ds(clip_of(base + 2 * t + q), 1), :] for q in range(2)]
            for q, rs in enumerate((even, odd)):
                for c in range(2):
                    lanes = slice(c * 128, (c + 1) * 128)
                    v = cols[c][rs] + emb[q][:, lanes]
                    got = window[1][rs, lanes].astype(F32) + silu(v)
                    store(t, slice(q * wide + c * 128, q * wide + (c + 1) * 128), got)
            tail = jnp.where(
                low, side[even] + swap_halves(mid[even]), swap_halves(side[odd]) + mid[odd]
            )
            tail = tail + jnp.concatenate([emb[0][:, wide:], emb[1][:, wide:]], axis=1)
            res = jnp.concatenate([tails[1][even], tails[1][odd]], axis=1).astype(F32)
            store(t, slice(2 * wide, 2 * wide + 128), res + silu(tail))
        return 0

    lax.fori_loop(0, steps, step, 0)


def keep_if(condition, x):
    return jnp.where(condition, x, jnp.zeros_like(x))


def conv_kernel(flag_ref, len_ref, lat_ref, top_ref, bot_ref, w_ref, table_ref, o_ref):
    frames, rows, across, _ = lat_ref.shape
    real = across * rows // o_ref.shape[0]

    def lines(f):
        top = keep_if(flag_ref[0] > 0, top_ref[f])
        bot = keep_if(flag_ref[1] > 0, bot_ref[f])
        return [top] + [lat_ref[f, i] for i in range(rows)] + [bot]

    def store(t, lanes, value):
        store_groups(o_ref, t, lanes, value, real)

    conv_rows(lines, store, 2, rows, flag_ref[2], frames // 2, len_ref, w_ref, table_ref)


def inner_kernel(flag_ref, len_ref, lat_ref, w_ref, table_ref, o_ref):
    frames, rows, across, _ = lat_ref.shape
    groups = o_ref.shape[0] // rows
    first = flag_ref[0]

    def lines(f):
        above = keep_if(first == 1, lat_ref[f, 0])
        below = keep_if(first == 0, lat_ref[f, rows - 1])
        return [above] + [lat_ref[f, k + first] for k in range(rows - 1)] + [below]

    def store(t, lanes, value):
        dst = o_ref.at[pl.ds(first * groups, (rows - 1) * groups)]
        store_groups(dst, t, lanes, value, PIX)

    count = 6 if frames % 6 == 0 else 2
    conv_rows(
        lines, store, count, rows - 1, flag_ref[2], frames // count, len_ref, w_ref, table_ref
    )


def edge_kernel(
    flag_ref, len_ref, lat_ref, halo_ref, w_ref, table_ref, inner_hbm, o_hbm, edge, sem
):
    frames, rows, across, _ = lat_ref.shape
    groups = edge.shape[0]
    first = flag_ref[0]

    def lines(f):
        halo = halo_ref[f]
        above = jnp.where(first == 1, halo, lat_ref[f, rows - 2])
        below = jnp.where(first == 0, halo, lat_ref[f, 1])
        return [above, lat_ref[f, (1 - first) * (rows - 1)], below]

    def store(t, lanes, value):
        store_groups(edge, t, lanes, value, PIX)

    conv_rows(lines, store, frames, 1, flag_ref[2], 1, len_ref, w_ref, table_ref)
    dst = o_hbm.at[pl.ds((1 - first) * (rows - 1) * groups, groups)]
    out = pltpu.make_async_copy(edge, dst, sem)
    out.start()
    out.wait()


def low_lanes():
    return lax.broadcasted_iota(jnp.int32, (1, 128), 1) < 64


def swap_halves(tail):
    return pltpu.roll(tail, 64, 1)


def split_pair(x):
    tail = x[:, 512:640]
    even = jnp.concatenate([x[:, 0:256], tail], axis=1)
    odd = jnp.concatenate([x[:, 256:512], swap_halves(tail)], axis=1)
    return even, odd


def join_pair(even, odd):
    tail = jnp.where(low_lanes(), even[:, 256:384], swap_halves(odd[:, 256:384]))
    return even[:, 0:256], odd[:, 0:256], tail


def pad_weight(dst, src, row, col):
    ch = src.shape[-1]
    dst[pl.ds(row, dst_tile(ch)), pl.ds(col, dst_tile(ch))] = jnp.zeros(
        (dst_tile(ch), dst_tile(ch)), BF16
    )
    dst[pl.ds(row, ch), pl.ds(col, ch)] = src


def dst_tile(ch):
    return -(-ch // 128) * 128


def sources(m_ref, start, count, base, frames, len_ref):
    own = m_ref.shape[1] - PIX
    x = m_ref[pl.ds(start, count)].astype(F32)

    def pair(v):
        return split_pair(v.reshape(count * own, v.shape[-1]))

    cur = pair(x[:, :own])
    before = pair(jnp.concatenate([x[:, own:], x[:, : own - PIX]], axis=1))[1]
    after = pair(x[:, PIX:])[0]
    unit = lax.broadcasted_iota(jnp.int32, (count, own, 1), 1).reshape(count * own, 1) >> 3
    even = base + 2 * unit
    ids = [clip_ids(even + k, len_ref) for k in (-1, 0, 1, 2)]
    into = jnp.where((ids[0] == ids[1]) & (even > 0), 1.0, 0.0)
    inside = jnp.where(ids[1] == ids[2], 1.0, 0.0)
    out = jnp.where((ids[2] == ids[3]) & (even < frames - 2), 1.0, 0.0)
    stack = lambda a, b: jnp.concatenate([a, b], axis=0)
    previous = stack(before * into, cur[0] * inside)
    following = stack(cur[1] * inside, after * out)
    return previous, stack(*cur), following


def prepare_kernel(len_ref, wq_ref, wk_ref, wv_ref, wo_ref, tw_ref, wqkv, wo, tw, bias):
    pad = wo.shape[0]
    frames = bias.shape[0]
    units = frames // 2
    for j, ref in enumerate((wq_ref, wk_ref, wv_ref)):
        pad_weight(wqkv, ref[...], 0, j * pad)
    pad_weight(wo, wo_ref[...], 0, 0)
    for j in range(3):
        pad_weight(tw, tw_ref[j], j * pad, 0)
    place = lambda axis: lax.broadcasted_iota(jnp.int32, (frames, frames), axis)
    frame = lambda i: jnp.where(i < units, 2 * i, 2 * (i - units) + 1)
    same = clip_ids(frame(place(0)), len_ref) == clip_ids(frame(place(1)), len_ref)
    bias[...] = jnp.where(same, 0.0, -1e30)


def attention_kernel(
    act_hbm, wqkv_hbm, wo_hbm, bias_hbm, o_hbm,
    n5, d5, wqkv, wo, bias, m32, act_ref, o_ref, sems, in_sems, out_sems
):
    rows, ch2 = act_ref.shape
    ch = ch2 // 2
    pad = dst_tile(ch)
    units = rows // PIX
    frames = units * 2
    head = ch // HEADS
    chunk = 96

    def arriving(i):
        at = pl.ds(pl.multiple_of(i * chunk, 8), chunk)
        return pltpu.make_async_copy(act_hbm.at[at], act_ref.at[at], in_sems.at[i])

    for i in range(rows // chunk):
        arriving(i).start()
    fetches = [
        pltpu.make_async_copy(src, dst, sems.at[k])
        for k, (src, dst) in enumerate(((wqkv_hbm, wqkv), (wo_hbm, wo), (bias_hbm, bias)))
    ]
    for f in fetches:
        f.start()
    low = low_lanes()

    def norm(i, _):
        arriving(i).wait()
        at = pl.ds(pl.multiple_of(i * chunk, 8), chunk)
        x = act_ref[at, :].astype(F32)
        cols = [x[:, c * 128 : (c + 1) * 128] for c in range(5)]

        def sums(v):
            a = v[0] + v[1] + jnp.where(low, v[4], 0.0)
            b = v[2] + v[3] + jnp.where(low, 0.0, v[4])
            return [jnp.sum(t, axis=-1, keepdims=True) * (1.0 / ch) for t in (a, b)]

        def spread_out(a, b):
            return [a, a, b, b, jnp.where(low, a, b)]

        center = [v - m for v, m in zip(cols, spread_out(*sums(cols)))]
        var = sums([v * v for v in center])
        gain = spread_out(*[lax.rsqrt(v + 1e-05) for v in var])
        for c in range(5):
            n5[c, at, :] = (center[c] * gain[c]).astype(BF16).astype(F32)
        return 0

    lax.fori_loop(0, rows // chunk, norm, 0)
    for f in fetches:
        f.wait()

    factor = head ** (-0.5) * math.log2(math.e)
    lane = lax.broadcasted_iota(jnp.int32, (1, pad), 1)
    group = 4

    def pixels(i, _):
        parts = []
        for g in range(group):
            at = pl.ds(i * group + g, units, stride=PIX)
            cols = [n5[c, at, :] for c in range(5)]
            parts.append(jnp.concatenate([cols[0], cols[1], cols[4]], axis=1))
            parts.append(jnp.concatenate([cols[2], cols[3], swap_halves(cols[4])], axis=1))
        n = jnp.concatenate(parts, axis=0).astype(BF16)
        qkv = jnp.dot(n, wqkv[...], preferred_element_type=F32).astype(BF16)
        att = []
        for g in range(group):
            q, k, v = (
                qkv[g * frames : (g + 1) * frames, j * pad : (j + 1) * pad] for j in range(3)
            )
            acc = [None, None]
            for h in range(HEADS):
                w = 0 if (h + 1) * head <= 256 else 1
                win = slice(w * 128, w * 128 + 256)
                mine = (lane >= h * head) & (lane < (h + 1) * head)
                mine = jnp.where(mine, 1.0, 0.0).astype(BF16)
                s = lax.dot_general(
                    (q * mine)[:, win],
                    k[:, win],
                    (((1,), (1,)), ((), ())),
                    preferred_element_type=F32,
                )
                s = s * factor + bias[...]
                e = jnp.exp2(s - jnp.max(s, axis=-1, keepdims=True))
                prob = (e * (1.0 / jnp.sum(e, axis=-1, keepdims=True))).astype(BF16)
                got = jnp.dot(prob, (v * mine)[:, win], preferred_element_type=F32)
                acc[w] = got if acc[w] is None else acc[w] + got
            att.append(
                jnp.concatenate(
                    [acc[0][:, :128], acc[0][:, 128:] + acc[1][:, :128], acc[1][:, 128:]], axis=1
                )
            )
        att = jnp.concatenate(att, axis=0).astype(BF16)
        delta = jnp.dot(att, wo[...], preferred_element_type=F32)
        for g in range(group):
            at = pl.ds(i * group + g, units, stride=PIX)
            base = g * frames
            even, odd = delta[base : base + units], delta[base + units : base + frames]
            d5[0, at, :] = even[:, 0:128]
            d5[1, at, :] = even[:, 128:256]
            d5[2, at, :] = odd[:, 0:128]
            d5[3, at, :] = odd[:, 128:256]
            d5[4, at, :] = even[:, 256:384] + swap_halves(odd[:, 256:384])
        return 0

    lax.fori_loop(0, PIX // group, pixels, 0)

    own = o_ref.shape[1] - PIX

    def leaving(i):
        at = (i, pl.ds(0, own))
        return pltpu.make_async_copy(o_ref.at[at], o_hbm.at[at], out_sems.at[i])

    def mix(i, _):
        at = pl.ds(pl.multiple_of(i * own, 8), own)
        delta = jnp.concatenate([d5[c, at, :] for c in range(5)], axis=1)
        m = (act_ref[at, :].astype(F32) + delta).astype(BF16)
        o_ref[i, 0:own, :] = m
        m32[at, :] = m.astype(F32)
        leaving(i).start()
        return 0

    lax.fori_loop(0, rows // own, mix, 0)

    def edges(i, _):
        after = m32[pl.ds(pl.multiple_of(jnp.minimum((i + 1) * own, rows - PIX), 8), PIX), :]
        before = m32[pl.ds(pl.multiple_of(jnp.maximum(i * own - PIX, 0), 8), PIX), :]
        tail = jnp.where(low, after[:, 512:640], before[:, 512:640])
        edge = jnp.concatenate([after[:, 0:256], before[:, 256:512], tail], axis=1)
        o_ref[i, own : own + PIX, :] = edge.astype(BF16)
        return 0

    lax.fori_loop(0, rows // own, edges, 0)
    at = (slice(None), pl.ds(own, PIX))
    last = pltpu.make_async_copy(o_ref.at[at], o_hbm.at[at], sems.at[3])
    last.start()
    for i in range(rows // own):
        leaving(i).wait()
    last.wait()


def temporal_kernel(flag_ref, len_ref, m_ref, tw, o_ref):
    shards = m_ref.shape[0]
    frames, rows, across, ch = o_ref.shape
    units = frames // 2
    groups = shards // rows
    real = across // groups
    total_frames = flag_ref[3]

    def join(blocks):
        return jnp.concatenate([b[:real] for b in blocks], axis=0).astype(BF16)

    def step(i, _):
        src = sources(m_ref, i * groups, groups, flag_ref[2], total_frames, len_ref)
        rounded = jnp.concatenate([v.astype(BF16) for v in src], axis=1)
        total = src[1] + jnp.dot(rounded, tw[...], preferred_element_type=F32)
        total = total.reshape(2, groups, units, PIX, total.shape[-1])
        for u in range(units):
            for q in range(2):
                got = join([total[q, g, u] for g in range(groups)])
                o_ref[2 * u + q, i] = got[:, :ch]
        return 0

    lax.fori_loop(0, rows, step, 0)


def grad_kernel(flag_ref, len_ref, m_ref, cot_ref, mine_ref, other_ref, grad, full):
    shards = m_ref.shape[0]
    ch = m_ref.shape[-1] // 2
    pad = dst_tile(ch)
    count = 8

    def step(i, _):
        src = sources(m_ref, i * count, count, flag_ref[2], flag_ref[3], len_ref)
        rounded = jnp.concatenate([v.astype(BF16) for v in src], axis=1)
        cot = cot_ref[pl.ds(i * count, count), :, :].astype(F32)
        cot = split_pair(cot.reshape(-1, 2 * ch))
        cot = jnp.concatenate(cot, axis=0).astype(BF16)
        got = lax.dot_general(cot, rounded, (((0,), (0,)), ((), ())), preferred_element_type=F32)

        @pl.when(i == 0)
        def _():
            grad[...] = got

        @pl.when(i > 0)
        def _():
            grad[...] += got

        return 0

    lax.fori_loop(0, shards // count, step, 0)
    for j in range(3):
        full[j * ch : (j + 1) * ch, :] = grad[:, j * pad : (j + 1) * pad].T[:ch, :ch]
    core = flag_ref[4]
    n = mine_ref.shape[0]
    mine_ref[...] = full[pl.ds(pl.multiple_of(core * n, 8), n), :]
    other_ref[...] = full[pl.ds(pl.multiple_of((1 - core) * n, 8), n), :].astype(BF16)


def tree(parts):
    while len(parts) > 1:
        parts = [parts[i] + parts[i + 1] for i in range(0, len(parts), 2)]
    return parts[0]


def swaps(n, k):
    return [(i, i ^ k) for i in range(n)]


def ordered(parts, place):
    stacked = jnp.stack(parts)
    return jnp.concatenate(
        [lax.dynamic_index_in_dim(stacked, place ^ j, 0, False) for j in range(len(parts))], 0
    )


def shares_kernel(flag_ref, g_ref, got_ref, *refs):
    outs, total = refs[:-1], refs[-1]
    total[...] = g_ref[...] + got_ref[...].astype(F32)
    for k, o_ref in enumerate(outs):
        share = o_ref.shape[0]
        at = pl.ds(pl.multiple_of((flag_ref[5] ^ k) * share, 8), share)
        o_ref[...] = total[at, :].astype(o_ref.dtype)


def finish_kernel(flag_ref, own_ref, other_ref, o_ref):
    parts, share, _ = own_ref.shape
    for k in range(parts):
        at = (flag_ref[5] ^ k) * share
        mine = at + flag_ref[4] * parts * share
        theirs = at + (1 - flag_ref[4]) * parts * share
        o_ref[pl.ds(pl.multiple_of(mine, 8), share), :] = own_ref[k].astype(F32)
        o_ref[pl.ds(pl.multiple_of(theirs, 8), share), :] = other_ref[k].astype(F32)


def reduce_all(g, other, block_out, flags):
    core = lax.axis_index("c")
    n_plane = lax.axis_size("y") * lax.axis_size("x")
    place = lax.axis_index("y") * lax.axis_size("x") + lax.axis_index("x")
    n_z = lax.axis_size("z")
    share = g.shape[0] // n_plane

    def cut(v, i, size):
        return lax.dynamic_slice_in_dim(v, i * size, size, 0)

    got = lax.ppermute(other, "c", swaps(2, 1))
    if share % 8:
        g = g + got.astype(F32)
        cuts = [cut(g, place, share)]
        cuts += [cut(g, place ^ k, share).astype(BF16) for k in range(1, n_plane)]
    else:
        kinds = [jax.ShapeDtypeStruct((share, g.shape[1]), F32 if k == 0 else BF16) for k in range(n_plane)]
        cuts = call(
            shares_kernel,
            kinds,
            [SMEM, VMEM, VMEM],
            scratch=[pltpu.VMEM(g.shape, F32)],
            bytes_accessed=10 * g.size,
        )(flags, g, got)
    parts = [cuts[0]]
    for sent in cuts[1:]:
        k = len(parts)
        parts.append(lax.ppermute(sent, PLANE, swaps(n_plane, k)).astype(F32))
    mine = tree(parts).astype(BF16)
    mine, block_out = lax.optimization_barrier((mine, block_out))
    parts = [mine.astype(F32)]
    for k in range(1, n_z):
        parts.append(lax.ppermute(mine, "z", swaps(n_z, k)).astype(F32))
    total = tree(parts).astype(BF16)
    parts = [total] + [lax.ppermute(total, PLANE, swaps(n_plane, k)) for k in range(1, n_plane)]
    if share % 8:
        own = ordered(parts, place)
        other = lax.ppermute(own, "c", swaps(2, 1))
        low = jnp.where(core == 0, own, other)
        high = jnp.where(core == 0, other, own)
        return jnp.concatenate([low, high], 0).astype(F32), block_out
    own = jnp.stack(parts)
    other = lax.ppermute(own, "c", swaps(2, 1))
    whole = jax.ShapeDtypeStruct((2 * g.shape[0], g.shape[1]), F32)
    grads = call(finish_kernel, whole, [SMEM, VMEM, VMEM], bytes_accessed=4 * g.size)(
        flags, own, other
    )
    return grads, block_out


def exchange(x):
    shape = x.shape
    flat = x.reshape(shape[0], shape[1] * shape[2], shape[3])
    flat = lax.all_to_all(flat, SEQ, split_axis=0, concat_axis=0, tiled=True)
    return flat.reshape(shape)


def body(
    latents,
    clip_lengths,
    timesteps,
    spatial_weight,
    time_weight,
    query_weight,
    key_weight,
    value_weight,
    out_weight,
    temporal_weight,
    cotangent,
):
    f_dev, rows, across, ch = latents.shape
    shards = lax.axis_size("z") * lax.axis_size("y") * lax.axis_size("c")
    n_rows = lax.axis_size("x")
    assert rows * across <= shards * PIX and shards % rows == 0 and f_dev % 2 == 0
    half = f_dev // 2
    packed = jax.ShapeDtypeStruct((shards, half, PIX, 2 * ch), BF16)
    positions = f_dev * rows * across
    size = positions * ch * 2
    dense = 2 * positions * ch * ch

    row = lax.axis_index("x")
    if n_rows == 2:
        edge = lax.dynamic_index_in_dim(latents, (1 - row) * (rows - 1), 1, False)
        got = lax.ppermute(edge, "x", swaps(2, 1))
        top, bot = got, got
    else:
        up = [(i, i + 1) for i in range(n_rows - 1)]
        top = lax.ppermute(latents[:, rows - 1], "x", up)
        bot = lax.ppermute(latents[:, 0], "x", [(j, i) for i, j in up])
    seq = (lax.axis_index("z") * lax.axis_size("y") + lax.axis_index("y")) * 2 + lax.axis_index("c")
    place = lax.axis_index("y") * n_rows + row
    core = lax.axis_index("c")
    flags = jnp.stack(
        [row > 0, row < n_rows - 1, seq * f_dev, shards * f_dev, core, place]
    ).astype(jnp.int32)
    taps, table = call(
        conv_weight_kernel,
        (jax.ShapeDtypeStruct((1024, 1024), BF16), jax.ShapeDtypeStruct((CLIPS, ch), F32)),
        [VMEM] * 4,
        bytes_accessed=2 * size,
    )(spatial_weight, *angles_of(timesteps, ch // 2), time_weight)
    work = dict(flops=9 * dense, bytes_accessed=2 * size + 9 * ch * ch * 2)
    if n_rows == 2 and rows * across == shards * PIX and rows > 2:
        inner = call(inner_kernel, packed, [SMEM, SMEM] + [VMEM] * 3, **work)(
            flags, clip_lengths, latents, taps, table
        )
        active = call(
            edge_kernel,
            packed,
            [SMEM, SMEM] + [VMEM] * 4 + [ANY],
            scratch=[
                pltpu.VMEM((shards // rows, half, PIX, 2 * ch), BF16),
                pltpu.SemaphoreType.DMA(()),
            ],
            out_space=ANY,
            aliases={6: 0},
            **work,
        )(flags, clip_lengths, latents, top, taps, table, inner)
    else:
        active = call(conv_kernel, packed, [SMEM, SMEM] + [VMEM] * 5, **work)(
            flags, clip_lengths, latents, top, bot, taps, table
        )
    active = exchange(active)
    cot = call(pack_kernel, packed, [VMEM], bytes_accessed=2 * size)(cotangent)

    n_packed = shards * half * PIX
    flat = jax.ShapeDtypeStruct((n_packed, 2 * ch), BF16)
    units = n_packed // PIX
    tiles = -(-ch // 128)
    columns = pltpu.VMEM((5, n_packed, 128), F32)
    whole = pltpu.VMEM(flat.shape, F32)
    pad = tiles * 128
    weights = [
        jax.ShapeDtypeStruct((pad, 3 * pad), BF16),
        jax.ShapeDtypeStruct((pad, pad), BF16),
        jax.ShapeDtypeStruct((3 * pad, pad), BF16),
        jax.ShapeDtypeStruct((2 * units, 2 * units), F32),
    ]
    prepared = call(prepare_kernel, weights, [SMEM] + [VMEM] * 5, bytes_accessed=4 * size)(
        clip_lengths, query_weight, key_weight, value_weight, out_weight, temporal_weight
    )
    cot, active, prepared = lax.optimization_barrier((cot, active, prepared))
    wqkv, wo, tw, bias = prepared
    mixed = call(
        attention_kernel,
        jax.ShapeDtypeStruct((shards, (half + 1) * PIX, 2 * ch), BF16),
        [ANY] * 4,
        scratch=[columns, columns]
        + [pltpu.VMEM(w.shape, w.dtype) for w in (weights[0], weights[1], weights[3])]
        + [
            whole,
            pltpu.VMEM(flat.shape, BF16),
            pltpu.VMEM((shards, (half + 1) * PIX, 2 * ch), BF16),
            pltpu.SemaphoreType.DMA((4,)),
            pltpu.SemaphoreType.DMA((n_packed // 96,)),
            pltpu.SemaphoreType.DMA((shards,)),
        ],
        out_space=ANY,
        flops=7 * dense,
        bytes_accessed=4 * size,
        limit=WHOLE_VMEM,
    )(active.reshape(flat.shape), wqkv, wo, bias)
    mixed = lax.all_to_all(mixed, SEQ, split_axis=0, concat_axis=0, tiled=True)
    half_grad = (3 * ch // 2, ch)
    mine, other = call(
        grad_kernel,
        (jax.ShapeDtypeStruct(half_grad, F32), jax.ShapeDtypeStruct(half_grad, BF16)),
        [SMEM, SMEM, VMEM, VMEM],
        scratch=[pltpu.VMEM((pad, 3 * pad), F32), pltpu.VMEM((3 * ch, ch), F32)],
        flops=3 * dense,
        bytes_accessed=3 * size,
    )(flags, clip_lengths, mixed, cot.reshape(shards, half * PIX, 2 * ch))
    mixed, mine, other = lax.optimization_barrier((mixed, mine, other))
    block_out = call(
        temporal_kernel,
        jax.ShapeDtypeStruct(latents.shape, BF16),
        [SMEM, SMEM, VMEM, VMEM],
        flops=3 * dense,
        bytes_accessed=3 * size,
    )(flags, clip_lengths, mixed, tw)
    grads, block_out = reduce_all(mine, other, block_out, flags)
    return block_out, grads.reshape(3, ch, ch)


def solution(mesh):
    n_seq, n_row = mesh.devices.shape
    grid = Mesh(mesh.devices.reshape(n_seq // 4, 2, 2, n_row), ("z", "y", "c", "x"))
    spread = P(SEQ, "x", None, None)
    in_specs = (spread,) + (P(),) * 9 + (spread,)
    return jax.shard_map(
        body, mesh=grid, in_specs=in_specs, out_specs=(spread, P()), check_vma=False
    )
```

```python
import math

import jax
import jax.numpy as jnp
from jax import lax
from jax.experimental import pallas as pl
from jax.experimental.pallas import tpu as pltpu
from jax.sharding import Mesh
from jax.sharding import PartitionSpec as P

HEADS = 8
CLIPS = 4
SEQ = ("z", "y", "c")
PLANE = ("y", "x")
BF16 = jnp.bfloat16
F32 = jnp.float32
VMEM = pltpu.VMEM
SMEM = pltpu.SMEM
ANY = pl.ANY
PIX = 8
VMEM_LIMIT = 24 * 2**20
WHOLE_VMEM = 60 * 2**20


def time_table(timesteps, time_weight):
    half_width = time_weight.shape[0] // 2
    frequency = jnp.exp(-math.log(10000.0) * jnp.arange(half_width, dtype=F32) / half_width)
    angles = timesteps.astype(F32)[:, None] * frequency[None, :]
    embedded = jnp.concatenate([jnp.cos(angles), jnp.sin(angles)], axis=1)
    return jnp.dot(embedded, time_weight.astype(F32), precision=lax.Precision.HIGHEST)


def call(
    kernel, out_shape, in_spaces, scratch=(), flops=0, bytes_accessed=0, out_space=VMEM, aliases=None, limit=VMEM_LIMIT
):
    return pl.pallas_call(
        kernel,
        out_shape=out_shape,
        in_specs=[pl.BlockSpec(memory_space=s) for s in in_spaces],
        out_specs=jax.tree.map(lambda _: pl.BlockSpec(memory_space=out_space), out_shape),
        scratch_shapes=scratch,
        input_output_aliases=aliases or {},
        cost_estimate=pl.CostEstimate(
            flops=flops, bytes_accessed=bytes_accessed, transcendentals=0
        ),
        compiler_params=pltpu.CompilerParams(vmem_limit_bytes=limit),
    )


def clip_ids(frame, len_ref):
    bound = jnp.int32(0)
    ids = jnp.zeros(frame.shape, jnp.int32)
    for k in range(CLIPS):
        bound = bound + len_ref[k]
        ids = ids + jnp.where(frame >= bound, 1, 0)
    return ids


def take(row, g, real):
    if real == PIX:
        return row[g * PIX : (g + 1) * PIX]
    piece = row[g * real : (g + 1) * real].astype(F32)
    return jnp.concatenate([piece, jnp.zeros((PIX - real, row.shape[-1]), F32)], 0).astype(BF16)


def pack_kernel(x_ref, o_ref):
    frames, rows, across, ch = x_ref.shape
    real = across * rows // o_ref.shape[0]
    wide = 256

    def step(t, _):
        flat = [
            jnp.concatenate([x_ref[2 * t + q, i] for i in range(rows)], axis=0) for q in range(2)
        ]
        for q in range(2):
            store_groups(o_ref, t, slice(q * wide, (q + 1) * wide), flat[q][:, :wide], real)
        tail = jnp.concatenate([flat[0][:, wide:], flat[1][:, wide:]], axis=1)
        store_groups(o_ref, t, slice(2 * wide, 2 * ch), tail, real)
        return 0

    lax.fori_loop(0, frames // 2, step, 0)


def conv_weight_kernel(w_ref, o_ref):
    ch = w_ref.shape[-1]
    wide = 256
    rest = ch - wide
    none = jnp.zeros((ch, rest), BF16)
    for a in range(3):
        taps = [w_ref[a, b] for b in range(3)]
        tails = [
            jnp.concatenate([taps[0][:, wide:], taps[1][:, wide:]], axis=1),
            jnp.concatenate([taps[2][:, wide:], none], axis=1),
        ]
        for src, dst, size in ((0, a * wide, wide), (wide, 3 * wide + a * rest, rest)):
            rows = pl.ds(dst, size)
            for b in range(3):
                o_ref[rows, b * wide : (b + 1) * wide] = taps[b][src : src + size, :wide]
            for k in range(2):
                o_ref[rows, 3 * wide + k * 128 : 3 * wide + (k + 1) * 128] = tails[k][
                    src : src + size
                ]
    o_ref[3 * wide + 3 * rest :, :] = jnp.zeros((rest, 4 * wide), BF16)


def store_groups(o_ref, t, lanes, value, real):
    shards = o_ref.shape[0]
    value = value.astype(BF16)
    if real == PIX:
        o_ref[:, t, :, lanes] = value.reshape(shards, PIX, value.shape[-1])
        return
    for d in range(shards):
        o_ref[d, t, :, lanes] = take(value, d, real)


def silu(v):
    return 0.5 * v * (1.0 + jnp.tanh(0.5 * v))


def conv_rows(lines, store, count, n_rows, base, steps, len_ref, w_ref, table_ref):
    wide = 256
    low = low_lanes()

    def clip_of(frame):
        bound = jnp.int32(0)
        place = jnp.int32(0)
        for k in range(CLIPS):
            bound = bound + len_ref[k]
            place = place + jnp.where(frame >= bound, 1, 0)
        return jnp.minimum(place, CLIPS - 1)

    def step(g, _):
        kept = [lines(g * count + k) for k in range(count)]
        across = kept[0][0].shape[0]
        pos = n_rows * across
        window = [
            jnp.concatenate([r for one in kept for r in one[a : a + n_rows]], axis=0)
            for a in range(3)
        ]
        tails = [w[:, wide:] for w in window]
        x = jnp.concatenate(
            [w[:, :wide] for w in window]
            + [
                jnp.concatenate([tails[0], tails[1]], axis=1),
                jnp.concatenate([tails[2], jnp.zeros_like(tails[2])], axis=1),
            ],
            axis=1,
        )
        y = jnp.dot(x, w_ref[...], preferred_element_type=F32)
        n = count * pos
        col = lax.broadcasted_iota(jnp.int32, (n, 128), 0) & (across - 1)
        first, last = col == 0, col == across - 1

        def shifted(left, right):
            return jnp.where(first, 0.0, pltpu.roll(left, 1, 0)) + jnp.where(
                last, 0.0, pltpu.roll(right, n - 1, 0)
            )

        cols = []
        for c in range(2):
            at = lambda b: y[:, b * wide + c * 128 : b * wide + (c + 1) * 128]
            cols.append(shifted(at(0), at(2)) + at(1))
        mid = y[:, 3 * wide : 3 * wide + 128]
        side = shifted(mid, y[:, 3 * wide + 128 :])
        for k in range(count // 2):
            t = g * (count // 2) + k
            even = slice(2 * k * pos, (2 * k + 1) * pos)
            odd = slice((2 * k + 1) * pos, (2 * k + 2) * pos)
            emb = [table_ref[pl.ds(clip_of(base + 2 * t + q), 1), :] for q in range(2)]
            for q, rs in enumerate((even, odd)):
                for c in range(2):
                    lanes = slice(c * 128, (c + 1) * 128)
                    v = cols[c][rs] + emb[q][:, lanes]
                    got = window[1][rs, lanes].astype(F32) + silu(v)
                    store(t, slice(q * wide + c * 128, q * wide + (c + 1) * 128), got)
            tail = jnp.where(
                low, side[even] + swap_halves(mid[even]), swap_halves(side[odd]) + mid[odd]
            )
            tail = tail + jnp.concatenate([emb[0][:, wide:], emb[1][:, wide:]], axis=1)
            res = jnp.concatenate([tails[1][even], tails[1][odd]], axis=1).astype(F32)
            store(t, slice(2 * wide, 2 * wide + 128), res + silu(tail))
        return 0

    lax.fori_loop(0, steps, step, 0)


def keep_if(condition, x):
    return jnp.where(condition, x, jnp.zeros_like(x))


def conv_kernel(flag_ref, len_ref, lat_ref, top_ref, bot_ref, w_ref, table_ref, o_ref):
    frames, rows, across, _ = lat_ref.shape
    real = across * rows // o_ref.shape[0]

    def lines(f):
        top = keep_if(flag_ref[0] > 0, top_ref[f])
        bot = keep_if(flag_ref[1] > 0, bot_ref[f])
        return [top] + [lat_ref[f, i] for i in range(rows)] + [bot]

    def store(t, lanes, value):
        store_groups(o_ref, t, lanes, value, real)

    conv_rows(lines, store, 2, rows, flag_ref[2], frames // 2, len_ref, w_ref, table_ref)


def inner_kernel(flag_ref, len_ref, lat_ref, w_ref, table_ref, o_ref):
    frames, rows, across, _ = lat_ref.shape
    groups = o_ref.shape[0] // rows
    first = flag_ref[0]

    def lines(f):
        above = keep_if(first == 1, lat_ref[f, 0])
        below = keep_if(first == 0, lat_ref[f, rows - 1])
        return [above] + [lat_ref[f, k + first] for k in range(rows - 1)] + [below]

    def store(t, lanes, value):
        dst = o_ref.at[pl.ds(first * groups, (rows - 1) * groups)]
        store_groups(dst, t, lanes, value, PIX)

    count = 6 if frames % 6 == 0 else 2
    conv_rows(
        lines, store, count, rows - 1, flag_ref[2], frames // count, len_ref, w_ref, table_ref
    )


def edge_kernel(
    flag_ref, len_ref, lat_ref, halo_ref, w_ref, table_ref, inner_hbm, o_hbm, edge, sem
):
    frames, rows, across, _ = lat_ref.shape
    groups = edge.shape[0]
    first = flag_ref[0]

    def lines(f):
        halo = halo_ref[f]
        above = jnp.where(first == 1, halo, lat_ref[f, rows - 2])
        below = jnp.where(first == 0, halo, lat_ref[f, 1])
        return [above, lat_ref[f, (1 - first) * (rows - 1)], below]

    def store(t, lanes, value):
        store_groups(edge, t, lanes, value, PIX)

    conv_rows(lines, store, frames, 1, flag_ref[2], 1, len_ref, w_ref, table_ref)
    dst = o_hbm.at[pl.ds((1 - first) * (rows - 1) * groups, groups)]
    out = pltpu.make_async_copy(edge, dst, sem)
    out.start()
    out.wait()


def low_lanes():
    return lax.broadcasted_iota(jnp.int32, (1, 128), 1) < 64


def swap_halves(tail):
    return pltpu.roll(tail, 64, 1)


def split_pair(x):
    tail = x[:, 512:640]
    even = jnp.concatenate([x[:, 0:256], tail], axis=1)
    odd = jnp.concatenate([x[:, 256:512], swap_halves(tail)], axis=1)
    return even, odd


def join_pair(even, odd):
    tail = jnp.where(low_lanes(), even[:, 256:384], swap_halves(odd[:, 256:384]))
    return even[:, 0:256], odd[:, 0:256], tail


def pad_weight(dst, src, row, col):
    ch = src.shape[-1]
    dst[pl.ds(row, dst_tile(ch)), pl.ds(col, dst_tile(ch))] = jnp.zeros(
        (dst_tile(ch), dst_tile(ch)), BF16
    )
    dst[pl.ds(row, ch), pl.ds(col, ch)] = src


def dst_tile(ch):
    return -(-ch // 128) * 128


def sources(m_ref, start, count, base, frames, len_ref):
    own = m_ref.shape[1] - PIX
    x = m_ref[pl.ds(start, count)].astype(F32)

    def pair(v):
        return split_pair(v.reshape(count * own, v.shape[-1]))

    cur = pair(x[:, :own])
    before = pair(jnp.concatenate([x[:, own:], x[:, : own - PIX]], axis=1))[1]
    after = pair(x[:, PIX:])[0]
    unit = lax.broadcasted_iota(jnp.int32, (count, own, 1), 1).reshape(count * own, 1) >> 3
    even = base + 2 * unit
    ids = [clip_ids(even + k, len_ref) for k in (-1, 0, 1, 2)]
    into = jnp.where((ids[0] == ids[1]) & (even > 0), 1.0, 0.0)
    inside = jnp.where(ids[1] == ids[2], 1.0, 0.0)
    out = jnp.where((ids[2] == ids[3]) & (even < frames - 2), 1.0, 0.0)
    stack = lambda a, b: jnp.concatenate([a, b], axis=0)
    previous = stack(before * into, cur[0] * inside)
    following = stack(cur[1] * inside, after * out)
    return previous, stack(*cur), following


def prepare_kernel(len_ref, wq_ref, wk_ref, wv_ref, wo_ref, tw_ref, wqkv, wo, tw, bias):
    pad = wo.shape[0]
    frames = bias.shape[0]
    units = frames // 2
    for j, ref in enumerate((wq_ref, wk_ref, wv_ref)):
        pad_weight(wqkv, ref[...], 0, j * pad)
    pad_weight(wo, wo_ref[...], 0, 0)
    for j in range(3):
        pad_weight(tw, tw_ref[j], j * pad, 0)
    place = lambda axis: lax.broadcasted_iota(jnp.int32, (frames, frames), axis)
    frame = lambda i: jnp.where(i < units, 2 * i, 2 * (i - units) + 1)
    same = clip_ids(frame(place(0)), len_ref) == clip_ids(frame(place(1)), len_ref)
    bias[...] = jnp.where(same, 0.0, -1e30)


def attention_kernel(
    act_hbm, wqkv_hbm, wo_hbm, bias_hbm, o_hbm,
    n5, d5, wqkv, wo, bias, m32, act_ref, o_ref, sems, in_sems, out_sems
):
    rows, ch2 = act_ref.shape
    ch = ch2 // 2
    pad = dst_tile(ch)
    units = rows // PIX
    frames = units * 2
    head = ch // HEADS
    chunk = 96

    def arriving(i):
        at = pl.ds(pl.multiple_of(i * chunk, 8), chunk)
        return pltpu.make_async_copy(act_hbm.at[at], act_ref.at[at], in_sems.at[i])

    for i in range(rows // chunk):
        arriving(i).start()
    fetches = [
        pltpu.make_async_copy(src, dst, sems.at[k])
        for k, (src, dst) in enumerate(((wqkv_hbm, wqkv), (wo_hbm, wo), (bias_hbm, bias)))
    ]
    for f in fetches:
        f.start()
    low = low_lanes()

    def norm(i, _):
        arriving(i).wait()
        at = pl.ds(pl.multiple_of(i * chunk, 8), chunk)
        x = act_ref[at, :].astype(F32)
        cols = [x[:, c * 128 : (c + 1) * 128] for c in range(5)]

        def sums(v):
            a = v[0] + v[1] + jnp.where(low, v[4], 0.0)
            b = v[2] + v[3] + jnp.where(low, 0.0, v[4])
            return [jnp.sum(t, axis=-1, keepdims=True) * (1.0 / ch) for t in (a, b)]

        def spread_out(a, b):
            return [a, a, b, b, jnp.where(low, a, b)]

        center = [v - m for v, m in zip(cols, spread_out(*sums(cols)))]
        var = sums([v * v for v in center])
        gain = spread_out(*[lax.rsqrt(v + 1e-05) for v in var])
        for c in range(5):
            n5[c, at, :] = (center[c] * gain[c]).astype(BF16).astype(F32)
        return 0

    lax.fori_loop(0, rows // chunk, norm, 0)
    for f in fetches:
        f.wait()

    factor = head ** (-0.5) * math.log2(math.e)
    lane = lax.broadcasted_iota(jnp.int32, (1, pad), 1)
    group = 4

    def pixels(i, _):
        parts = []
        for g in range(group):
            at = pl.ds(i * group + g, units, stride=PIX)
            cols = [n5[c, at, :] for c in range(5)]
            parts.append(jnp.concatenate([cols[0], cols[1], cols[4]], axis=1))
            parts.append(jnp.concatenate([cols[2], cols[3], swap_halves(cols[4])], axis=1))
        n = jnp.concatenate(parts, axis=0).astype(BF16)
        qkv = jnp.dot(n, wqkv[...], preferred_element_type=F32).astype(BF16)
        att = []
        for g in range(group):
            q, k, v = (
                qkv[g * frames : (g + 1) * frames, j * pad : (j + 1) * pad] for j in range(3)
            )
            acc = [None, None]
            for h in range(HEADS):
                w = 0 if (h + 1) * head <= 256 else 1
                win = slice(w * 128, w * 128 + 256)
                mine = (lane >= h * head) & (lane < (h + 1) * head)
                mine = jnp.where(mine, 1.0, 0.0).astype(BF16)
                s = lax.dot_general(
                    (q * mine)[:, win],
                    k[:, win],
                    (((1,), (1,)), ((), ())),
                    preferred_element_type=F32,
                )
                s = s * factor + bias[...]
                e = jnp.exp2(s - jnp.max(s, axis=-1, keepdims=True))
                prob = (e * (1.0 / jnp.sum(e, axis=-1, keepdims=True))).astype(BF16)
                got = jnp.dot(prob, (v * mine)[:, win], preferred_element_type=F32)
                acc[w] = got if acc[w] is None else acc[w] + got
            att.append(
                jnp.concatenate(
                    [acc[0][:, :128], acc[0][:, 128:] + acc[1][:, :128], acc[1][:, 128:]], axis=1
                )
            )
        att = jnp.concatenate(att, axis=0).astype(BF16)
        delta = jnp.dot(att, wo[...], preferred_element_type=F32)
        for g in range(group):
            at = pl.ds(i * group + g, units, stride=PIX)
            base = g * frames
            even, odd = delta[base : base + units], delta[base + units : base + frames]
            d5[0, at, :] = even[:, 0:128]
            d5[1, at, :] = even[:, 128:256]
            d5[2, at, :] = odd[:, 0:128]
            d5[3, at, :] = odd[:, 128:256]
            d5[4, at, :] = even[:, 256:384] + swap_halves(odd[:, 256:384])
        return 0

    lax.fori_loop(0, PIX // group, pixels, 0)

    own = o_ref.shape[1] - PIX

    def leaving(i):
        at = (i, pl.ds(0, own))
        return pltpu.make_async_copy(o_ref.at[at], o_hbm.at[at], out_sems.at[i])

    def mix(i, _):
        at = pl.ds(pl.multiple_of(i * own, 8), own)
        delta = jnp.concatenate([d5[c, at, :] for c in range(5)], axis=1)
        m = (act_ref[at, :].astype(F32) + delta).astype(BF16)
        o_ref[i, 0:own, :] = m
        m32[at, :] = m.astype(F32)
        leaving(i).start()
        return 0

    lax.fori_loop(0, rows // own, mix, 0)

    def edges(i, _):
        after = m32[pl.ds(pl.multiple_of(jnp.minimum((i + 1) * own, rows - PIX), 8), PIX), :]
        before = m32[pl.ds(pl.multiple_of(jnp.maximum(i * own - PIX, 0), 8), PIX), :]
        tail = jnp.where(low, after[:, 512:640], before[:, 512:640])
        edge = jnp.concatenate([after[:, 0:256], before[:, 256:512], tail], axis=1)
        o_ref[i, own : own + PIX, :] = edge.astype(BF16)
        return 0

    lax.fori_loop(0, rows // own, edges, 0)
    at = (slice(None), pl.ds(own, PIX))
    last = pltpu.make_async_copy(o_ref.at[at], o_hbm.at[at], sems.at[3])
    last.start()
    for i in range(rows // own):
        leaving(i).wait()
    last.wait()


def temporal_kernel(flag_ref, len_ref, m_ref, tw, o_ref):
    shards = m_ref.shape[0]
    frames, rows, across, ch = o_ref.shape
    units = frames // 2
    groups = shards // rows
    real = across // groups
    total_frames = flag_ref[3]

    def join(blocks):
        return jnp.concatenate([b[:real] for b in blocks], axis=0).astype(BF16)

    def step(i, _):
        src = sources(m_ref, i * groups, groups, flag_ref[2], total_frames, len_ref)
        rounded = jnp.concatenate([v.astype(BF16) for v in src], axis=1)
        total = src[1] + jnp.dot(rounded, tw[...], preferred_element_type=F32)
        total = total.reshape(2, groups, units, PIX, total.shape[-1])
        for u in range(units):
            for q in range(2):
                got = join([total[q, g, u] for g in range(groups)])
                o_ref[2 * u + q, i] = got[:, :ch]
        return 0

    lax.fori_loop(0, rows, step, 0)


def grad_kernel(flag_ref, len_ref, m_ref, cot_ref, mine_ref, other_ref, grad, full):
    shards = m_ref.shape[0]
    ch = m_ref.shape[-1] // 2
    pad = dst_tile(ch)
    count = 8

    def step(i, _):
        src = sources(m_ref, i * count, count, flag_ref[2], flag_ref[3], len_ref)
        rounded = jnp.concatenate([v.astype(BF16) for v in src], axis=1)
        cot = cot_ref[pl.ds(i * count, count), :, :].astype(F32)
        cot = split_pair(cot.reshape(-1, 2 * ch))
        cot = jnp.concatenate(cot, axis=0).astype(BF16)
        got = lax.dot_general(cot, rounded, (((0,), (0,)), ((), ())), preferred_element_type=F32)

        @pl.when(i == 0)
        def _():
            grad[...] = got

        @pl.when(i > 0)
        def _():
            grad[...] += got

        return 0

    lax.fori_loop(0, shards // count, step, 0)
    for j in range(3):
        full[j * ch : (j + 1) * ch, :] = grad[:, j * pad : (j + 1) * pad].T[:ch, :ch]
    core = flag_ref[4]
    n = mine_ref.shape[0]
    mine_ref[...] = full[pl.ds(pl.multiple_of(core * n, 8), n), :]
    other_ref[...] = full[pl.ds(pl.multiple_of((1 - core) * n, 8), n), :].astype(BF16)


def tree(parts):
    while len(parts) > 1:
        parts = [parts[i] + parts[i + 1] for i in range(0, len(parts), 2)]
    return parts[0]


def swaps(n, k):
    return [(i, i ^ k) for i in range(n)]


def ordered(parts, place):
    stacked = jnp.stack(parts)
    return jnp.concatenate(
        [lax.dynamic_index_in_dim(stacked, place ^ j, 0, False) for j in range(len(parts))], 0
    )


def shares_kernel(flag_ref, g_ref, got_ref, *refs):
    outs, total = refs[:-1], refs[-1]
    total[...] = g_ref[...] + got_ref[...].astype(F32)
    for k, o_ref in enumerate(outs):
        share = o_ref.shape[0]
        at = pl.ds(pl.multiple_of((flag_ref[5] ^ k) * share, 8), share)
        o_ref[...] = total[at, :].astype(o_ref.dtype)


def finish_kernel(flag_ref, own_ref, other_ref, o_ref):
    parts, share, _ = own_ref.shape
    for k in range(parts):
        at = (flag_ref[5] ^ k) * share
        mine = at + flag_ref[4] * parts * share
        theirs = at + (1 - flag_ref[4]) * parts * share
        o_ref[pl.ds(pl.multiple_of(mine, 8), share), :] = own_ref[k].astype(F32)
        o_ref[pl.ds(pl.multiple_of(theirs, 8), share), :] = other_ref[k].astype(F32)


def reduce_all(g, other, block_out, flags):
    core = lax.axis_index("c")
    n_plane = lax.axis_size("y") * lax.axis_size("x")
    place = lax.axis_index("y") * lax.axis_size("x") + lax.axis_index("x")
    n_z = lax.axis_size("z")
    share = g.shape[0] // n_plane

    def cut(v, i, size):
        return lax.dynamic_slice_in_dim(v, i * size, size, 0)

    got = lax.ppermute(other, "c", swaps(2, 1))
    if share % 8:
        g = g + got.astype(F32)
        cuts = [cut(g, place, share)]
        cuts += [cut(g, place ^ k, share).astype(BF16) for k in range(1, n_plane)]
    else:
        kinds = [jax.ShapeDtypeStruct((share, g.shape[1]), F32 if k == 0 else BF16) for k in range(n_plane)]
        cuts = call(
            shares_kernel,
            kinds,
            [SMEM, VMEM, VMEM],
            scratch=[pltpu.VMEM(g.shape, F32)],
            bytes_accessed=10 * g.size,
        )(flags, g, got)
    parts = [cuts[0]]
    for sent in cuts[1:]:
        k = len(parts)
        parts.append(lax.ppermute(sent, PLANE, swaps(n_plane, k)).astype(F32))
    mine = tree(parts).astype(BF16)
    mine, block_out = lax.optimization_barrier((mine, block_out))
    parts = [mine.astype(F32)]
    for k in range(1, n_z):
        parts.append(lax.ppermute(mine, "z", swaps(n_z, k)).astype(F32))
    total = tree(parts).astype(BF16)
    parts = [total] + [lax.ppermute(total, PLANE, swaps(n_plane, k)) for k in range(1, n_plane)]
    if share % 8:
        own = ordered(parts, place)
        other = lax.ppermute(own, "c", swaps(2, 1))
        low = jnp.where(core == 0, own, other)
        high = jnp.where(core == 0, other, own)
        return jnp.concatenate([low, high], 0).astype(F32), block_out
    own = jnp.stack(parts)
    other = lax.ppermute(own, "c", swaps(2, 1))
    whole = jax.ShapeDtypeStruct((2 * g.shape[0], g.shape[1]), F32)
    grads = call(finish_kernel, whole, [SMEM, VMEM, VMEM], bytes_accessed=4 * g.size)(
        flags, own, other
    )
    return grads, block_out


def exchange(x):
    shape = x.shape
    flat = x.reshape(shape[0], shape[1] * shape[2], shape[3])
    flat = lax.all_to_all(flat, SEQ, split_axis=0, concat_axis=0, tiled=True)
    return flat.reshape(shape)


def body(
    latents,
    clip_lengths,
    timesteps,
    spatial_weight,
    time_weight,
    query_weight,
    key_weight,
    value_weight,
    out_weight,
    temporal_weight,
    cotangent,
):
    f_dev, rows, across, ch = latents.shape
    shards = lax.axis_size("z") * lax.axis_size("y") * lax.axis_size("c")
    n_rows = lax.axis_size("x")
    assert rows * across <= shards * PIX and shards % rows == 0 and f_dev % 2 == 0
    half = f_dev // 2
    packed = jax.ShapeDtypeStruct((shards, half, PIX, 2 * ch), BF16)
    positions = f_dev * rows * across
    size = positions * ch * 2
    dense = 2 * positions * ch * ch

    row = lax.axis_index("x")
    taps = call(
        conv_weight_kernel,
        jax.ShapeDtypeStruct((1024, 1024), BF16),
        [VMEM],
        bytes_accessed=2 * size,
    )(spatial_weight)
    if n_rows == 2:
        edge = lax.dynamic_index_in_dim(latents, (1 - row) * (rows - 1), 1, False)
        edge, taps = lax.optimization_barrier((edge, taps))
        got = lax.ppermute(edge, "x", swaps(2, 1))
        top, bot = got, got
    else:
        up = [(i, i + 1) for i in range(n_rows - 1)]
        top = lax.ppermute(latents[:, rows - 1], "x", up)
        bot = lax.ppermute(latents[:, 0], "x", [(j, i) for i, j in up])
    seq = (lax.axis_index("z") * lax.axis_size("y") + lax.axis_index("y")) * 2 + lax.axis_index("c")
    place = lax.axis_index("y") * n_rows + row
    core = lax.axis_index("c")
    flags = jnp.stack(
        [row > 0, row < n_rows - 1, seq * f_dev, shards * f_dev, core, place]
    ).astype(jnp.int32)
    table = time_table(timesteps, time_weight)
    work = dict(flops=9 * dense, bytes_accessed=2 * size + 9 * ch * ch * 2)
    if n_rows == 2 and rows * across == shards * PIX and rows > 2:
        inner = call(inner_kernel, packed, [SMEM, SMEM] + [VMEM] * 3, **work)(
            flags, clip_lengths, latents, taps, table
        )
        active = call(
            edge_kernel,
            packed,
            [SMEM, SMEM] + [VMEM] * 4 + [ANY],
            scratch=[
                pltpu.VMEM((shards // rows, half, PIX, 2 * ch), BF16),
                pltpu.SemaphoreType.DMA(()),
            ],
            out_space=ANY,
            aliases={6: 0},
            **work,
        )(flags, clip_lengths, latents, top, taps, table, inner)
    else:
        active = call(conv_kernel, packed, [SMEM, SMEM] + [VMEM] * 5, **work)(
            flags, clip_lengths, latents, top, bot, taps, table
        )
    active = exchange(active)
    cot = call(pack_kernel, packed, [VMEM], bytes_accessed=2 * size)(cotangent)

    n_packed = shards * half * PIX
    flat = jax.ShapeDtypeStruct((n_packed, 2 * ch), BF16)
    units = n_packed // PIX
    tiles = -(-ch // 128)
    columns = pltpu.VMEM((5, n_packed, 128), F32)
    whole = pltpu.VMEM(flat.shape, F32)
    pad = tiles * 128
    weights = [
        jax.ShapeDtypeStruct((pad, 3 * pad), BF16),
        jax.ShapeDtypeStruct((pad, pad), BF16),
        jax.ShapeDtypeStruct((3 * pad, pad), BF16),
        jax.ShapeDtypeStruct((2 * units, 2 * units), F32),
    ]
    prepared = call(prepare_kernel, weights, [SMEM] + [VMEM] * 5, bytes_accessed=4 * size)(
        clip_lengths, query_weight, key_weight, value_weight, out_weight, temporal_weight
    )
    cot, active, prepared = lax.optimization_barrier((cot, active, prepared))
    wqkv, wo, tw, bias = prepared
    mixed = call(
        attention_kernel,
        jax.ShapeDtypeStruct((shards, (half + 1) * PIX, 2 * ch), BF16),
        [ANY] * 4,
        scratch=[columns, columns]
        + [pltpu.VMEM(w.shape, w.dtype) for w in (weights[0], weights[1], weights[3])]
        + [
            whole,
            pltpu.VMEM(flat.shape, BF16),
            pltpu.VMEM((shards, (half + 1) * PIX, 2 * ch), BF16),
            pltpu.SemaphoreType.DMA((4,)),
            pltpu.SemaphoreType.DMA((n_packed // 96,)),
            pltpu.SemaphoreType.DMA((shards,)),
        ],
        out_space=ANY,
        flops=7 * dense,
        bytes_accessed=4 * size,
        limit=WHOLE_VMEM,
    )(active.reshape(flat.shape), wqkv, wo, bias)
    mixed = lax.all_to_all(mixed, SEQ, split_axis=0, concat_axis=0, tiled=True)
    half_grad = (3 * ch // 2, ch)
    mine, other = call(
        grad_kernel,
        (jax.ShapeDtypeStruct(half_grad, F32), jax.ShapeDtypeStruct(half_grad, BF16)),
        [SMEM, SMEM, VMEM, VMEM],
        scratch=[pltpu.VMEM((pad, 3 * pad), F32), pltpu.VMEM((3 * ch, ch), F32)],
        flops=3 * dense,
        bytes_accessed=3 * size,
    )(flags, clip_lengths, mixed, cot.reshape(shards, half * PIX, 2 * ch))
    mixed, mine, other = lax.optimization_barrier((mixed, mine, other))
    block_out = call(
        temporal_kernel,
        jax.ShapeDtypeStruct(latents.shape, BF16),
        [SMEM, SMEM, VMEM, VMEM],
        flops=3 * dense,
        bytes_accessed=3 * size,
    )(flags, clip_lengths, mixed, tw)
    grads, block_out = reduce_all(mine, other, block_out, flags)
    return block_out, grads.reshape(3, ch, ch)


def solution(mesh):
    n_seq, n_row = mesh.devices.shape
    grid = Mesh(mesh.devices.reshape(n_seq // 4, 2, 2, n_row), ("z", "y", "c", "x"))
    spread = P(SEQ, "x", None, None)
    in_specs = (spread,) + (P(),) * 9 + (spread,)
    return jax.shard_map(
        body, mesh=grid, in_specs=in_specs, out_specs=(spread, P()), check_vma=False
    )
```

```python
import math

import jax
import jax.numpy as jnp
from jax import lax
from jax.experimental import pallas as pl
from jax.experimental.pallas import tpu as pltpu
from jax.sharding import Mesh
from jax.sharding import PartitionSpec as P

HEADS = 8
CLIPS = 4
SEQ = ("z", "y", "c")
PLANE = ("y", "x")
BF16 = jnp.bfloat16
F32 = jnp.float32
VMEM = pltpu.VMEM
SMEM = pltpu.SMEM
ANY = pl.ANY
PIX = 8
VMEM_LIMIT = 24 * 2**20
WHOLE_VMEM = 60 * 2**20


def time_table(timesteps, time_weight):
    half_width = time_weight.shape[0] // 2
    frequency = jnp.exp(-math.log(10000.0) * jnp.arange(half_width, dtype=F32) / half_width)
    angles = timesteps.astype(F32)[:, None] * frequency[None, :]
    embedded = jnp.concatenate([jnp.cos(angles), jnp.sin(angles)], axis=1)
    return jnp.dot(embedded, time_weight.astype(F32), precision=lax.Precision.HIGHEST)


def call(
    kernel, out_shape, in_spaces, scratch=(), flops=0, bytes_accessed=0, out_space=VMEM, aliases=None, limit=VMEM_LIMIT
):
    return pl.pallas_call(
        kernel,
        out_shape=out_shape,
        in_specs=[pl.BlockSpec(memory_space=s) for s in in_spaces],
        out_specs=jax.tree.map(lambda _: pl.BlockSpec(memory_space=out_space), out_shape),
        scratch_shapes=scratch,
        input_output_aliases=aliases or {},
        cost_estimate=pl.CostEstimate(
            flops=flops, bytes_accessed=bytes_accessed, transcendentals=0
        ),
        compiler_params=pltpu.CompilerParams(vmem_limit_bytes=limit),
    )


def clip_ids(frame, len_ref):
    bound = jnp.int32(0)
    ids = jnp.zeros(frame.shape, jnp.int32)
    for k in range(CLIPS):
        bound = bound + len_ref[k]
        ids = ids + jnp.where(frame >= bound, 1, 0)
    return ids


def take(row, g, real):
    if real == PIX:
        return row[g * PIX : (g + 1) * PIX]
    piece = row[g * real : (g + 1) * real].astype(F32)
    return jnp.concatenate([piece, jnp.zeros((PIX - real, row.shape[-1]), F32)], 0).astype(BF16)


def pack_kernel(x_ref, o_ref):
    frames, rows, across, ch = x_ref.shape
    real = across * rows // o_ref.shape[0]
    wide = 256

    def step(t, _):
        flat = [
            jnp.concatenate([x_ref[2 * t + q, i] for i in range(rows)], axis=0) for q in range(2)
        ]
        for q in range(2):
            store_groups(o_ref, t, slice(q * wide, (q + 1) * wide), flat[q][:, :wide], real)
        tail = jnp.concatenate([flat[0][:, wide:], flat[1][:, wide:]], axis=1)
        store_groups(o_ref, t, slice(2 * wide, 2 * ch), tail, real)
        return 0

    lax.fori_loop(0, frames // 2, step, 0)


def conv_weight_kernel(w_ref, o_ref):
    ch = w_ref.shape[-1]
    wide = 256
    rest = ch - wide
    none = jnp.zeros((ch, rest), BF16)
    for a in range(3):
        taps = [w_ref[a, b] for b in range(3)]
        tails = [
            jnp.concatenate([taps[0][:, wide:], taps[1][:, wide:]], axis=1),
            jnp.concatenate([taps[2][:, wide:], none], axis=1),
        ]
        for src, dst, size in ((0, a * wide, wide), (wide, 3 * wide + a * rest, rest)):
            rows = pl.ds(dst, size)
            for b in range(3):
                o_ref[rows, b * wide : (b + 1) * wide] = taps[b][src : src + size, :wide]
            for k in range(2):
                o_ref[rows, 3 * wide + k * 128 : 3 * wide + (k + 1) * 128] = tails[k][
                    src : src + size
                ]
    o_ref[3 * wide + 3 * rest :, :] = jnp.zeros((rest, 4 * wide), BF16)


def store_groups(o_ref, t, lanes, value, real):
    shards = o_ref.shape[0]
    value = value.astype(BF16)
    if real == PIX:
        o_ref[:, t, :, lanes] = value.reshape(shards, PIX, value.shape[-1])
        return
    for d in range(shards):
        o_ref[d, t, :, lanes] = take(value, d, real)


def silu(v):
    return 0.5 * v * (1.0 + jnp.tanh(0.5 * v))


def conv_rows(lines, store, count, n_rows, base, steps, len_ref, w_ref, table_ref):
    wide = 256
    low = low_lanes()

    def clip_of(frame):
        bound = jnp.int32(0)
        place = jnp.int32(0)
        for k in range(CLIPS):
            bound = bound + len_ref[k]
            place = place + jnp.where(frame >= bound, 1, 0)
        return jnp.minimum(place, CLIPS - 1)

    def step(g, _):
        kept = [lines(g * count + k) for k in range(count)]
        across = kept[0][0].shape[0]
        pos = n_rows * across
        window = [
            jnp.concatenate([r for one in kept for r in one[a : a + n_rows]], axis=0)
            for a in range(3)
        ]
        tails = [w[:, wide:] for w in window]
        x = jnp.concatenate(
            [w[:, :wide] for w in window]
            + [
                jnp.concatenate([tails[0], tails[1]], axis=1),
                jnp.concatenate([tails[2], jnp.zeros_like(tails[2])], axis=1),
            ],
            axis=1,
        )
        y = jnp.dot(x, w_ref[...], preferred_element_type=F32)
        n = count * pos
        col = lax.broadcasted_iota(jnp.int32, (n, 128), 0) & (across - 1)
        first, last = col == 0, col == across - 1

        def shifted(left, right):
            return jnp.where(first, 0.0, pltpu.roll(left, 1, 0)) + jnp.where(
                last, 0.0, pltpu.roll(right, n - 1, 0)
            )

        cols = []
        for c in range(2):
            at = lambda b: y[:, b * wide + c * 128 : b * wide + (c + 1) * 128]
            cols.append(shifted(at(0), at(2)) + at(1))
        mid = y[:, 3 * wide : 3 * wide + 128]
        side = shifted(mid, y[:, 3 * wide + 128 :])
        for k in range(count // 2):
            t = g * (count // 2) + k
            even = slice(2 * k * pos, (2 * k + 1) * pos)
            odd = slice((2 * k + 1) * pos, (2 * k + 2) * pos)
            emb = [table_ref[pl.ds(clip_of(base + 2 * t + q), 1), :] for q in range(2)]
            for q, rs in enumerate((even, odd)):
                for c in range(2):
                    lanes = slice(c * 128, (c + 1) * 128)
                    v = cols[c][rs] + emb[q][:, lanes]
                    got = window[1][rs, lanes].astype(F32) + silu(v)
                    store(t, slice(q * wide + c * 128, q * wide + (c + 1) * 128), got)
            tail = jnp.where(
                low, side[even] + swap_halves(mid[even]), swap_halves(side[odd]) + mid[odd]
            )
            tail = tail + jnp.concatenate([emb[0][:, wide:], emb[1][:, wide:]], axis=1)
            res = jnp.concatenate([tails[1][even], tails[1][odd]], axis=1).astype(F32)
            store(t, slice(2 * wide, 2 * wide + 128), res + silu(tail))
        return 0

    lax.fori_loop(0, steps, step, 0)


def keep_if(condition, x):
    return jnp.where(condition, x, jnp.zeros_like(x))


def conv_kernel(flag_ref, len_ref, lat_ref, top_ref, bot_ref, w_ref, table_ref, o_ref):
    frames, rows, across, _ = lat_ref.shape
    real = across * rows // o_ref.shape[0]

    def lines(f):
        top = keep_if(flag_ref[0] > 0, top_ref[f])
        bot = keep_if(flag_ref[1] > 0, bot_ref[f])
        return [top] + [lat_ref[f, i] for i in range(rows)] + [bot]

    def store(t, lanes, value):
        store_groups(o_ref, t, lanes, value, real)

    conv_rows(lines, store, 2, rows, flag_ref[2], frames // 2, len_ref, w_ref, table_ref)


def inner_kernel(flag_ref, len_ref, lat_ref, w_ref, table_ref, o_ref):
    frames, rows, across, _ = lat_ref.shape
    groups = o_ref.shape[0] // rows
    first = flag_ref[0]

    def lines(f):
        above = keep_if(first == 1, lat_ref[f, 0])
        below = keep_if(first == 0, lat_ref[f, rows - 1])
        return [above] + [lat_ref[f, k + first] for k in range(rows - 1)] + [below]

    def store(t, lanes, value):
        dst = o_ref.at[pl.ds(first * groups, (rows - 1) * groups)]
        store_groups(dst, t, lanes, value, PIX)

    count = 6 if frames % 6 == 0 else 2
    conv_rows(
        lines, store, count, rows - 1, flag_ref[2], frames // count, len_ref, w_ref, table_ref
    )


def edge_kernel(
    flag_ref, len_ref, lat_ref, halo_ref, w_ref, table_ref, inner_hbm, o_hbm, edge, sem
):
    frames, rows, across, _ = lat_ref.shape
    groups = edge.shape[0]
    first = flag_ref[0]

    def lines(f):
        halo = halo_ref[f]
        above = jnp.where(first == 1, halo, lat_ref[f, rows - 2])
        below = jnp.where(first == 0, halo, lat_ref[f, 1])
        return [above, lat_ref[f, (1 - first) * (rows - 1)], below]

    def store(t, lanes, value):
        store_groups(edge, t, lanes, value, PIX)

    conv_rows(lines, store, frames, 1, flag_ref[2], 1, len_ref, w_ref, table_ref)
    dst = o_hbm.at[pl.ds((1 - first) * (rows - 1) * groups, groups)]
    out = pltpu.make_async_copy(edge, dst, sem)
    out.start()
    out.wait()


def low_lanes():
    return lax.broadcasted_iota(jnp.int32, (1, 128), 1) < 64


def swap_halves(tail):
    return pltpu.roll(tail, 64, 1)


def split_pair(x):
    tail = x[:, 512:640]
    even = jnp.concatenate([x[:, 0:256], tail], axis=1)
    odd = jnp.concatenate([x[:, 256:512], swap_halves(tail)], axis=1)
    return even, odd


def join_pair(even, odd):
    tail = jnp.where(low_lanes(), even[:, 256:384], swap_halves(odd[:, 256:384]))
    return even[:, 0:256], odd[:, 0:256], tail


def pad_weight(dst, src, row, col):
    ch = src.shape[-1]
    dst[pl.ds(row, dst_tile(ch)), pl.ds(col, dst_tile(ch))] = jnp.zeros(
        (dst_tile(ch), dst_tile(ch)), BF16
    )
    dst[pl.ds(row, ch), pl.ds(col, ch)] = src


def dst_tile(ch):
    return -(-ch // 128) * 128


def sources(m_ref, start, count, base, frames, len_ref):
    own = m_ref.shape[1] - PIX
    x = m_ref[pl.ds(start, count)].astype(F32)

    def pair(v):
        return split_pair(v.reshape(count * own, v.shape[-1]))

    cur = pair(x[:, :own])
    before = pair(jnp.concatenate([x[:, own:], x[:, : own - PIX]], axis=1))[1]
    after = pair(x[:, PIX:])[0]
    unit = lax.broadcasted_iota(jnp.int32, (count, own, 1), 1).reshape(count * own, 1) >> 3
    even = base + 2 * unit
    ids = [clip_ids(even + k, len_ref) for k in (-1, 0, 1, 2)]
    into = jnp.where((ids[0] == ids[1]) & (even > 0), 1.0, 0.0)
    inside = jnp.where(ids[1] == ids[2], 1.0, 0.0)
    out = jnp.where((ids[2] == ids[3]) & (even < frames - 2), 1.0, 0.0)
    stack = lambda a, b: jnp.concatenate([a, b], axis=0)
    previous = stack(before * into, cur[0] * inside)
    following = stack(cur[1] * inside, after * out)
    return previous, stack(*cur), following


def prepare_kernel(len_ref, wq_ref, wk_ref, wv_ref, wo_ref, tw_ref, wqkv, wo, tw, bias):
    pad = wo.shape[0]
    frames = bias.shape[0]
    units = frames // 2
    for j, ref in enumerate((wq_ref, wk_ref, wv_ref)):
        pad_weight(wqkv, ref[...], 0, j * pad)
    pad_weight(wo, wo_ref[...], 0, 0)
    for j in range(3):
        pad_weight(tw, tw_ref[j], j * pad, 0)
    place = lambda axis: lax.broadcasted_iota(jnp.int32, (frames, frames), axis)
    frame = lambda i: jnp.where(i < units, 2 * i, 2 * (i - units) + 1)
    same = clip_ids(frame(place(0)), len_ref) == clip_ids(frame(place(1)), len_ref)
    bias[...] = jnp.where(same, 0.0, -1e30)


def attention_kernel(
    act_hbm, wqkv_hbm, wo_hbm, bias_hbm, o_hbm,
    n5, d5, wqkv, wo, bias, m32, act_ref, o_ref, sems, in_sems, out_sems
):
    rows, ch2 = act_ref.shape
    ch = ch2 // 2
    pad = dst_tile(ch)
    units = rows // PIX
    frames = units * 2
    head = ch // HEADS
    chunk = 96

    def arriving(i):
        at = pl.ds(pl.multiple_of(i * chunk, 8), chunk)
        return pltpu.make_async_copy(act_hbm.at[at], act_ref.at[at], in_sems.at[i])

    for i in range(rows // chunk):
        arriving(i).start()
    fetches = [
        pltpu.make_async_copy(src, dst, sems.at[k])
        for k, (src, dst) in enumerate(((wqkv_hbm, wqkv), (wo_hbm, wo), (bias_hbm, bias)))
    ]
    for f in fetches:
        f.start()
    low = low_lanes()

    def norm(i, _):
        arriving(i).wait()
        at = pl.ds(pl.multiple_of(i * chunk, 8), chunk)
        x = act_ref[at, :].astype(F32)
        cols = [x[:, c * 128 : (c + 1) * 128] for c in range(5)]

        def sums(v):
            a = v[0] + v[1] + jnp.where(low, v[4], 0.0)
            b = v[2] + v[3] + jnp.where(low, 0.0, v[4])
            return [jnp.sum(t, axis=-1, keepdims=True) * (1.0 / ch) for t in (a, b)]

        def spread_out(a, b):
            return [a, a, b, b, jnp.where(low, a, b)]

        center = [v - m for v, m in zip(cols, spread_out(*sums(cols)))]
        var = sums([v * v for v in center])
        gain = spread_out(*[lax.rsqrt(v + 1e-05) for v in var])
        for c in range(5):
            n5[c, at, :] = (center[c] * gain[c]).astype(BF16).astype(F32)
        return 0

    lax.fori_loop(0, rows // chunk, norm, 0)
    for f in fetches:
        f.wait()

    factor = head ** (-0.5) * math.log2(math.e)
    lane = lax.broadcasted_iota(jnp.int32, (1, pad), 1)
    group = 4

    def pixels(i, _):
        parts = []
        for g in range(group):
            at = pl.ds(i * group + g, units, stride=PIX)
            cols = [n5[c, at, :] for c in range(5)]
            parts.append(jnp.concatenate([cols[0], cols[1], cols[4]], axis=1))
            parts.append(jnp.concatenate([cols[2], cols[3], swap_halves(cols[4])], axis=1))
        n = jnp.concatenate(parts, axis=0).astype(BF16)
        qkv = jnp.dot(n, wqkv[...], preferred_element_type=F32).astype(BF16)
        att = []
        for g in range(group):
            q, k, v = (
                qkv[g * frames : (g + 1) * frames, j * pad : (j + 1) * pad] for j in range(3)
            )
            acc = [None, None]
            for h in range(HEADS):
                w = 0 if (h + 1) * head <= 256 else 1
                win = slice(w * 128, w * 128 + 256)
                mine = (lane >= h * head) & (lane < (h + 1) * head)
                mine = jnp.where(mine, 1.0, 0.0).astype(BF16)
                s = lax.dot_general(
                    (q * mine)[:, win],
                    k[:, win],
                    (((1,), (1,)), ((), ())),
                    preferred_element_type=F32,
                )
                s = s * factor + bias[...]
                e = jnp.exp2(s - jnp.max(s, axis=-1, keepdims=True))
                prob = (e * (1.0 / jnp.sum(e, axis=-1, keepdims=True))).astype(BF16)
                got = jnp.dot(prob, (v * mine)[:, win], preferred_element_type=F32)
                acc[w] = got if acc[w] is None else acc[w] + got
            att.append(
                jnp.concatenate(
                    [acc[0][:, :128], acc[0][:, 128:] + acc[1][:, :128], acc[1][:, 128:]], axis=1
                )
            )
        att = jnp.concatenate(att, axis=0).astype(BF16)
        delta = jnp.dot(att, wo[...], preferred_element_type=F32)
        for g in range(group):
            at = pl.ds(i * group + g, units, stride=PIX)
            base = g * frames
            even, odd = delta[base : base + units], delta[base + units : base + frames]
            d5[0, at, :] = even[:, 0:128]
            d5[1, at, :] = even[:, 128:256]
            d5[2, at, :] = odd[:, 0:128]
            d5[3, at, :] = odd[:, 128:256]
            d5[4, at, :] = even[:, 256:384] + swap_halves(odd[:, 256:384])
        return 0

    lax.fori_loop(0, PIX // group, pixels, 0)

    own = o_ref.shape[1] - PIX

    def leaving(i):
        at = (i, pl.ds(0, own))
        return pltpu.make_async_copy(o_ref.at[at], o_hbm.at[at], out_sems.at[i])

    def mix(i, _):
        at = pl.ds(pl.multiple_of(i * own, 8), own)
        delta = jnp.concatenate([d5[c, at, :] for c in range(5)], axis=1)
        m = (act_ref[at, :].astype(F32) + delta).astype(BF16)
        o_ref[i, 0:own, :] = m
        m32[at, :] = m.astype(F32)
        leaving(i).start()
        return 0

    lax.fori_loop(0, rows // own, mix, 0)

    def edges(i, _):
        after = m32[pl.ds(pl.multiple_of(jnp.minimum((i + 1) * own, rows - PIX), 8), PIX), :]
        before = m32[pl.ds(pl.multiple_of(jnp.maximum(i * own - PIX, 0), 8), PIX), :]
        tail = jnp.where(low, after[:, 512:640], before[:, 512:640])
        edge = jnp.concatenate([after[:, 0:256], before[:, 256:512], tail], axis=1)
        o_ref[i, own : own + PIX, :] = edge.astype(BF16)
        return 0

    lax.fori_loop(0, rows // own, edges, 0)
    at = (slice(None), pl.ds(own, PIX))
    last = pltpu.make_async_copy(o_ref.at[at], o_hbm.at[at], sems.at[3])
    last.start()
    for i in range(rows // own):
        leaving(i).wait()
    last.wait()


def temporal_kernel(flag_ref, len_ref, m_ref, tw, o_ref):
    shards = m_ref.shape[0]
    frames, rows, across, ch = o_ref.shape
    units = frames // 2
    groups = shards // rows
    real = across // groups
    total_frames = flag_ref[3]

    def join(blocks):
        return jnp.concatenate([b[:real] for b in blocks], axis=0).astype(BF16)

    def step(i, _):
        src = sources(m_ref, i * groups, groups, flag_ref[2], total_frames, len_ref)
        rounded = jnp.concatenate([v.astype(BF16) for v in src], axis=1)
        total = src[1] + jnp.dot(rounded, tw[...], preferred_element_type=F32)
        total = total.reshape(2, groups, units, PIX, total.shape[-1])
        for u in range(units):
            for q in range(2):
                got = join([total[q, g, u] for g in range(groups)])
                o_ref[2 * u + q, i] = got[:, :ch]
        return 0

    lax.fori_loop(0, rows, step, 0)


def grad_kernel(flag_ref, len_ref, m_ref, cot_ref, mine_ref, other_ref, grad, full):
    shards = m_ref.shape[0]
    ch = m_ref.shape[-1] // 2
    pad = dst_tile(ch)
    count = 8

    def step(i, _):
        src = sources(m_ref, i * count, count, flag_ref[2], flag_ref[3], len_ref)
        rounded = jnp.concatenate([v.astype(BF16) for v in src], axis=1)
        cot = cot_ref[pl.ds(i * count, count), :, :].astype(F32)
        cot = split_pair(cot.reshape(-1, 2 * ch))
        cot = jnp.concatenate(cot, axis=0).astype(BF16)
        got = lax.dot_general(cot, rounded, (((0,), (0,)), ((), ())), preferred_element_type=F32)

        @pl.when(i == 0)
        def _():
            grad[...] = got

        @pl.when(i > 0)
        def _():
            grad[...] += got

        return 0

    lax.fori_loop(0, shards // count, step, 0)
    for j in range(3):
        full[j * ch : (j + 1) * ch, :] = grad[:, j * pad : (j + 1) * pad].T[:ch, :ch]
    core = flag_ref[4]
    n = mine_ref.shape[0]
    mine_ref[...] = full[pl.ds(pl.multiple_of(core * n, 8), n), :]
    other_ref[...] = full[pl.ds(pl.multiple_of((1 - core) * n, 8), n), :].astype(BF16)


def tree(parts):
    while len(parts) > 1:
        parts = [parts[i] + parts[i + 1] for i in range(0, len(parts), 2)]
    return parts[0]


def swaps(n, k):
    return [(i, i ^ k) for i in range(n)]


def ordered(parts, place):
    stacked = jnp.stack(parts)
    return jnp.concatenate(
        [lax.dynamic_index_in_dim(stacked, place ^ j, 0, False) for j in range(len(parts))], 0
    )


def finish_kernel(flag_ref, own_ref, other_ref, o_ref):
    parts, share, _ = own_ref.shape
    for k in range(parts):
        at = (flag_ref[5] ^ k) * share
        mine = at + flag_ref[4] * parts * share
        theirs = at + (1 - flag_ref[4]) * parts * share
        o_ref[pl.ds(pl.multiple_of(mine, 8), share), :] = own_ref[k].astype(F32)
        o_ref[pl.ds(pl.multiple_of(theirs, 8), share), :] = other_ref[k].astype(F32)


def reduce_all(g, other, block_out, flags):
    core = lax.axis_index("c")
    n_plane = lax.axis_size("y") * lax.axis_size("x")
    place = lax.axis_index("y") * lax.axis_size("x") + lax.axis_index("x")
    n_z = lax.axis_size("z")
    share = g.shape[0] // n_plane

    def cut(v, i, size):
        return lax.dynamic_slice_in_dim(v, i * size, size, 0)

    g = g + lax.ppermute(other, "c", swaps(2, 1)).astype(F32)
    parts = [cut(g, place, share)]
    for k in range(1, n_plane):
        sent = cut(g, place ^ k, share).astype(BF16)
        parts.append(lax.ppermute(sent, PLANE, swaps(n_plane, k)).astype(F32))
    mine = tree(parts).astype(BF16)
    mine, block_out = lax.optimization_barrier((mine, block_out))
    parts = [mine.astype(F32)]
    for k in range(1, n_z):
        parts.append(lax.ppermute(mine, "z", swaps(n_z, k)).astype(F32))
    total = tree(parts).astype(BF16)
    parts = [total] + [lax.ppermute(total, PLANE, swaps(n_plane, k)) for k in range(1, n_plane)]
    if share % 8:
        own = ordered(parts, place)
        other = lax.ppermute(own, "c", swaps(2, 1))
        low = jnp.where(core == 0, own, other)
        high = jnp.where(core == 0, other, own)
        return jnp.concatenate([low, high], 0).astype(F32), block_out
    own = jnp.stack(parts)
    other = lax.ppermute(own, "c", swaps(2, 1))
    whole = jax.ShapeDtypeStruct((2 * g.shape[0], g.shape[1]), F32)
    grads = call(finish_kernel, whole, [SMEM, VMEM, VMEM], bytes_accessed=4 * g.size)(
        flags, own, other
    )
    return grads, block_out


def exchange(x):
    shape = x.shape
    flat = x.reshape(shape[0], shape[1] * shape[2], shape[3])
    flat = lax.all_to_all(flat, SEQ, split_axis=0, concat_axis=0, tiled=True)
    return flat.reshape(shape)


def body(
    latents,
    clip_lengths,
    timesteps,
    spatial_weight,
    time_weight,
    query_weight,
    key_weight,
    value_weight,
    out_weight,
    temporal_weight,
    cotangent,
):
    f_dev, rows, across, ch = latents.shape
    shards = lax.axis_size("z") * lax.axis_size("y") * lax.axis_size("c")
    n_rows = lax.axis_size("x")
    assert rows * across <= shards * PIX and shards % rows == 0 and f_dev % 2 == 0
    half = f_dev // 2
    packed = jax.ShapeDtypeStruct((shards, half, PIX, 2 * ch), BF16)
    positions = f_dev * rows * across
    size = positions * ch * 2
    dense = 2 * positions * ch * ch

    row = lax.axis_index("x")
    if n_rows == 2:
        edge = lax.dynamic_index_in_dim(latents, (1 - row) * (rows - 1), 1, False)
        got = lax.ppermute(edge, "x", swaps(2, 1))
        top, bot = got, got
    else:
        up = [(i, i + 1) for i in range(n_rows - 1)]
        top = lax.ppermute(latents[:, rows - 1], "x", up)
        bot = lax.ppermute(latents[:, 0], "x", [(j, i) for i, j in up])
    seq = (lax.axis_index("z") * lax.axis_size("y") + lax.axis_index("y")) * 2 + lax.axis_index("c")
    place = lax.axis_index("y") * n_rows + row
    core = lax.axis_index("c")
    flags = jnp.stack(
        [row > 0, row < n_rows - 1, seq * f_dev, shards * f_dev, core, place]
    ).astype(jnp.int32)
    table = time_table(timesteps, time_weight)
    taps = call(
        conv_weight_kernel,
        jax.ShapeDtypeStruct((1024, 1024), BF16),
        [VMEM],
        bytes_accessed=2 * size,
    )(spatial_weight)
    work = dict(flops=9 * dense, bytes_accessed=2 * size + 9 * ch * ch * 2)
    if n_rows == 2 and rows * across == shards * PIX and rows > 2:
        inner = call(inner_kernel, packed, [SMEM, SMEM] + [VMEM] * 3, **work)(
            flags, clip_lengths, latents, taps, table
        )
        active = call(
            edge_kernel,
            packed,
            [SMEM, SMEM] + [VMEM] * 4 + [ANY],
            scratch=[
                pltpu.VMEM((shards // rows, half, PIX, 2 * ch), BF16),
                pltpu.SemaphoreType.DMA(()),
            ],
            out_space=ANY,
            aliases={6: 0},
            **work,
        )(flags, clip_lengths, latents, top, taps, table, inner)
    else:
        active = call(conv_kernel, packed, [SMEM, SMEM] + [VMEM] * 5, **work)(
            flags, clip_lengths, latents, top, bot, taps, table
        )
    active = exchange(active)
    cot = call(pack_kernel, packed, [VMEM], bytes_accessed=2 * size)(cotangent)

    n_packed = shards * half * PIX
    flat = jax.ShapeDtypeStruct((n_packed, 2 * ch), BF16)
    units = n_packed // PIX
    tiles = -(-ch // 128)
    columns = pltpu.VMEM((5, n_packed, 128), F32)
    whole = pltpu.VMEM(flat.shape, F32)
    pad = tiles * 128
    weights = [
        jax.ShapeDtypeStruct((pad, 3 * pad), BF16),
        jax.ShapeDtypeStruct((pad, pad), BF16),
        jax.ShapeDtypeStruct((3 * pad, pad), BF16),
        jax.ShapeDtypeStruct((2 * units, 2 * units), F32),
    ]
    prepared = call(prepare_kernel, weights, [SMEM] + [VMEM] * 5, bytes_accessed=4 * size)(
        clip_lengths, query_weight, key_weight, value_weight, out_weight, temporal_weight
    )
    cot, active, prepared = lax.optimization_barrier((cot, active, prepared))
    wqkv, wo, tw, bias = prepared
    mixed = call(
        attention_kernel,
        jax.ShapeDtypeStruct((shards, (half + 1) * PIX, 2 * ch), BF16),
        [ANY] * 4,
        scratch=[columns, columns]
        + [pltpu.VMEM(w.shape, w.dtype) for w in (weights[0], weights[1], weights[3])]
        + [
            whole,
            pltpu.VMEM(flat.shape, BF16),
            pltpu.VMEM((shards, (half + 1) * PIX, 2 * ch), BF16),
            pltpu.SemaphoreType.DMA((4,)),
            pltpu.SemaphoreType.DMA((n_packed // 96,)),
            pltpu.SemaphoreType.DMA((shards,)),
        ],
        out_space=ANY,
        flops=7 * dense,
        bytes_accessed=4 * size,
        limit=WHOLE_VMEM,
    )(active.reshape(flat.shape), wqkv, wo, bias)
    mixed = lax.all_to_all(mixed, SEQ, split_axis=0, concat_axis=0, tiled=True)
    half_grad = (3 * ch // 2, ch)
    mine, other = call(
        grad_kernel,
        (jax.ShapeDtypeStruct(half_grad, F32), jax.ShapeDtypeStruct(half_grad, BF16)),
        [SMEM, SMEM, VMEM, VMEM],
        scratch=[pltpu.VMEM((pad, 3 * pad), F32), pltpu.VMEM((3 * ch, ch), F32)],
        flops=3 * dense,
        bytes_accessed=3 * size,
    )(flags, clip_lengths, mixed, cot.reshape(shards, half * PIX, 2 * ch))
    mixed, mine, other = lax.optimization_barrier((mixed, mine, other))
    block_out = call(
        temporal_kernel,
        jax.ShapeDtypeStruct(latents.shape, BF16),
        [SMEM, SMEM, VMEM, VMEM],
        flops=3 * dense,
        bytes_accessed=3 * size,
    )(flags, clip_lengths, mixed, tw)
    grads, block_out = reduce_all(mine, other, block_out, flags)
    return block_out, grads.reshape(3, ch, ch)


def solution(mesh):
    n_seq, n_row = mesh.devices.shape
    grid = Mesh(mesh.devices.reshape(n_seq // 4, 2, 2, n_row), ("z", "y", "c", "x"))
    spread = P(SEQ, "x", None, None)
    in_specs = (spread,) + (P(),) * 9 + (spread,)
    return jax.shard_map(
        body, mesh=grid, in_specs=in_specs, out_specs=(spread, P()), check_vma=False
    )
```

```python
import math

import jax
import jax.numpy as jnp
from jax import lax
from jax.experimental import pallas as pl
from jax.experimental.pallas import tpu as pltpu
from jax.sharding import Mesh
from jax.sharding import PartitionSpec as P

HEADS = 8
CLIPS = 4
SEQ = ("z", "y", "c")
PLANE = ("y", "x")
BF16 = jnp.bfloat16
F32 = jnp.float32
VMEM = pltpu.VMEM
SMEM = pltpu.SMEM
ANY = pl.ANY
PIX = 8
VMEM_LIMIT = 24 * 2**20
WHOLE_VMEM = 60 * 2**20


def time_table(timesteps, time_weight):
    half_width = time_weight.shape[0] // 2
    frequency = jnp.exp(-math.log(10000.0) * jnp.arange(half_width, dtype=F32) / half_width)
    angles = timesteps.astype(F32)[:, None] * frequency[None, :]
    embedded = jnp.concatenate([jnp.cos(angles), jnp.sin(angles)], axis=1)
    return jnp.dot(embedded, time_weight.astype(F32), precision=lax.Precision.HIGHEST)


def call(
    kernel, out_shape, in_spaces, scratch=(), flops=0, bytes_accessed=0, out_space=VMEM, aliases=None, limit=VMEM_LIMIT
):
    return pl.pallas_call(
        kernel,
        out_shape=out_shape,
        in_specs=[pl.BlockSpec(memory_space=s) for s in in_spaces],
        out_specs=jax.tree.map(lambda _: pl.BlockSpec(memory_space=out_space), out_shape),
        scratch_shapes=scratch,
        input_output_aliases=aliases or {},
        cost_estimate=pl.CostEstimate(
            flops=flops, bytes_accessed=bytes_accessed, transcendentals=0
        ),
        compiler_params=pltpu.CompilerParams(vmem_limit_bytes=limit),
    )


def clip_ids(frame, len_ref):
    bound = jnp.int32(0)
    ids = jnp.zeros(frame.shape, jnp.int32)
    for k in range(CLIPS):
        bound = bound + len_ref[k]
        ids = ids + jnp.where(frame >= bound, 1, 0)
    return ids


def take(row, g, real):
    if real == PIX:
        return row[g * PIX : (g + 1) * PIX]
    piece = row[g * real : (g + 1) * real].astype(F32)
    return jnp.concatenate([piece, jnp.zeros((PIX - real, row.shape[-1]), F32)], 0).astype(BF16)


def pack_kernel(x_ref, o_ref):
    frames, rows, across, ch = x_ref.shape
    real = across * rows // o_ref.shape[0]
    wide = 256

    def step(t, _):
        flat = [
            jnp.concatenate([x_ref[2 * t + q, i] for i in range(rows)], axis=0) for q in range(2)
        ]
        for q in range(2):
            store_groups(o_ref, t, slice(q * wide, (q + 1) * wide), flat[q][:, :wide], real)
        tail = jnp.concatenate([flat[0][:, wide:], flat[1][:, wide:]], axis=1)
        store_groups(o_ref, t, slice(2 * wide, 2 * ch), tail, real)
        return 0

    lax.fori_loop(0, frames // 2, step, 0)


def conv_weight_kernel(w_ref, o_ref):
    ch = w_ref.shape[-1]
    wide = 256
    rest = ch - wide
    none = jnp.zeros((ch, rest), BF16)
    for a in range(3):
        taps = [w_ref[a, b] for b in range(3)]
        tails = [
            jnp.concatenate([taps[0][:, wide:], taps[1][:, wide:]], axis=1),
            jnp.concatenate([taps[2][:, wide:], none], axis=1),
        ]
        for src, dst, size in ((0, a * wide, wide), (wide, 3 * wide + a * rest, rest)):
            rows = pl.ds(dst, size)
            for b in range(3):
                o_ref[rows, b * wide : (b + 1) * wide] = taps[b][src : src + size, :wide]
            for k in range(2):
                o_ref[rows, 3 * wide + k * 128 : 3 * wide + (k + 1) * 128] = tails[k][
                    src : src + size
                ]
    o_ref[3 * wide + 3 * rest :, :] = jnp.zeros((rest, 4 * wide), BF16)


def store_groups(o_ref, t, lanes, value, real):
    shards = o_ref.shape[0]
    value = value.astype(BF16)
    if real == PIX:
        o_ref[:, t, :, lanes] = value.reshape(shards, PIX, value.shape[-1])
        return
    for d in range(shards):
        o_ref[d, t, :, lanes] = take(value, d, real)


def silu(v):
    return 0.5 * v * (1.0 + jnp.tanh(0.5 * v))


def conv_rows(lines, store, count, n_rows, base, steps, len_ref, w_ref, table_ref):
    wide = 256
    low = low_lanes()

    def clip_of(frame):
        bound = jnp.int32(0)
        place = jnp.int32(0)
        for k in range(CLIPS):
            bound = bound + len_ref[k]
            place = place + jnp.where(frame >= bound, 1, 0)
        return jnp.minimum(place, CLIPS - 1)

    def step(g, _):
        kept = [lines(g * count + k) for k in range(count)]
        across = kept[0][0].shape[0]
        pos = n_rows * across
        window = [
            jnp.concatenate([r for one in kept for r in one[a : a + n_rows]], axis=0)
            for a in range(3)
        ]
        tails = [w[:, wide:] for w in window]
        x = jnp.concatenate(
            [w[:, :wide] for w in window]
            + [
                jnp.concatenate([tails[0], tails[1]], axis=1),
                jnp.concatenate([tails[2], jnp.zeros_like(tails[2])], axis=1),
            ],
            axis=1,
        )
        y = jnp.dot(x, w_ref[...], preferred_element_type=F32)
        n = count * pos
        col = lax.broadcasted_iota(jnp.int32, (n, 128), 0) & (across - 1)
        first, last = col == 0, col == across - 1

        def shifted(left, right):
            return jnp.where(first, 0.0, pltpu.roll(left, 1, 0)) + jnp.where(
                last, 0.0, pltpu.roll(right, n - 1, 0)
            )

        cols = []
        for c in range(2):
            at = lambda b: y[:, b * wide + c * 128 : b * wide + (c + 1) * 128]
            cols.append(shifted(at(0), at(2)) + at(1))
        mid = y[:, 3 * wide : 3 * wide + 128]
        side = shifted(mid, y[:, 3 * wide + 128 :])
        for k in range(count // 2):
            t = g * (count // 2) + k
            even = slice(2 * k * pos, (2 * k + 1) * pos)
            odd = slice((2 * k + 1) * pos, (2 * k + 2) * pos)
            emb = [table_ref[pl.ds(clip_of(base + 2 * t + q), 1), :] for q in range(2)]
            for q, rs in enumerate((even, odd)):
                for c in range(2):
                    lanes = slice(c * 128, (c + 1) * 128)
                    v = cols[c][rs] + emb[q][:, lanes]
                    got = window[1][rs, lanes].astype(F32) + silu(v)
                    store(t, slice(q * wide + c * 128, q * wide + (c + 1) * 128), got)
            tail = jnp.where(
                low, side[even] + swap_halves(mid[even]), swap_halves(side[odd]) + mid[odd]
            )
            tail = tail + jnp.concatenate([emb[0][:, wide:], emb[1][:, wide:]], axis=1)
            res = jnp.concatenate([tails[1][even], tails[1][odd]], axis=1).astype(F32)
            store(t, slice(2 * wide, 2 * wide + 128), res + silu(tail))
        return 0

    lax.fori_loop(0, steps, step, 0)


def keep_if(condition, x):
    return jnp.where(condition, x, jnp.zeros_like(x))


def conv_kernel(flag_ref, len_ref, lat_ref, top_ref, bot_ref, w_ref, table_ref, o_ref):
    frames, rows, across, _ = lat_ref.shape
    real = across * rows // o_ref.shape[0]

    def lines(f):
        top = keep_if(flag_ref[0] > 0, top_ref[f])
        bot = keep_if(flag_ref[1] > 0, bot_ref[f])
        return [top] + [lat_ref[f, i] for i in range(rows)] + [bot]

    def store(t, lanes, value):
        store_groups(o_ref, t, lanes, value, real)

    conv_rows(lines, store, 2, rows, flag_ref[2], frames // 2, len_ref, w_ref, table_ref)


def inner_kernel(flag_ref, len_ref, lat_ref, w_ref, table_ref, o_ref):
    frames, rows, across, _ = lat_ref.shape
    groups = o_ref.shape[0] // rows
    first = flag_ref[0]

    def lines(f):
        above = keep_if(first == 1, lat_ref[f, 0])
        below = keep_if(first == 0, lat_ref[f, rows - 1])
        return [above] + [lat_ref[f, k + first] for k in range(rows - 1)] + [below]

    def store(t, lanes, value):
        dst = o_ref.at[pl.ds(first * groups, (rows - 1) * groups)]
        store_groups(dst, t, lanes, value, PIX)

    count = 6 if frames % 6 == 0 else 2
    conv_rows(
        lines, store, count, rows - 1, flag_ref[2], frames // count, len_ref, w_ref, table_ref
    )


def edge_kernel(
    flag_ref, len_ref, lat_ref, halo_ref, w_ref, table_ref, inner_hbm, o_hbm, edge, sem
):
    frames, rows, across, _ = lat_ref.shape
    groups = edge.shape[0]
    first = flag_ref[0]

    def lines(f):
        halo = halo_ref[f]
        above = jnp.where(first == 1, halo, lat_ref[f, rows - 2])
        below = jnp.where(first == 0, halo, lat_ref[f, 1])
        return [above, lat_ref[f, (1 - first) * (rows - 1)], below]

    def store(t, lanes, value):
        store_groups(edge, t, lanes, value, PIX)

    conv_rows(lines, store, frames, 1, flag_ref[2], 1, len_ref, w_ref, table_ref)
    dst = o_hbm.at[pl.ds((1 - first) * (rows - 1) * groups, groups)]
    out = pltpu.make_async_copy(edge, dst, sem)
    out.start()
    out.wait()


def low_lanes():
    return lax.broadcasted_iota(jnp.int32, (1, 128), 1) < 64


def swap_halves(tail):
    return pltpu.roll(tail, 64, 1)


def split_pair(x):
    tail = x[:, 512:640]
    even = jnp.concatenate([x[:, 0:256], tail], axis=1)
    odd = jnp.concatenate([x[:, 256:512], swap_halves(tail)], axis=1)
    return even, odd


def join_pair(even, odd):
    tail = jnp.where(low_lanes(), even[:, 256:384], swap_halves(odd[:, 256:384]))
    return even[:, 0:256], odd[:, 0:256], tail


def pad_weight(dst, src, row, col):
    ch = src.shape[-1]
    dst[pl.ds(row, dst_tile(ch)), pl.ds(col, dst_tile(ch))] = jnp.zeros(
        (dst_tile(ch), dst_tile(ch)), BF16
    )
    dst[pl.ds(row, ch), pl.ds(col, ch)] = src


def dst_tile(ch):
    return -(-ch // 128) * 128


def sources(m_ref, start, count, base, frames, len_ref):
    own = m_ref.shape[1] - PIX
    x = m_ref[pl.ds(start, count)].astype(F32)

    def pair(v):
        return split_pair(v.reshape(count * own, v.shape[-1]))

    cur = pair(x[:, :own])
    before = pair(jnp.concatenate([x[:, own:], x[:, : own - PIX]], axis=1))[1]
    after = pair(x[:, PIX:])[0]
    unit = lax.broadcasted_iota(jnp.int32, (count, own, 1), 1).reshape(count * own, 1) >> 3
    even = base + 2 * unit
    ids = [clip_ids(even + k, len_ref) for k in (-1, 0, 1, 2)]
    into = jnp.where((ids[0] == ids[1]) & (even > 0), 1.0, 0.0)
    inside = jnp.where(ids[1] == ids[2], 1.0, 0.0)
    out = jnp.where((ids[2] == ids[3]) & (even < frames - 2), 1.0, 0.0)
    stack = lambda a, b: jnp.concatenate([a, b], axis=0)
    previous = stack(before * into, cur[0] * inside)
    following = stack(cur[1] * inside, after * out)
    return previous, stack(*cur), following


def prepare_kernel(len_ref, wq_ref, wk_ref, wv_ref, wo_ref, tw_ref, wqkv, wo, tw, bias):
    pad = wo.shape[0]
    frames = bias.shape[0]
    units = frames // 2
    for j, ref in enumerate((wq_ref, wk_ref, wv_ref)):
        pad_weight(wqkv, ref[...], 0, j * pad)
    pad_weight(wo, wo_ref[...], 0, 0)
    for j in range(3):
        pad_weight(tw, tw_ref[j], j * pad, 0)
    place = lambda axis: lax.broadcasted_iota(jnp.int32, (frames, frames), axis)
    frame = lambda i: jnp.where(i < units, 2 * i, 2 * (i - units) + 1)
    same = clip_ids(frame(place(0)), len_ref) == clip_ids(frame(place(1)), len_ref)
    bias[...] = jnp.where(same, 0.0, -1e30)


def attention_kernel(
    act_hbm, wqkv_hbm, wo_hbm, bias_hbm, o_hbm,
    n5, d5, wqkv, wo, bias, m32, act_ref, o_ref, sems, in_sems, out_sems
):
    rows, ch2 = act_ref.shape
    ch = ch2 // 2
    pad = dst_tile(ch)
    units = rows // PIX
    frames = units * 2
    head = ch // HEADS
    chunk = 192

    def arriving(i):
        at = pl.ds(pl.multiple_of(i * chunk, 8), chunk)
        return pltpu.make_async_copy(act_hbm.at[at], act_ref.at[at], in_sems.at[i])

    for i in range(rows // chunk):
        arriving(i).start()
    fetches = [
        pltpu.make_async_copy(src, dst, sems.at[k])
        for k, (src, dst) in enumerate(((wqkv_hbm, wqkv), (wo_hbm, wo), (bias_hbm, bias)))
    ]
    for f in fetches:
        f.start()
    low = low_lanes()

    def norm(i, _):
        arriving(i).wait()
        at = pl.ds(pl.multiple_of(i * chunk, 8), chunk)
        x = act_ref[at, :].astype(F32)
        cols = [x[:, c * 128 : (c + 1) * 128] for c in range(5)]

        def sums(v):
            a = v[0] + v[1] + jnp.where(low, v[4], 0.0)
            b = v[2] + v[3] + jnp.where(low, 0.0, v[4])
            return [jnp.sum(t, axis=-1, keepdims=True) * (1.0 / ch) for t in (a, b)]

        def spread_out(a, b):
            return [a, a, b, b, jnp.where(low, a, b)]

        center = [v - m for v, m in zip(cols, spread_out(*sums(cols)))]
        var = sums([v * v for v in center])
        gain = spread_out(*[lax.rsqrt(v + 1e-05) for v in var])
        for c in range(5):
            n5[c, at, :] = (center[c] * gain[c]).astype(BF16).astype(F32)
        return 0

    lax.fori_loop(0, rows // chunk, norm, 0)
    for f in fetches:
        f.wait()

    factor = head ** (-0.5) * math.log2(math.e)
    lane = lax.broadcasted_iota(jnp.int32, (1, pad), 1)
    group = 4

    def pixels(i, _):
        parts = []
        for g in range(group):
            at = pl.ds(i * group + g, units, stride=PIX)
            cols = [n5[c, at, :] for c in range(5)]
            parts.append(jnp.concatenate([cols[0], cols[1], cols[4]], axis=1))
            parts.append(jnp.concatenate([cols[2], cols[3], swap_halves(cols[4])], axis=1))
        n = jnp.concatenate(parts, axis=0).astype(BF16)
        qkv = jnp.dot(n, wqkv[...], preferred_element_type=F32).astype(BF16)
        att = []
        for g in range(group):
            q, k, v = (
                qkv[g * frames : (g + 1) * frames, j * pad : (j + 1) * pad] for j in range(3)
            )
            acc = [None, None]
            for h in range(HEADS):
                w = 0 if (h + 1) * head <= 256 else 1
                win = slice(w * 128, w * 128 + 256)
                mine = (lane >= h * head) & (lane < (h + 1) * head)
                mine = jnp.where(mine, 1.0, 0.0).astype(BF16)
                s = lax.dot_general(
                    (q * mine)[:, win],
                    k[:, win],
                    (((1,), (1,)), ((), ())),
                    preferred_element_type=F32,
                )
                s = s * factor + bias[...]
                e = jnp.exp2(s - jnp.max(s, axis=-1, keepdims=True))
                prob = (e * (1.0 / jnp.sum(e, axis=-1, keepdims=True))).astype(BF16)
                got = jnp.dot(prob, (v * mine)[:, win], preferred_element_type=F32)
                acc[w] = got if acc[w] is None else acc[w] + got
            att.append(
                jnp.concatenate(
                    [acc[0][:, :128], acc[0][:, 128:] + acc[1][:, :128], acc[1][:, 128:]], axis=1
                )
            )
        att = jnp.concatenate(att, axis=0).astype(BF16)
        delta = jnp.dot(att, wo[...], preferred_element_type=F32)
        for g in range(group):
            at = pl.ds(i * group + g, units, stride=PIX)
            base = g * frames
            even, odd = delta[base : base + units], delta[base + units : base + frames]
            d5[0, at, :] = even[:, 0:128]
            d5[1, at, :] = even[:, 128:256]
            d5[2, at, :] = odd[:, 0:128]
            d5[3, at, :] = odd[:, 128:256]
            d5[4, at, :] = even[:, 256:384] + swap_halves(odd[:, 256:384])
        return 0

    lax.fori_loop(0, PIX // group, pixels, 0)

    own = o_ref.shape[1] - PIX

    def leaving(i):
        at = (i, pl.ds(0, own))
        return pltpu.make_async_copy(o_ref.at[at], o_hbm.at[at], out_sems.at[i])

    def mix(i, _):
        at = pl.ds(pl.multiple_of(i * own, 8), own)
        delta = jnp.concatenate([d5[c, at, :] for c in range(5)], axis=1)
        m = (act_ref[at, :].astype(F32) + delta).astype(BF16)
        o_ref[i, 0:own, :] = m
        m32[at, :] = m.astype(F32)
        leaving(i).start()
        return 0

    lax.fori_loop(0, rows // own, mix, 0, unroll=4)

    def edges(i, _):
        after = m32[pl.ds(pl.multiple_of(jnp.minimum((i + 1) * own, rows - PIX), 8), PIX), :]
        before = m32[pl.ds(pl.multiple_of(jnp.maximum(i * own - PIX, 0), 8), PIX), :]
        tail = jnp.where(low, after[:, 512:640], before[:, 512:640])
        edge = jnp.concatenate([after[:, 0:256], before[:, 256:512], tail], axis=1)
        o_ref[i, own : own + PIX, :] = edge.astype(BF16)
        return 0

    lax.fori_loop(0, rows // own, edges, 0, unroll=4)
    at = (slice(None), pl.ds(own, PIX))
    last = pltpu.make_async_copy(o_ref.at[at], o_hbm.at[at], sems.at[3])
    last.start()
    for i in range(rows // own):
        leaving(i).wait()
    last.wait()


def temporal_kernel(flag_ref, len_ref, m_ref, tw, o_ref):
    shards = m_ref.shape[0]
    frames, rows, across, ch = o_ref.shape
    units = frames // 2
    groups = shards // rows
    real = across // groups
    total_frames = flag_ref[3]

    def join(blocks):
        return jnp.concatenate([b[:real] for b in blocks], axis=0).astype(BF16)

    def step(i, _):
        src = sources(m_ref, i * groups, groups, flag_ref[2], total_frames, len_ref)
        rounded = jnp.concatenate([v.astype(BF16) for v in src], axis=1)
        total = src[1] + jnp.dot(rounded, tw[...], preferred_element_type=F32)
        total = total.reshape(2, groups, units, PIX, total.shape[-1])
        for u in range(units):
            for q in range(2):
                got = join([total[q, g, u] for g in range(groups)])
                o_ref[2 * u + q, i] = got[:, :ch]
        return 0

    lax.fori_loop(0, rows, step, 0)


def grad_kernel(flag_ref, len_ref, m_ref, cot_ref, mine_ref, other_ref, grad, full):
    shards = m_ref.shape[0]
    ch = m_ref.shape[-1] // 2
    pad = dst_tile(ch)
    count = 16

    def step(i, _):
        src = sources(m_ref, i * count, count, flag_ref[2], flag_ref[3], len_ref)
        rounded = jnp.concatenate([v.astype(BF16) for v in src], axis=1)
        cot = cot_ref[pl.ds(i * count, count), :, :].astype(F32)
        cot = split_pair(cot.reshape(-1, 2 * ch))
        cot = jnp.concatenate(cot, axis=0).astype(BF16)
        got = lax.dot_general(cot, rounded, (((0,), (0,)), ((), ())), preferred_element_type=F32)

        @pl.when(i == 0)
        def _():
            grad[...] = got

        @pl.when(i > 0)
        def _():
            grad[...] += got

        return 0

    lax.fori_loop(0, shards // count, step, 0)
    for j in range(3):
        full[j * ch : (j + 1) * ch, :] = grad[:, j * pad : (j + 1) * pad].T[:ch, :ch]
    core = flag_ref[4]
    n = mine_ref.shape[0]
    mine_ref[...] = full[pl.ds(pl.multiple_of(core * n, 8), n), :]
    other_ref[...] = full[pl.ds(pl.multiple_of((1 - core) * n, 8), n), :].astype(BF16)


def tree(parts):
    while len(parts) > 1:
        parts = [parts[i] + parts[i + 1] for i in range(0, len(parts), 2)]
    return parts[0]


def swaps(n, k):
    return [(i, i ^ k) for i in range(n)]


def ordered(parts, place):
    stacked = jnp.stack(parts)
    return jnp.concatenate(
        [lax.dynamic_index_in_dim(stacked, place ^ j, 0, False) for j in range(len(parts))], 0
    )


def finish_kernel(flag_ref, own_ref, other_ref, o_ref):
    parts, share, _ = own_ref.shape
    for k in range(parts):
        at = (flag_ref[5] ^ k) * share
        mine = at + flag_ref[4] * parts * share
        theirs = at + (1 - flag_ref[4]) * parts * share
        o_ref[pl.ds(pl.multiple_of(mine, 8), share), :] = own_ref[k].astype(F32)
        o_ref[pl.ds(pl.multiple_of(theirs, 8), share), :] = other_ref[k].astype(F32)


def reduce_all(g, other, block_out, flags):
    core = lax.axis_index("c")
    n_plane = lax.axis_size("y") * lax.axis_size("x")
    place = lax.axis_index("y") * lax.axis_size("x") + lax.axis_index("x")
    n_z = lax.axis_size("z")
    share = g.shape[0] // n_plane

    def cut(v, i, size):
        return lax.dynamic_slice_in_dim(v, i * size, size, 0)

    g = g + lax.ppermute(other, "c", swaps(2, 1)).astype(F32)
    parts = [cut(g, place, share)]
    for k in range(1, n_plane):
        sent = cut(g, place ^ k, share).astype(BF16)
        parts.append(lax.ppermute(sent, PLANE, swaps(n_plane, k)).astype(F32))
    mine = tree(parts).astype(BF16)
    mine, block_out = lax.optimization_barrier((mine, block_out))
    parts = [mine.astype(F32)]
    for k in range(1, n_z):
        parts.append(lax.ppermute(mine, "z", swaps(n_z, k)).astype(F32))
    total = tree(parts).astype(BF16)
    parts = [total] + [lax.ppermute(total, PLANE, swaps(n_plane, k)) for k in range(1, n_plane)]
    if share % 8:
        own = ordered(parts, place)
        other = lax.ppermute(own, "c", swaps(2, 1))
        low = jnp.where(core == 0, own, other)
        high = jnp.where(core == 0, other, own)
        return jnp.concatenate([low, high], 0).astype(F32), block_out
    own = jnp.stack(parts)
    other = lax.ppermute(own, "c", swaps(2, 1))
    whole = jax.ShapeDtypeStruct((2 * g.shape[0], g.shape[1]), F32)
    grads = call(finish_kernel, whole, [SMEM, VMEM, VMEM], bytes_accessed=4 * g.size)(
        flags, own, other
    )
    return grads, block_out


def exchange(x):
    shape = x.shape
    flat = x.reshape(shape[0], shape[1] * shape[2], shape[3])
    flat = lax.all_to_all(flat, SEQ, split_axis=0, concat_axis=0, tiled=True)
    return flat.reshape(shape)


def body(
    latents,
    clip_lengths,
    timesteps,
    spatial_weight,
    time_weight,
    query_weight,
    key_weight,
    value_weight,
    out_weight,
    temporal_weight,
    cotangent,
):
    f_dev, rows, across, ch = latents.shape
    shards = lax.axis_size("z") * lax.axis_size("y") * lax.axis_size("c")
    n_rows = lax.axis_size("x")
    assert rows * across <= shards * PIX and shards % rows == 0 and f_dev % 2 == 0
    half = f_dev // 2
    packed = jax.ShapeDtypeStruct((shards, half, PIX, 2 * ch), BF16)
    positions = f_dev * rows * across
    size = positions * ch * 2
    dense = 2 * positions * ch * ch

    row = lax.axis_index("x")
    if n_rows == 2:
        edge = lax.dynamic_index_in_dim(latents, (1 - row) * (rows - 1), 1, False)
        got = lax.ppermute(edge, "x", swaps(2, 1))
        top, bot = got, got
    else:
        up = [(i, i + 1) for i in range(n_rows - 1)]
        top = lax.ppermute(latents[:, rows - 1], "x", up)
        bot = lax.ppermute(latents[:, 0], "x", [(j, i) for i, j in up])
    seq = (lax.axis_index("z") * lax.axis_size("y") + lax.axis_index("y")) * 2 + lax.axis_index("c")
    place = lax.axis_index("y") * n_rows + row
    core = lax.axis_index("c")
    flags = jnp.stack(
        [row > 0, row < n_rows - 1, seq * f_dev, shards * f_dev, core, place]
    ).astype(jnp.int32)
    table = time_table(timesteps, time_weight)
    taps = call(
        conv_weight_kernel,
        jax.ShapeDtypeStruct((1024, 1024), BF16),
        [VMEM],
        bytes_accessed=2 * size,
    )(spatial_weight)
    work = dict(flops=9 * dense, bytes_accessed=2 * size + 9 * ch * ch * 2)
    if n_rows == 2 and rows * across == shards * PIX and rows > 2:
        inner = call(inner_kernel, packed, [SMEM, SMEM] + [VMEM] * 3, **work)(
            flags, clip_lengths, latents, taps, table
        )
        active = call(
            edge_kernel,
            packed,
            [SMEM, SMEM] + [VMEM] * 4 + [ANY],
            scratch=[
                pltpu.VMEM((shards // rows, half, PIX, 2 * ch), BF16),
                pltpu.SemaphoreType.DMA(()),
            ],
            out_space=ANY,
            aliases={6: 0},
            **work,
        )(flags, clip_lengths, latents, top, taps, table, inner)
    else:
        active = call(conv_kernel, packed, [SMEM, SMEM] + [VMEM] * 5, **work)(
            flags, clip_lengths, latents, top, bot, taps, table
        )
    active = exchange(active)
    cot = call(pack_kernel, packed, [VMEM], bytes_accessed=2 * size)(cotangent)

    n_packed = shards * half * PIX
    flat = jax.ShapeDtypeStruct((n_packed, 2 * ch), BF16)
    units = n_packed // PIX
    tiles = -(-ch // 128)
    columns = pltpu.VMEM((5, n_packed, 128), F32)
    whole = pltpu.VMEM(flat.shape, F32)
    pad = tiles * 128
    weights = [
        jax.ShapeDtypeStruct((pad, 3 * pad), BF16),
        jax.ShapeDtypeStruct((pad, pad), BF16),
        jax.ShapeDtypeStruct((3 * pad, pad), BF16),
        jax.ShapeDtypeStruct((2 * units, 2 * units), F32),
    ]
    prepared = call(prepare_kernel, weights, [SMEM] + [VMEM] * 5, bytes_accessed=4 * size)(
        clip_lengths, query_weight, key_weight, value_weight, out_weight, temporal_weight
    )
    cot, active, prepared = lax.optimization_barrier((cot, active, prepared))
    wqkv, wo, tw, bias = prepared
    mixed = call(
        attention_kernel,
        jax.ShapeDtypeStruct((shards, (half + 1) * PIX, 2 * ch), BF16),
        [ANY] * 4,
        scratch=[columns, columns]
        + [pltpu.VMEM(w.shape, w.dtype) for w in (weights[0], weights[1], weights[3])]
        + [
            whole,
            pltpu.VMEM(flat.shape, BF16),
            pltpu.VMEM((shards, (half + 1) * PIX, 2 * ch), BF16),
            pltpu.SemaphoreType.DMA((4,)),
            pltpu.SemaphoreType.DMA((n_packed // 192,)),
            pltpu.SemaphoreType.DMA((shards,)),
        ],
        out_space=ANY,
        flops=7 * dense,
        bytes_accessed=4 * size,
        limit=WHOLE_VMEM,
    )(active.reshape(flat.shape), wqkv, wo, bias)
    mixed = lax.all_to_all(mixed, SEQ, split_axis=0, concat_axis=0, tiled=True)
    half_grad = (3 * ch // 2, ch)
    mine, other = call(
        grad_kernel,
        (jax.ShapeDtypeStruct(half_grad, F32), jax.ShapeDtypeStruct(half_grad, BF16)),
        [SMEM, SMEM, VMEM, VMEM],
        scratch=[pltpu.VMEM((pad, 3 * pad), F32), pltpu.VMEM((3 * ch, ch), F32)],
        flops=3 * dense,
        bytes_accessed=3 * size,
    )(flags, clip_lengths, mixed, cot.reshape(shards, half * PIX, 2 * ch))
    mixed, mine, other = lax.optimization_barrier((mixed, mine, other))
    block_out = call(
        temporal_kernel,
        jax.ShapeDtypeStruct(latents.shape, BF16),
        [SMEM, SMEM, VMEM, VMEM],
        flops=3 * dense,
        bytes_accessed=3 * size,
    )(flags, clip_lengths, mixed, tw)
    grads, block_out = reduce_all(mine, other, block_out, flags)
    return block_out, grads.reshape(3, ch, ch)


def solution(mesh):
    n_seq, n_row = mesh.devices.shape
    grid = Mesh(mesh.devices.reshape(n_seq // 4, 2, 2, n_row), ("z", "y", "c", "x"))
    spread = P(SEQ, "x", None, None)
    in_specs = (spread,) + (P(),) * 9 + (spread,)
    return jax.shard_map(
        body, mesh=grid, in_specs=in_specs, out_specs=(spread, P()), check_vma=False
    )
```

```python
import math

import jax
import jax.numpy as jnp
from jax import lax
from jax.experimental import pallas as pl
from jax.experimental.pallas import tpu as pltpu
from jax.sharding import Mesh
from jax.sharding import PartitionSpec as P

HEADS = 8
CLIPS = 4
SEQ = ("z", "y", "c")
PLANE = ("y", "x")
BF16 = jnp.bfloat16
F32 = jnp.float32
VMEM = pltpu.VMEM
SMEM = pltpu.SMEM
ANY = pl.ANY
PIX = 8
VMEM_LIMIT = 24 * 2**20
WHOLE_VMEM = 60 * 2**20


def time_table(timesteps, time_weight):
    half_width = time_weight.shape[0] // 2
    frequency = jnp.exp(-math.log(10000.0) * jnp.arange(half_width, dtype=F32) / half_width)
    angles = timesteps.astype(F32)[:, None] * frequency[None, :]
    embedded = jnp.concatenate([jnp.cos(angles), jnp.sin(angles)], axis=1)
    return jnp.dot(embedded, time_weight.astype(F32), precision=lax.Precision.HIGHEST)


def call(
    kernel, out_shape, in_spaces, scratch=(), flops=0, bytes_accessed=0, out_space=VMEM, aliases=None, limit=VMEM_LIMIT
):
    return pl.pallas_call(
        kernel,
        out_shape=out_shape,
        in_specs=[pl.BlockSpec(memory_space=s) for s in in_spaces],
        out_specs=jax.tree.map(lambda _: pl.BlockSpec(memory_space=out_space), out_shape),
        scratch_shapes=scratch,
        input_output_aliases=aliases or {},
        cost_estimate=pl.CostEstimate(
            flops=flops, bytes_accessed=bytes_accessed, transcendentals=0
        ),
        compiler_params=pltpu.CompilerParams(vmem_limit_bytes=limit),
    )


def clip_ids(frame, len_ref):
    bound = jnp.int32(0)
    ids = jnp.zeros(frame.shape, jnp.int32)
    for k in range(CLIPS):
        bound = bound + len_ref[k]
        ids = ids + jnp.where(frame >= bound, 1, 0)
    return ids


def take(row, g, real):
    if real == PIX:
        return row[g * PIX : (g + 1) * PIX]
    piece = row[g * real : (g + 1) * real].astype(F32)
    return jnp.concatenate([piece, jnp.zeros((PIX - real, row.shape[-1]), F32)], 0).astype(BF16)


def pack_kernel(x_ref, o_ref):
    frames, rows, across, ch = x_ref.shape
    real = across * rows // o_ref.shape[0]
    wide = 256

    def step(t, _):
        flat = [
            jnp.concatenate([x_ref[2 * t + q, i] for i in range(rows)], axis=0) for q in range(2)
        ]
        for q in range(2):
            store_groups(o_ref, t, slice(q * wide, (q + 1) * wide), flat[q][:, :wide], real)
        tail = jnp.concatenate([flat[0][:, wide:], flat[1][:, wide:]], axis=1)
        store_groups(o_ref, t, slice(2 * wide, 2 * ch), tail, real)
        return 0

    lax.fori_loop(0, frames // 2, step, 0)


def conv_weight_kernel(w_ref, o_ref):
    ch = w_ref.shape[-1]
    wide = 256
    rest = ch - wide
    none = jnp.zeros((ch, rest), BF16)
    for a in range(3):
        taps = [w_ref[a, b] for b in range(3)]
        tails = [
            jnp.concatenate([taps[0][:, wide:], taps[1][:, wide:]], axis=1),
            jnp.concatenate([taps[2][:, wide:], none], axis=1),
        ]
        for src, dst, size in ((0, a * wide, wide), (wide, 3 * wide + a * rest, rest)):
            rows = pl.ds(dst, size)
            for b in range(3):
                o_ref[rows, b * wide : (b + 1) * wide] = taps[b][src : src + size, :wide]
            for k in range(2):
                o_ref[rows, 3 * wide + k * 128 : 3 * wide + (k + 1) * 128] = tails[k][
                    src : src + size
                ]
    o_ref[3 * wide + 3 * rest :, :] = jnp.zeros((rest, 4 * wide), BF16)


def store_groups(o_ref, t, lanes, value, real):
    shards = o_ref.shape[0]
    value = value.astype(BF16)
    if real == PIX:
        o_ref[:, t, :, lanes] = value.reshape(shards, PIX, value.shape[-1])
        return
    for d in range(shards):
        o_ref[d, t, :, lanes] = take(value, d, real)


def silu(v):
    return 0.5 * v * (1.0 + jnp.tanh(0.5 * v))


def conv_rows(lines, store, count, n_rows, base, steps, len_ref, w_ref, table_ref):
    wide = 256
    low = low_lanes()

    def clip_of(frame):
        bound = jnp.int32(0)
        place = jnp.int32(0)
        for k in range(CLIPS):
            bound = bound + len_ref[k]
            place = place + jnp.where(frame >= bound, 1, 0)
        return jnp.minimum(place, CLIPS - 1)

    def step(g, _):
        kept = [lines(g * count + k) for k in range(count)]
        across = kept[0][0].shape[0]
        pos = n_rows * across
        window = [
            jnp.concatenate([r for one in kept for r in one[a : a + n_rows]], axis=0)
            for a in range(3)
        ]
        tails = [w[:, wide:] for w in window]
        x = jnp.concatenate(
            [w[:, :wide] for w in window]
            + [
                jnp.concatenate([tails[0], tails[1]], axis=1),
                jnp.concatenate([tails[2], jnp.zeros_like(tails[2])], axis=1),
            ],
            axis=1,
        )
        y = jnp.dot(x, w_ref[...], preferred_element_type=F32)
        n = count * pos
        col = lax.broadcasted_iota(jnp.int32, (n, 128), 0) & (across - 1)
        first, last = col == 0, col == across - 1

        def shifted(left, right):
            return jnp.where(first, 0.0, pltpu.roll(left, 1, 0)) + jnp.where(
                last, 0.0, pltpu.roll(right, n - 1, 0)
            )

        cols = []
        for c in range(2):
            at = lambda b: y[:, b * wide + c * 128 : b * wide + (c + 1) * 128]
            cols.append(shifted(at(0), at(2)) + at(1))
        mid = y[:, 3 * wide : 3 * wide + 128]
        side = shifted(mid, y[:, 3 * wide + 128 :])
        for k in range(count // 2):
            t = g * (count // 2) + k
            even = slice(2 * k * pos, (2 * k + 1) * pos)
            odd = slice((2 * k + 1) * pos, (2 * k + 2) * pos)
            emb = [table_ref[pl.ds(clip_of(base + 2 * t + q), 1), :] for q in range(2)]
            for q, rs in enumerate((even, odd)):
                for c in range(2):
                    lanes = slice(c * 128, (c + 1) * 128)
                    v = cols[c][rs] + emb[q][:, lanes]
                    got = window[1][rs, lanes].astype(F32) + silu(v)
                    store(t, slice(q * wide + c * 128, q * wide + (c + 1) * 128), got)
            tail = jnp.where(
                low, side[even] + swap_halves(mid[even]), swap_halves(side[odd]) + mid[odd]
            )
            tail = tail + jnp.concatenate([emb[0][:, wide:], emb[1][:, wide:]], axis=1)
            res = jnp.concatenate([tails[1][even], tails[1][odd]], axis=1).astype(F32)
            store(t, slice(2 * wide, 2 * wide + 128), res + silu(tail))
        return 0

    lax.fori_loop(0, steps, step, 0)


def keep_if(condition, x):
    return jnp.where(condition, x, jnp.zeros_like(x))


def conv_kernel(flag_ref, len_ref, lat_ref, top_ref, bot_ref, w_ref, table_ref, o_ref):
    frames, rows, across, _ = lat_ref.shape
    real = across * rows // o_ref.shape[0]

    def lines(f):
        top = keep_if(flag_ref[0] > 0, top_ref[f])
        bot = keep_if(flag_ref[1] > 0, bot_ref[f])
        return [top] + [lat_ref[f, i] for i in range(rows)] + [bot]

    def store(t, lanes, value):
        store_groups(o_ref, t, lanes, value, real)

    conv_rows(lines, store, 2, rows, flag_ref[2], frames // 2, len_ref, w_ref, table_ref)


def inner_kernel(flag_ref, len_ref, lat_ref, w_ref, table_ref, o_ref):
    frames, rows, across, _ = lat_ref.shape
    groups = o_ref.shape[0] // rows
    first = flag_ref[0]

    def lines(f):
        above = keep_if(first == 1, lat_ref[f, 0])
        below = keep_if(first == 0, lat_ref[f, rows - 1])
        return [above] + [lat_ref[f, k + first] for k in range(rows - 1)] + [below]

    def store(t, lanes, value):
        dst = o_ref.at[pl.ds(first * groups, (rows - 1) * groups)]
        store_groups(dst, t, lanes, value, PIX)

    count = 6 if frames % 6 == 0 else 2
    conv_rows(
        lines, store, count, rows - 1, flag_ref[2], frames // count, len_ref, w_ref, table_ref
    )


def edge_kernel(
    flag_ref, len_ref, lat_ref, halo_ref, w_ref, table_ref, inner_hbm, o_hbm, edge, sem
):
    frames, rows, across, _ = lat_ref.shape
    groups = edge.shape[0]
    first = flag_ref[0]

    def lines(f):
        halo = halo_ref[f]
        above = jnp.where(first == 1, halo, lat_ref[f, rows - 2])
        below = jnp.where(first == 0, halo, lat_ref[f, 1])
        return [above, lat_ref[f, (1 - first) * (rows - 1)], below]

    def store(t, lanes, value):
        store_groups(edge, t, lanes, value, PIX)

    conv_rows(lines, store, frames, 1, flag_ref[2], 1, len_ref, w_ref, table_ref)
    dst = o_hbm.at[pl.ds((1 - first) * (rows - 1) * groups, groups)]
    out = pltpu.make_async_copy(edge, dst, sem)
    out.start()
    out.wait()


def low_lanes():
    return lax.broadcasted_iota(jnp.int32, (1, 128), 1) < 64


def swap_halves(tail):
    return pltpu.roll(tail, 64, 1)


def split_pair(x):
    tail = x[:, 512:640]
    even = jnp.concatenate([x[:, 0:256], tail], axis=1)
    odd = jnp.concatenate([x[:, 256:512], swap_halves(tail)], axis=1)
    return even, odd


def join_pair(even, odd):
    tail = jnp.where(low_lanes(), even[:, 256:384], swap_halves(odd[:, 256:384]))
    return even[:, 0:256], odd[:, 0:256], tail


def pad_weight(dst, src, row, col):
    ch = src.shape[-1]
    dst[pl.ds(row, dst_tile(ch)), pl.ds(col, dst_tile(ch))] = jnp.zeros(
        (dst_tile(ch), dst_tile(ch)), BF16
    )
    dst[pl.ds(row, ch), pl.ds(col, ch)] = src


def dst_tile(ch):
    return -(-ch // 128) * 128


def sources(m_ref, start, count, base, frames, len_ref):
    own = m_ref.shape[1] - PIX
    x = m_ref[pl.ds(start, count)].astype(F32)

    def pair(v):
        return split_pair(v.reshape(count * own, v.shape[-1]))

    cur = pair(x[:, :own])
    before = pair(jnp.concatenate([x[:, own:], x[:, : own - PIX]], axis=1))[1]
    after = pair(x[:, PIX:])[0]
    unit = lax.broadcasted_iota(jnp.int32, (count, own, 1), 1).reshape(count * own, 1) >> 3
    even = base + 2 * unit
    ids = [clip_ids(even + k, len_ref) for k in (-1, 0, 1, 2)]
    into = jnp.where((ids[0] == ids[1]) & (even > 0), 1.0, 0.0)
    inside = jnp.where(ids[1] == ids[2], 1.0, 0.0)
    out = jnp.where((ids[2] == ids[3]) & (even < frames - 2), 1.0, 0.0)
    stack = lambda a, b: jnp.concatenate([a, b], axis=0)
    previous = stack(before * into, cur[0] * inside)
    following = stack(cur[1] * inside, after * out)
    return previous, stack(*cur), following


def prepare_kernel(len_ref, wq_ref, wk_ref, wv_ref, wo_ref, tw_ref, wqkv, wo, tw, bias):
    pad = wo.shape[0]
    frames = bias.shape[0]
    units = frames // 2
    for j, ref in enumerate((wq_ref, wk_ref, wv_ref)):
        pad_weight(wqkv, ref[...], 0, j * pad)
    pad_weight(wo, wo_ref[...], 0, 0)
    for j in range(3):
        pad_weight(tw, tw_ref[j], j * pad, 0)
    place = lambda axis: lax.broadcasted_iota(jnp.int32, (frames, frames), axis)
    frame = lambda i: jnp.where(i < units, 2 * i, 2 * (i - units) + 1)
    same = clip_ids(frame(place(0)), len_ref) == clip_ids(frame(place(1)), len_ref)
    bias[...] = jnp.where(same, 0.0, -1e30)


def attention_kernel(
    act_hbm, wqkv_hbm, wo_hbm, bias_hbm, o_hbm,
    n5, d5, wqkv, wo, bias, m32, act_ref, o_ref, sems, in_sems, out_sems
):
    rows, ch2 = act_ref.shape
    ch = ch2 // 2
    pad = dst_tile(ch)
    units = rows // PIX
    frames = units * 2
    head = ch // HEADS
    chunk = 192

    def arriving(i):
        at = pl.ds(pl.multiple_of(i * chunk, 8), chunk)
        return pltpu.make_async_copy(act_hbm.at[at], act_ref.at[at], in_sems.at[i])

    for i in range(rows // chunk):
        arriving(i).start()
    fetches = [
        pltpu.make_async_copy(src, dst, sems.at[k])
        for k, (src, dst) in enumerate(((wqkv_hbm, wqkv), (wo_hbm, wo), (bias_hbm, bias)))
    ]
    for f in fetches:
        f.start()
    low = low_lanes()

    def norm(i, _):
        arriving(i).wait()
        at = pl.ds(pl.multiple_of(i * chunk, 8), chunk)
        x = act_ref[at, :].astype(F32)
        cols = [x[:, c * 128 : (c + 1) * 128] for c in range(5)]

        def sums(v):
            a = v[0] + v[1] + jnp.where(low, v[4], 0.0)
            b = v[2] + v[3] + jnp.where(low, 0.0, v[4])
            return [jnp.sum(t, axis=-1, keepdims=True) * (1.0 / ch) for t in (a, b)]

        def spread_out(a, b):
            return [a, a, b, b, jnp.where(low, a, b)]

        center = [v - m for v, m in zip(cols, spread_out(*sums(cols)))]
        var = sums([v * v for v in center])
        gain = spread_out(*[lax.rsqrt(v + 1e-05) for v in var])
        for c in range(5):
            n5[c, at, :] = (center[c] * gain[c]).astype(BF16).astype(F32)
        return 0

    lax.fori_loop(0, rows // chunk, norm, 0)
    for f in fetches:
        f.wait()

    factor = head ** (-0.5) * math.log2(math.e)
    lane = lax.broadcasted_iota(jnp.int32, (1, pad), 1)
    group = 4

    def pixels(i, _):
        parts = []
        for g in range(group):
            at = pl.ds(i * group + g, units, stride=PIX)
            cols = [n5[c, at, :] for c in range(5)]
            parts.append(jnp.concatenate([cols[0], cols[1], cols[4]], axis=1))
            parts.append(jnp.concatenate([cols[2], cols[3], swap_halves(cols[4])], axis=1))
        n = jnp.concatenate(parts, axis=0).astype(BF16)
        qkv = jnp.dot(n, wqkv[...], preferred_element_type=F32).astype(BF16)
        att = []
        for g in range(group):
            q, k, v = (
                qkv[g * frames : (g + 1) * frames, j * pad : (j + 1) * pad] for j in range(3)
            )
            acc = [None, None]
            for h in range(HEADS):
                w = 0 if (h + 1) * head <= 256 else 1
                win = slice(w * 128, w * 128 + 256)
                mine = (lane >= h * head) & (lane < (h + 1) * head)
                mine = jnp.where(mine, 1.0, 0.0).astype(BF16)
                s = lax.dot_general(
                    (q * mine)[:, win],
                    k[:, win],
                    (((1,), (1,)), ((), ())),
                    preferred_element_type=F32,
                )
                s = s * factor + bias[...]
                e = jnp.exp2(s - jnp.max(s, axis=-1, keepdims=True))
                prob = (e * (1.0 / jnp.sum(e, axis=-1, keepdims=True))).astype(BF16)
                got = jnp.dot(prob, (v * mine)[:, win], preferred_element_type=F32)
                acc[w] = got if acc[w] is None else acc[w] + got
            att.append(
                jnp.concatenate(
                    [acc[0][:, :128], acc[0][:, 128:] + acc[1][:, :128], acc[1][:, 128:]], axis=1
                )
            )
        att = jnp.concatenate(att, axis=0).astype(BF16)
        delta = jnp.dot(att, wo[...], preferred_element_type=F32)
        for g in range(group):
            at = pl.ds(i * group + g, units, stride=PIX)
            base = g * frames
            even, odd = delta[base : base + units], delta[base + units : base + frames]
            d5[0, at, :] = even[:, 0:128]
            d5[1, at, :] = even[:, 128:256]
            d5[2, at, :] = odd[:, 0:128]
            d5[3, at, :] = odd[:, 128:256]
            d5[4, at, :] = even[:, 256:384] + swap_halves(odd[:, 256:384])
        return 0

    lax.fori_loop(0, PIX // group, pixels, 0)

    own = o_ref.shape[1] - PIX

    def leaving(i):
        at = (i, pl.ds(0, own))
        return pltpu.make_async_copy(o_ref.at[at], o_hbm.at[at], out_sems.at[i])

    def mix(i, _):
        at = pl.ds(pl.multiple_of(i * own, 8), own)
        delta = jnp.concatenate([d5[c, at, :] for c in range(5)], axis=1)
        m = (act_ref[at, :].astype(F32) + delta).astype(BF16)
        o_ref[i, 0:own, :] = m
        m32[at, :] = m.astype(F32)
        leaving(i).start()
        return 0

    lax.fori_loop(0, rows // own, mix, 0, unroll=4)

    def edges(i, _):
        after = m32[pl.ds(pl.multiple_of(jnp.minimum((i + 1) * own, rows - PIX), 8), PIX), :]
        before = m32[pl.ds(pl.multiple_of(jnp.maximum(i * own - PIX, 0), 8), PIX), :]
        tail = jnp.where(low, after[:, 512:640], before[:, 512:640])
        edge = jnp.concatenate([after[:, 0:256], before[:, 256:512], tail], axis=1)
        o_ref[i, own : own + PIX, :] = edge.astype(BF16)
        return 0

    lax.fori_loop(0, rows // own, edges, 0, unroll=4)
    at = (slice(None), pl.ds(own, PIX))
    last = pltpu.make_async_copy(o_ref.at[at], o_hbm.at[at], sems.at[3])
    last.start()
    for i in range(rows // own):
        leaving(i).wait()
    last.wait()


def temporal_kernel(flag_ref, len_ref, m_ref, tw, o_ref):
    shards = m_ref.shape[0]
    frames, rows, across, ch = o_ref.shape
    units = frames // 2
    groups = shards // rows
    real = across // groups
    total_frames = flag_ref[3]
    lines = 4 if rows % 4 == 0 else 1
    count = groups * lines

    def join(blocks):
        return jnp.concatenate([b[:real] for b in blocks], axis=0).astype(BF16)

    def step(i, _):
        src = sources(m_ref, i * count, count, flag_ref[2], total_frames, len_ref)
        rounded = jnp.concatenate([v.astype(BF16) for v in src], axis=1)
        total = src[1] + jnp.dot(rounded, tw[...], preferred_element_type=F32)
        total = total.reshape(2, count, units, PIX, total.shape[-1])
        for u in range(units):
            for q in range(2):
                for r in range(lines):
                    got = join([total[q, r * groups + g, u] for g in range(groups)])
                    o_ref[2 * u + q, i * lines + r] = got[:, :ch]
        return 0

    lax.fori_loop(0, rows // lines, step, 0)


def grad_kernel(flag_ref, len_ref, m_ref, cot_ref, mine_ref, other_ref, grad, full):
    shards = m_ref.shape[0]
    ch = m_ref.shape[-1] // 2
    pad = dst_tile(ch)
    count = 16

    def step(i, _):
        src = sources(m_ref, i * count, count, flag_ref[2], flag_ref[3], len_ref)
        rounded = jnp.concatenate([v.astype(BF16) for v in src], axis=1)
        cot = cot_ref[pl.ds(i * count, count), :, :].astype(F32)
        cot = split_pair(cot.reshape(-1, 2 * ch))
        cot = jnp.concatenate(cot, axis=0).astype(BF16)
        got = lax.dot_general(cot, rounded, (((0,), (0,)), ((), ())), preferred_element_type=F32)

        @pl.when(i == 0)
        def _():
            grad[...] = got

        @pl.when(i > 0)
        def _():
            grad[...] += got

        return 0

    lax.fori_loop(0, shards // count, step, 0)
    for j in range(3):
        full[j * ch : (j + 1) * ch, :] = grad[:, j * pad : (j + 1) * pad].T[:ch, :ch]
    core = flag_ref[4]
    n = mine_ref.shape[0]
    mine_ref[...] = full[pl.ds(pl.multiple_of(core * n, 8), n), :]
    other_ref[...] = full[pl.ds(pl.multiple_of((1 - core) * n, 8), n), :].astype(BF16)


def tree(parts):
    while len(parts) > 1:
        parts = [parts[i] + parts[i + 1] for i in range(0, len(parts), 2)]
    return parts[0]


def swaps(n, k):
    return [(i, i ^ k) for i in range(n)]


def ordered(parts, place):
    stacked = jnp.stack(parts)
    return jnp.concatenate(
        [lax.dynamic_index_in_dim(stacked, place ^ j, 0, False) for j in range(len(parts))], 0
    )


def finish_kernel(flag_ref, own_ref, other_ref, o_ref):
    parts, share, _ = own_ref.shape
    for k in range(parts):
        at = (flag_ref[5] ^ k) * share
        mine = at + flag_ref[4] * parts * share
        theirs = at + (1 - flag_ref[4]) * parts * share
        o_ref[pl.ds(pl.multiple_of(mine, 8), share), :] = own_ref[k].astype(F32)
        o_ref[pl.ds(pl.multiple_of(theirs, 8), share), :] = other_ref[k].astype(F32)


def reduce_all(g, other, block_out, flags):
    core = lax.axis_index("c")
    n_plane = lax.axis_size("y") * lax.axis_size("x")
    place = lax.axis_index("y") * lax.axis_size("x") + lax.axis_index("x")
    n_z = lax.axis_size("z")
    share = g.shape[0] // n_plane

    def cut(v, i, size):
        return lax.dynamic_slice_in_dim(v, i * size, size, 0)

    g = g + lax.ppermute(other, "c", swaps(2, 1)).astype(F32)
    parts = [cut(g, place, share)]
    for k in range(1, n_plane):
        sent = cut(g, place ^ k, share).astype(BF16)
        parts.append(lax.ppermute(sent, PLANE, swaps(n_plane, k)).astype(F32))
    mine = tree(parts).astype(BF16)
    mine, block_out = lax.optimization_barrier((mine, block_out))
    parts = [mine.astype(F32)]
    for k in range(1, n_z):
        parts.append(lax.ppermute(mine, "z", swaps(n_z, k)).astype(F32))
    total = tree(parts).astype(BF16)
    parts = [total] + [lax.ppermute(total, PLANE, swaps(n_plane, k)) for k in range(1, n_plane)]
    if share % 8:
        own = ordered(parts, place)
        other = lax.ppermute(own, "c", swaps(2, 1))
        low = jnp.where(core == 0, own, other)
        high = jnp.where(core == 0, other, own)
        return jnp.concatenate([low, high], 0).astype(F32), block_out
    own = jnp.stack(parts)
    other = lax.ppermute(own, "c", swaps(2, 1))
    whole = jax.ShapeDtypeStruct((2 * g.shape[0], g.shape[1]), F32)
    grads = call(finish_kernel, whole, [SMEM, VMEM, VMEM], bytes_accessed=4 * g.size)(
        flags, own, other
    )
    return grads, block_out


def exchange(x):
    shape = x.shape
    flat = x.reshape(shape[0], shape[1] * shape[2], shape[3])
    flat = lax.all_to_all(flat, SEQ, split_axis=0, concat_axis=0, tiled=True)
    return flat.reshape(shape)


def body(
    latents,
    clip_lengths,
    timesteps,
    spatial_weight,
    time_weight,
    query_weight,
    key_weight,
    value_weight,
    out_weight,
    temporal_weight,
    cotangent,
):
    f_dev, rows, across, ch = latents.shape
    shards = lax.axis_size("z") * lax.axis_size("y") * lax.axis_size("c")
    n_rows = lax.axis_size("x")
    assert rows * across <= shards * PIX and shards % rows == 0 and f_dev % 2 == 0
    half = f_dev // 2
    packed = jax.ShapeDtypeStruct((shards, half, PIX, 2 * ch), BF16)
    positions = f_dev * rows * across
    size = positions * ch * 2
    dense = 2 * positions * ch * ch

    row = lax.axis_index("x")
    if n_rows == 2:
        edge = lax.dynamic_index_in_dim(latents, (1 - row) * (rows - 1), 1, False)
        got = lax.ppermute(edge, "x", swaps(2, 1))
        top, bot = got, got
    else:
        up = [(i, i + 1) for i in range(n_rows - 1)]
        top = lax.ppermute(latents[:, rows - 1], "x", up)
        bot = lax.ppermute(latents[:, 0], "x", [(j, i) for i, j in up])
    seq = (lax.axis_index("z") * lax.axis_size("y") + lax.axis_index("y")) * 2 + lax.axis_index("c")
    place = lax.axis_index("y") * n_rows + row
    core = lax.axis_index("c")
    flags = jnp.stack(
        [row > 0, row < n_rows - 1, seq * f_dev, shards * f_dev, core, place]
    ).astype(jnp.int32)
    table = time_table(timesteps, time_weight)
    taps = call(
        conv_weight_kernel,
        jax.ShapeDtypeStruct((1024, 1024), BF16),
        [VMEM],
        bytes_accessed=2 * size,
    )(spatial_weight)
    work = dict(flops=9 * dense, bytes_accessed=2 * size + 9 * ch * ch * 2)
    if n_rows == 2 and rows * across == shards * PIX and rows > 2:
        inner = call(inner_kernel, packed, [SMEM, SMEM] + [VMEM] * 3, **work)(
            flags, clip_lengths, latents, taps, table
        )
        active = call(
            edge_kernel,
            packed,
            [SMEM, SMEM] + [VMEM] * 4 + [ANY],
            scratch=[
                pltpu.VMEM((shards // rows, half, PIX, 2 * ch), BF16),
                pltpu.SemaphoreType.DMA(()),
            ],
            out_space=ANY,
            aliases={6: 0},
            **work,
        )(flags, clip_lengths, latents, top, taps, table, inner)
    else:
        active = call(conv_kernel, packed, [SMEM, SMEM] + [VMEM] * 5, **work)(
            flags, clip_lengths, latents, top, bot, taps, table
        )
    active = exchange(active)
    cot = call(pack_kernel, packed, [VMEM], bytes_accessed=2 * size)(cotangent)

    n_packed = shards * half * PIX
    flat = jax.ShapeDtypeStruct((n_packed, 2 * ch), BF16)
    units = n_packed // PIX
    tiles = -(-ch // 128)
    columns = pltpu.VMEM((5, n_packed, 128), F32)
    whole = pltpu.VMEM(flat.shape, F32)
    pad = tiles * 128
    weights = [
        jax.ShapeDtypeStruct((pad, 3 * pad), BF16),
        jax.ShapeDtypeStruct((pad, pad), BF16),
        jax.ShapeDtypeStruct((3 * pad, pad), BF16),
        jax.ShapeDtypeStruct((2 * units, 2 * units), F32),
    ]
    prepared = call(prepare_kernel, weights, [SMEM] + [VMEM] * 5, bytes_accessed=4 * size)(
        clip_lengths, query_weight, key_weight, value_weight, out_weight, temporal_weight
    )
    cot, active, prepared = lax.optimization_barrier((cot, active, prepared))
    wqkv, wo, tw, bias = prepared
    mixed = call(
        attention_kernel,
        jax.ShapeDtypeStruct((shards, (half + 1) * PIX, 2 * ch), BF16),
        [ANY] * 4,
        scratch=[columns, columns]
        + [pltpu.VMEM(w.shape, w.dtype) for w in (weights[0], weights[1], weights[3])]
        + [
            whole,
            pltpu.VMEM(flat.shape, BF16),
            pltpu.VMEM((shards, (half + 1) * PIX, 2 * ch), BF16),
            pltpu.SemaphoreType.DMA((4,)),
            pltpu.SemaphoreType.DMA((n_packed // 192,)),
            pltpu.SemaphoreType.DMA((shards,)),
        ],
        out_space=ANY,
        flops=7 * dense,
        bytes_accessed=4 * size,
        limit=WHOLE_VMEM,
    )(active.reshape(flat.shape), wqkv, wo, bias)
    mixed = lax.all_to_all(mixed, SEQ, split_axis=0, concat_axis=0, tiled=True)
    half_grad = (3 * ch // 2, ch)
    mine, other = call(
        grad_kernel,
        (jax.ShapeDtypeStruct(half_grad, F32), jax.ShapeDtypeStruct(half_grad, BF16)),
        [SMEM, SMEM, VMEM, VMEM],
        scratch=[pltpu.VMEM((pad, 3 * pad), F32), pltpu.VMEM((3 * ch, ch), F32)],
        flops=3 * dense,
        bytes_accessed=3 * size,
    )(flags, clip_lengths, mixed, cot.reshape(shards, half * PIX, 2 * ch))
    mixed, mine, other = lax.optimization_barrier((mixed, mine, other))
    block_out = call(
        temporal_kernel,
        jax.ShapeDtypeStruct(latents.shape, BF16),
        [SMEM, SMEM, VMEM, VMEM],
        flops=3 * dense,
        bytes_accessed=3 * size,
    )(flags, clip_lengths, mixed, tw)
    grads, block_out = reduce_all(mine, other, block_out, flags)
    return block_out, grads.reshape(3, ch, ch)


def solution(mesh):
    n_seq, n_row = mesh.devices.shape
    grid = Mesh(mesh.devices.reshape(n_seq // 4, 2, 2, n_row), ("z", "y", "c", "x"))
    spread = P(SEQ, "x", None, None)
    in_specs = (spread,) + (P(),) * 9 + (spread,)
    return jax.shard_map(
        body, mesh=grid, in_specs=in_specs, out_specs=(spread, P()), check_vma=False
    )
```
